128 devices in a mesh: row: 32 (over z, y, x_lo), col: 2 (over core), layer: 2 (over x_hi).
Axes of the slice: x: 4 (x_hi: 2, x_lo: 2; x = x_hi * 2 + x_lo), y: 4, z: 4, core: 2. Of those that a mesh axis runs over, the one named last changes fastest.
Arguments:
- dens_resp: bfloat16 [5120, 5120], P('row', ('col', 'layer')), may hold values from -0.078125 to 0.078125
- density: bfloat16 [5120, 5120], P('row', ('col', 'layer')), may hold values from -0.078125 to 0.078125
- fock: bfloat16 [5120, 5120], P('row', ('col', 'layer')), may hold values from -6 to 6
- fock_resp: bfloat16 [5120, 5120], P('row', ('col', 'layer')), may hold values from -6 to 6
- pattern: int32 [40, 40], replicated, may hold values 0 or 1
Outputs:
- sym_resp: float32 [5120, 5120], P(('row', 'col', 'layer'))
The draws below stay inside these ranges and needn't reach their ends.
All inputs are finite; a program needn't handle non-finite values.
Results may differ from the reference program's by a relative error of at most 0.0029.
Values may be sent and summed in bfloat16 or wider, within the bound.
No kernel may reach another device: no remote copies, remote signals or barrier semaphores. Data moves between devices by JAX's collectives and lax.ppermute only.
A program may use at most 128 MiB of HBM per device.

```python
import jax
import jax.numpy as jnp

BLK = 128
N = 5120
NB = 40


def plant(drawn, key, low, top_value):
    spot = [jax.random.randint(jax.random.fold_in(key, axis), (), 0, length) for axis, length in enumerate(drawn.shape)]
    main_axis = drawn.shape.index(max(drawn.shape))
    neighbour = spot[:main_axis] + [(spot[main_axis] + 1) % drawn.shape[main_axis]] + spot[main_axis + 1:]
    return drawn.at[tuple(spot)].set(low).at[tuple(neighbour)].set(top_value)


def level_of(stream_key, dims, pieces, least, high):
    factor_of = 1.0
    for axis_at, parts in pieces:
        draws = jax.random.uniform(jax.random.fold_in(jax.random.fold_in(stream_key, 6), axis_at), (parts,), jnp.float32, least / len(pieces), high / len(pieces))
        factor_of = factor_of * jnp.repeat(jnp.exp(draws), dims[axis_at] // parts).reshape((-1,) + (1,) * (len(dims) - 1 - axis_at))
    return factor_of


def bell_draw(own_key, shape, scale, reach, cuts=(), dtype=jnp.bfloat16):
    gain = level_of(own_key, shape, cuts, -0.22, 0.18) if cuts else 1.0
    drawn = jax.random.normal(own_key, shape, jnp.float32) * scale * gain
    return jnp.minimum(jnp.maximum(drawn, -reach), reach).astype(dtype)


def setup_inputs(seed: int = 0) -> dict:
    splits = jax.random.split(jax.random.key(seed), 6)
    return {
        "dens_resp": bell_draw(splits[0], (N, N), N ** -0.5, 0.078125, ((0, 32), (1, 4))),
        "density": bell_draw(splits[1], (N, N), N ** -0.5, 0.078125, ((0, 32), (1, 4))),
        "fock": bell_draw(splits[2], (N, N), 1.0, 6.0, ((0, 32), (1, 4))),
        "fock_resp": bell_draw(splits[3], (N, N), 1.0, 6.0, ((0, 32), (1, 4))),
        "pattern": plant((jax.random.randint(splits[4], (NB, NB), 0, 4) < 3).astype(jnp.int32), jax.random.fold_in(splits[4], 1), 0, 1),
    }


def reference(dens_resp, density, fock, fock_resp, pattern):
    first_sum = jnp.dot(dens_resp, fock, preferred_element_type=jnp.float32)
    first_sum = first_sum + jnp.dot(density, fock_resp, preferred_element_type=jnp.float32)
    mixed_rows = first_sum.astype(jnp.bfloat16)
    response = jnp.dot(mixed_rows, density, preferred_element_type=jnp.float32)
    symmetric = 0.5 * (response + response.T)
    kept_blocks = jnp.repeat(jnp.repeat(pattern.astype(jnp.float32), BLK, axis=0), BLK, axis=1)
    return symmetric * kept_blocks
```

```python
import jax
import jax.numpy as jnp
from jax import lax
from jax.sharding import Mesh
from jax.sharding import PartitionSpec as P

BLK = 128
AXES = ("z", "y", "xl", "core", "xh")
SIZES = (4, 4, 2, 2, 2)
f32 = jnp.float32
bf16 = jnp.bfloat16


def flip(value, z=0, y=0, xl=0, core=0, xh=0):
    masks = (z, y, xl, core, xh)
    pairs = []
    for source in range(128):
        rest, digits = source, []
        for size in reversed(SIZES):
            digits.append(rest % size)
            rest //= size
        target = 0
        for digit, size, mask in zip(reversed(digits), SIZES, masks):
            target = target * size + (digit ^ mask)
        pairs.append((source, target))
    return lax.ppermute(value, AXES, pairs)


def remap(value, rule):
    pairs = []
    for source in range(128):
        rest, digits = source, []
        for size in reversed(SIZES):
            digits.append(rest % size)
            rest //= size
        target = 0
        for digit, size in zip(rule(*reversed(digits)), SIZES):
            target = target * size + digit
        pairs.append((source, target))
    return lax.ppermute(value, AXES, pairs)


def pick(stack, index):
    return lax.dynamic_index_in_dim(stack, index, 0, keepdims=False)


def dot(a, b):
    return jnp.dot(a, b, preferred_element_type=f32)


def shards(dens_resp, density, fock, fock_resp, pattern):
    z, y, xl, core, xh = (lax.axis_index(name) for name in AXES)

    with jax.named_scope("right_pair"):
        rounds = []
        for turn in range(2):
            chosen = jnp.where((xl ^ turn) == 0, fock, fock_resp)
            rounds.append(
                remap(chosen, lambda a, b, c, d, e: (a, b, d, c ^ turn, e))
            )
        right = jnp.where(
            core == 0,
            jnp.concatenate((rounds[0], rounds[1])),
            jnp.concatenate((rounds[1], rounds[0])),
        )
    with jax.named_scope("right_gather"):
        rights = jnp.stack([right] + [flip(right, z=q) for q in (1, 2, 3)])

    with jax.named_scope("left_columns"):
        keep = jnp.where(core == 0, dens_resp, density)
        send = jnp.where(core == 0, density, dens_resp)
        came = flip(send, core=1)
        low = jnp.where(core == 0, keep, came).reshape(160, 4, 320)
        high = jnp.where(core == 0, came, keep).reshape(160, 4, 320)
        pieces = jnp.stack(
            [jnp.concatenate((low[:, j], high[:, j]), axis=1) for j in range(4)]
        )
        slots = [pick(pieces, y)] + [
            flip(pick(pieces, y ^ q), y=q) for q in (1, 2, 3)
        ]
        left = jnp.concatenate(slots)
    with jax.named_scope("left_gather"):
        lefts = {
            (0, 0): left,
            (1, 0): flip(left, xl=1),
            (0, 1): flip(left, xh=1),
            (1, 1): flip(left, xl=1, xh=1),
        }

    with jax.named_scope("density_columns"):
        cols = density.reshape(160, 4, 320).transpose(1, 0, 2)
        dslots = jnp.stack(
            [pick(cols, y)] + [flip(pick(cols, y ^ q), y=q) for q in (1, 2, 3)]
        )
        turned = remap(
            dslots,
            lambda a, b, c, d, e: (c * 2 + e, b, a // 2, d, a % 2),
        )
        dparts = jnp.stack([turned] + [flip(turned, z=q) for q in (1, 2, 3)])
        dfull = jnp.concatenate(
            [
                jnp.concatenate(
                    [
                        pick(pick(dparts, z ^ (nxl * 2 + nzl)), y ^ ny)
                        for nzl in range(2)
                    ],
                    axis=1,
                )
                for ny in range(4)
                for nxl in range(2)
            ]
        )

    with jax.named_scope("first_product"):
        rsel = [
            jnp.concatenate([pick(rights, z ^ (nzh * 2 + (xh ^ r))) for nzh in range(2)])
            for r in range(2)
        ]
        part = [
            dot(lefts[h, 0], rsel[0]) + dot(lefts[h, 1], rsel[1]) for h in range(2)
        ]
    with jax.named_scope("mixed_sum"):
        mine = jnp.where(core == 0, part[0], part[1]).reshape(4, 160, 1280)
        theirs = jnp.where(core == 0, part[1], part[0]).reshape(4, 160, 1280)
        both = [mine[q] + flip(theirs[q], core=1) for q in range(4)]
        total = both[0]
        for q in (1, 2, 3):
            total = total + flip(both[q], y=q)
        mixed = total.astype(bf16)

    with jax.named_scope("mixed_gather"):
        mslots = jnp.concatenate([mixed] + [flip(mixed, y=q) for q in (1, 2, 3)])
        mother = flip(mslots, core=1)
        mrows = jnp.where(
            core == 0,
            jnp.concatenate((mslots, mother)),
            jnp.concatenate((mother, mslots)),
        )

    with jax.named_scope("second_product"):
        resp = dot(mrows, dfull).reshape(2, 8, 2, 40, 640)
        own = resp[0][:, xh].reshape(320, 640)
        total = own
        for h, r in ((1, 0), (0, 1), (1, 1)):
            piece = lax.dynamic_index_in_dim(resp[h], xh ^ r, 1, keepdims=False)
            total = total + flip(piece.astype(bf16), xl=h, xh=r).astype(f32).reshape(320, 640)
        total = total.reshape(4, 2, 40, 640)
        stay = lax.dynamic_index_in_dim(total, core, 1, keepdims=False)
        away = flip(lax.dynamic_index_in_dim(total, 1 - core, 1, keepdims=False), core=1)
        rows = jnp.where(
            core == 0,
            jnp.concatenate((stay, away), axis=2),
            jnp.concatenate((away, stay), axis=2),
        )

    with jax.named_scope("direct"):
        direct = jnp.stack([rows[0]] + [flip(rows[q], y=q) for q in (1, 2, 3)])
        direct = direct.reshape(4, 40, 4, 320)
        long_rows = jnp.stack([pick(direct, y ^ ny) for ny in range(4)], axis=2)
        long_rows = long_rows.reshape(40, 5120)
    with jax.named_scope("transposed"):
        turned = rows.reshape(160, 1280).astype(bf16).T.reshape(32, 40, 160)
        turned = lax.all_to_all(
            turned, ("z", "xl", "core", "xh"), split_axis=0, concat_axis=0, tiled=True
        )
        turned = turned.reshape(4, 8, 40, 4, 40)
        flipped = jnp.stack(
            [
                lax.dynamic_index_in_dim(turned, y ^ ny, 3, keepdims=False)
                for ny in range(4)
            ],
            axis=3,
        )
        flipped = flipped.transpose(2, 0, 3, 1, 4).reshape(40, 5120)

    symmetric = 0.5 * (long_rows + flipped.astype(f32))
    first_row = ((((z * 4 + y) * 2 + xl) * 2 + core) * 2 + xh) * 40
    block_rows = (first_row + jnp.arange(40, dtype=jnp.int32)) // BLK
    block_count = pattern.shape[0]
    onehot = (
        block_rows[:, None] == jnp.arange(block_count, dtype=jnp.int32)[None, :]
    ).astype(f32)
    kept_blocks = jnp.dot(onehot, pattern.astype(f32), preferred_element_type=f32)
    kept_full = jnp.repeat(kept_blocks, BLK, axis=1)
    return symmetric * kept_full


def solution(mesh):
    fine = Mesh(mesh.devices.reshape(SIZES), AXES)
    split = P(("z", "y", "xl"), ("core", "xh"))
    return jax.shard_map(
        shards,
        mesh=fine,
        in_specs=(split, split, split, split, P()),
        out_specs=P(AXES, None),
        check_vma=False,
    )
```

```python
import jax
import jax.numpy as jnp
from jax import lax
from jax.sharding import Mesh
from jax.sharding import PartitionSpec as P

BLK = 128
AXES = ("z", "y", "xl", "core", "xh")
SIZES = (4, 4, 2, 2, 2)
f32 = jnp.float32
bf16 = jnp.bfloat16


def flip(value, z=0, y=0, xl=0, core=0, xh=0):
    masks = (z, y, xl, core, xh)
    pairs = []
    for source in range(128):
        rest, digits = source, []
        for size in reversed(SIZES):
            digits.append(rest % size)
            rest //= size
        target = 0
        for digit, size, mask in zip(reversed(digits), SIZES, masks):
            target = target * size + (digit ^ mask)
        pairs.append((source, target))
    return lax.ppermute(value, AXES, pairs)


def remap(value, rule):
    pairs = []
    for source in range(128):
        rest, digits = source, []
        for size in reversed(SIZES):
            digits.append(rest % size)
            rest //= size
        target = 0
        for digit, size in zip(rule(*reversed(digits)), SIZES):
            target = target * size + digit
        pairs.append((source, target))
    return lax.ppermute(value, AXES, pairs)


def pick(stack, index):
    return lax.dynamic_index_in_dim(stack, index, 0, keepdims=False)


def dot(a, b):
    return jnp.dot(a, b, preferred_element_type=f32)


def shards(dens_resp, density, fock, fock_resp, pattern):
    z, y, xl, core, xh = (lax.axis_index(name) for name in AXES)

    with jax.named_scope("left_columns"):
        keep = jnp.where(core == 0, dens_resp, density)
        send = jnp.where(core == 0, density, dens_resp)
        came = flip(send, core=1)
    with jax.named_scope("right_pair"):
        rounds = []
        for turn in range(2):
            chosen = jnp.where((xl ^ turn) == 0, fock, fock_resp)
            chosen, _ = lax.optimization_barrier((chosen, send))
            rounds.append(
                remap(chosen, lambda a, b, c, d, e: (a, b, d, c ^ turn, e))
            )
    with jax.named_scope("left_columns"):
        low = jnp.where(core == 0, keep, came).reshape(160, 4, 320)
        high = jnp.where(core == 0, came, keep).reshape(160, 4, 320)
        pieces = jnp.stack(
            [jnp.concatenate((low[:, j], high[:, j]), axis=1) for j in range(4)]
        )
        slots = [pick(pieces, y)] + [
            flip(pick(pieces, y ^ q), y=q) for q in (1, 2, 3)
        ]
        left = jnp.concatenate(slots)
    with jax.named_scope("right_gather"):
        rounds[0], rounds[1], left = lax.optimization_barrier((rounds[0], rounds[1], left))
        right = jnp.where(
            core == 0,
            jnp.concatenate((rounds[0], rounds[1])),
            jnp.concatenate((rounds[1], rounds[0])),
        )
        right, left = lax.optimization_barrier((right, left))
        rights = jnp.stack([right] + [flip(right, z=q) for q in (1, 2, 3)])
    with jax.named_scope("left_gather"):
        lefts = {
            (0, 0): left,
            (1, 0): flip(left, xl=1),
            (0, 1): flip(left, xh=1),
            (1, 1): flip(left, xl=1, xh=1),
        }

    with jax.named_scope("density_columns"):
        cols, _ = lax.optimization_barrier((density, left))
        cols = cols.reshape(160, 4, 320).transpose(1, 0, 2)
        dslots = jnp.stack(
            [pick(cols, y)] + [flip(pick(cols, y ^ q), y=q) for q in (1, 2, 3)]
        )

    with jax.named_scope("first_product"):
        rights, dslots = lax.optimization_barrier((rights, dslots))
        rsel = [
            jnp.concatenate([pick(rights, z ^ (nzh * 2 + (xh ^ r))) for nzh in range(2)])
            for r in range(2)
        ]
        theirs = [jnp.where(core == 0, lefts[1, r], lefts[0, r]) for r in range(2)]
        mine = [jnp.where(core == 0, lefts[0, r], lefts[1, r]) for r in range(2)]
        theirs = (dot(theirs[0], rsel[0]) + dot(theirs[1], rsel[1])).reshape(4, 160, 1280)
        mine = (dot(mine[0], rsel[0]) + dot(mine[1], rsel[1])).reshape(4, 160, 1280)
    with jax.named_scope("mixed_sum"):
        both = [None] * 4
        for q in (2, 1, 3, 0):
            both[q] = mine[q] + flip(theirs[q], core=1)
        sums = [flip(both[q], y=q) for q in (1, 2, 3)]

    with jax.named_scope("density_gather"):
        dslots, _ = lax.optimization_barrier((dslots, (both[0], both[1], both[2], both[3])))
        turned = remap(
            dslots,
            lambda a, b, c, d, e: (c * 2 + e, b, a // 2, d, a % 2),
        )
        dparts = jnp.stack([turned] + [flip(turned, z=q) for q in (1, 2, 3)])
    with jax.named_scope("mixed_sum"):
        sums, dparts = lax.optimization_barrier((sums, dparts))
        total = both[0] + sums[0] + sums[1] + sums[2]
        mixed = total.astype(bf16)

    with jax.named_scope("density_rows"):
        dfull = jnp.concatenate(
            [
                jnp.concatenate(
                    [
                        pick(pick(dparts, z ^ (nxl * 2 + nzl)), y ^ ny)
                        for nzl in range(2)
                    ],
                    axis=1,
                )
                for ny in range(4)
                for nxl in range(2)
            ]
        )

    with jax.named_scope("mixed_gather"):
        mslots = jnp.concatenate([mixed] + [flip(mixed, y=q) for q in (1, 2, 3)])
        mother = flip(mslots, core=1)

    with jax.named_scope("second_product"):
        near = dot(mslots, dfull).reshape(4, 160, 640)
        far = dot(mother, dfull).reshape(4, 160, 640)
        place = xl * 2 + xh
        straight = (xl ^ core) == 0

        def piece(r):
            q = place ^ r ^ y
            a, b = pick(near, q), pick(far, q)
            return jnp.where(straight, jnp.stack((a, b)), jnp.stack((b, a)))

        total = piece(0)
        for r in (1, 2, 3):
            came = flip(piece(r).astype(bf16), xl=r // 2, xh=r % 2)
            total = total + came.astype(f32)
        stay = pick(total, core)
        away = flip(pick(total, 1 - core), core=1)
        rows = jnp.where(
            core == 0,
            jnp.concatenate((stay, away), axis=1),
            jnp.concatenate((away, stay), axis=1),
        )

    with jax.named_scope("transposed"):
        turned = rows.astype(bf16).T.reshape(32, 40, 160)
        turned = lax.all_to_all(
            turned, ("z", "xl", "core", "xh"), split_axis=0, concat_axis=0, tiled=True
        )
        turned = turned.reshape(4, 2, 2, 2, 40, 160)
        flipped = turned.transpose(4, 0, 1, 3, 2, 5).reshape(40, 5120)
    with jax.named_scope("direct"):
        quarters = rows.reshape(4, 40, 1280)
        direct = jnp.stack(
            [
                remap(
                    pick(quarters, y ^ t),
                    lambda a, b, c, d, e: (a, c * 2 + e, d, (b ^ t) // 2, (b ^ t) % 2),
                )
                for t in range(4)
            ]
        ).reshape(4, 40, 4, 320)
        mark = core * 2 + xh
        long_rows = jnp.stack([pick(direct, mark ^ ny) for ny in range(4)], axis=2)
        long_rows = long_rows.reshape(40, 5120)

    symmetric = 0.5 * (long_rows + flipped.astype(f32))
    first_row = ((((z * 4 + y) * 2 + xl) * 2 + core) * 2 + xh) * 40
    block_rows = (first_row + jnp.arange(40, dtype=jnp.int32)) // BLK
    block_count = pattern.shape[0]
    onehot = (
        block_rows[:, None] == jnp.arange(block_count, dtype=jnp.int32)[None, :]
    ).astype(f32)
    kept_blocks = jnp.dot(onehot, pattern.astype(f32), preferred_element_type=f32)
    kept_full = jnp.repeat(kept_blocks, BLK, axis=1)
    return symmetric * kept_full


def solution(mesh):
    fine = Mesh(mesh.devices.reshape(SIZES), AXES)
    split = P(("z", "y", "xl"), ("core", "xh"))
    return jax.shard_map(
        shards,
        mesh=fine,
        in_specs=(split, split, split, split, P()),
        out_specs=P(AXES, None),
        check_vma=False,
    )
```

```python
import jax
import jax.numpy as jnp
from jax import lax
from jax.sharding import Mesh
from jax.sharding import PartitionSpec as P

BLK = 128
AXES = ("z", "y", "xl", "core", "xh")
SIZES = (4, 4, 2, 2, 2)
f32 = jnp.float32
bf16 = jnp.bfloat16


def flip(value, z=0, y=0, xl=0, core=0, xh=0):
    masks = (z, y, xl, core, xh)
    pairs = []
    for source in range(128):
        rest, digits = source, []
        for size in reversed(SIZES):
            digits.append(rest % size)
            rest //= size
        target = 0
        for digit, size, mask in zip(reversed(digits), SIZES, masks):
            target = target * size + (digit ^ mask)
        pairs.append((source, target))
    return lax.ppermute(value, AXES, pairs)


def remap(value, rule):
    pairs = []
    for source in range(128):
        rest, digits = source, []
        for size in reversed(SIZES):
            digits.append(rest % size)
            rest //= size
        target = 0
        for digit, size in zip(rule(*reversed(digits)), SIZES):
            target = target * size + digit
        pairs.append((source, target))
    return lax.ppermute(value, AXES, pairs)


def pick(stack, index):
    return lax.dynamic_index_in_dim(stack, index, 0, keepdims=False)


def ring_gather(block, axes):
    near, far = axes
    half = block.shape[0] // 2
    one = flip(block, **near)
    three = flip(block, **far)
    upper = flip(three[:half], **near)
    lower = flip(one[half:], **far)
    return one, three, jnp.concatenate((upper, lower))


def dot(a, b):
    return jnp.dot(a, b, preferred_element_type=f32)


def shards(dens_resp, density, fock, fock_resp, pattern):
    z, y, xl, core, xh = (lax.axis_index(name) for name in AXES)

    with jax.named_scope("left_columns"):
        keep = jnp.where(core == 0, dens_resp, density)
        send = jnp.where(core == 0, density, dens_resp)
        came = flip(send, core=1)
    with jax.named_scope("right_pair"):
        rounds = []
        for turn in range(2):
            chosen = jnp.where((xl ^ turn) == 0, fock, fock_resp)
            chosen, _ = lax.optimization_barrier((chosen, send))
            rounds.append(
                remap(chosen, lambda a, b, c, d, e: (a, b, d, c ^ turn, e))
            )
    with jax.named_scope("left_columns"):
        low = jnp.where(core == 0, keep, came).reshape(160, 4, 320)
        high = jnp.where(core == 0, came, keep).reshape(160, 4, 320)
        pieces = jnp.stack(
            [jnp.concatenate((low[:, j], high[:, j]), axis=1) for j in range(4)]
        )
        left = lax.all_to_all(pieces, "y", split_axis=0, concat_axis=0, tiled=True)
        left = left.reshape(640, 640)
    with jax.named_scope("density_turn"):
        turned, _ = lax.optimization_barrier((density, send))
        turned = remap(
            turned,
            lambda a, b, c, d, e: (c * 2 + e, b, a // 2, d, a % 2),
        )
    with jax.named_scope("right_gather"):
        rounds, left = lax.optimization_barrier((rounds, left))
        right = jnp.where(
            core == 0,
            jnp.concatenate((rounds[0], rounds[1])),
            jnp.concatenate((rounds[1], rounds[0])),
        )
        right, left, turned = lax.optimization_barrier((right, left, turned))
        one, three, two = ring_gather(right, ({"z": 1}, {"z": 3}))
        rights = [right, one, two, three]
    with jax.named_scope("left_gather"):
        one, three, two = ring_gather(left, ({"xl": 1}, {"xl": 1, "xh": 1}))
        lefts = {(0, 0): left, (1, 0): one, (0, 1): two, (1, 1): three}

    with jax.named_scope("density_columns"):
        turned, rights[1], rights[3] = lax.optimization_barrier((turned, rights[1], rights[3]))
        cols = turned.reshape(160, 4, 320).transpose(1, 0, 2)
        dslots = lax.all_to_all(cols, "y", split_axis=0, concat_axis=0, tiled=True)

    with jax.named_scope("swap_matrix"):
        at = jnp.arange(1280, dtype=jnp.int32)
        to = at // 40 % 4 * 320 + at // 160 * 40 + at % 40
        swap = (to[:, None] == at[None, :]).astype(bf16)

    with jax.named_scope("first_product"):
        rights, dslots, swap = lax.optimization_barrier((rights, dslots, swap))
        rights = jnp.stack(rights)
        rsel = [
            jnp.concatenate([pick(rights, z ^ (nzh * 2 + (xh ^ r))) for nzh in range(2)])
            for r in range(2)
        ]
        theirs = [jnp.where(core == 0, lefts[1, r], lefts[0, r]) for r in range(2)]
        mine = [jnp.where(core == 0, lefts[0, r], lefts[1, r]) for r in range(2)]
        theirs = (dot(theirs[0], rsel[0]) + dot(theirs[1], rsel[1])).reshape(4, 160, 1280)
        mine = (dot(mine[0], rsel[0]) + dot(mine[1], rsel[1])).reshape(4, 160, 1280)
    with jax.named_scope("mixed_sum"):
        both = [None] * 4
        for q in (2, 1, 3, 0):
            both[q] = pick(mine, y ^ q) + flip(pick(theirs, y ^ q), core=1)
        upper = flip(both[2][:80], y=1)
        lower = flip(both[2][80:], y=3)
        third = jnp.concatenate((both[3][:80] + upper, both[3][80:]))
        first = jnp.concatenate((both[1][:80], both[1][80:] + lower))
        sums = [flip(first, y=1), flip(third, y=3)]

    with jax.named_scope("density_gather"):
        dslots, _ = lax.optimization_barrier((dslots, both))
        dparts = [dslots] + [flip(dslots, z=q) for q in (1, 2, 3)]

    with jax.named_scope("mixed_sum"):
        sums, dparts = lax.optimization_barrier((sums, dparts))
        total = both[0] + sums[0] + sums[1]
        mixed = total.astype(bf16)

    with jax.named_scope("density_rows"):
        dparts = jnp.stack(dparts)
        dfull = jnp.concatenate(
            [
                jnp.concatenate(
                    [pick(dparts, z ^ (nxl * 2 + nzl))[ny] for nzl in range(2)],
                    axis=1,
                )
                for ny in range(4)
                for nxl in range(2)
            ]
        )

    with jax.named_scope("mixed_gather"):
        mslots = jnp.concatenate([mixed] + [flip(mixed, y=q) for q in (1, 2, 3)])
        mother = flip(mslots, core=1)

    with jax.named_scope("second_product"):
        near = dot(mslots, dfull).reshape(4, 160, 640)
        far = dot(mother, dfull).reshape(4, 160, 640)

        def piece(h, r):
            rows = jnp.where(core == h, near, far).reshape(8, 2, 40, 640)
            return lax.dynamic_index_in_dim(rows, xh ^ r, 1, keepdims=False).reshape(320, 640)

        total = piece(0, 0)
        for h, r in ((0, 1), (1, 0), (1, 1)):
            came = flip(piece(h, r).astype(bf16), xl=h, xh=r)
            total = total + came.astype(f32)
        total = total.reshape(4, 2, 40, 640)
        stay = lax.dynamic_index_in_dim(total, core, 1, keepdims=False)
        away = flip(lax.dynamic_index_in_dim(total, 1 - core, 1, keepdims=False), core=1)
        rows = jnp.where(
            core == 0,
            jnp.concatenate((stay, away), axis=2),
            jnp.concatenate((away, stay), axis=2),
        )

    with jax.named_scope("transposed"):
        sorted_rows = jnp.concatenate([pick(rows, y ^ ny) for ny in range(4)])
        turned = sorted_rows.astype(bf16).T.reshape(32, 40, 160)
        turned = lax.all_to_all(
            turned, ("z", "xl", "core", "xh"), split_axis=0, concat_axis=0, tiled=True
        )
        turned = turned.reshape(4, 8, 40, 160).transpose(0, 2, 1, 3).reshape(160, 1280)
        flipped = dot(turned, swap).reshape(4, 40, 1280)
        flipped = flipped.transpose(1, 0, 2).reshape(40, 5120)
    with jax.named_scope("direct"):
        direct = jnp.stack([rows[0]] + [flip(rows[q], y=q) for q in (1, 2, 3)])
        direct = direct.reshape(4, 40, 4, 320)
        long_rows = jnp.stack([pick(direct, y ^ ny) for ny in range(4)], axis=2)
        long_rows = long_rows.reshape(40, 5120)

    symmetric = 0.5 * (long_rows + flipped)
    first_row = ((((z * 4 + y) * 2 + xl) * 2 + core) * 2 + xh) * 40
    block_rows = (first_row + jnp.arange(40, dtype=jnp.int32)) // BLK
    block_count = pattern.shape[0]
    onehot = (
        block_rows[:, None] == jnp.arange(block_count, dtype=jnp.int32)[None, :]
    ).astype(f32)
    kept_blocks = jnp.dot(onehot, pattern.astype(f32), preferred_element_type=f32)
    kept_full = jnp.repeat(kept_blocks, BLK, axis=1)
    return symmetric * kept_full


def solution(mesh):
    fine = Mesh(mesh.devices.reshape(SIZES), AXES)
    split = P(("z", "y", "xl"), ("core", "xh"))
    return jax.shard_map(
        shards,
        mesh=fine,
        in_specs=(split, split, split, split, P()),
        out_specs=P(AXES, None),
        check_vma=False,
    )
```

```python
import jax
import jax.numpy as jnp
from jax import lax
from jax.sharding import Mesh
from jax.sharding import PartitionSpec as P

BLK = 128
AXES = ("z", "y", "xl", "core", "xh")
SIZES = (4, 4, 2, 2, 2)
f32 = jnp.float32
bf16 = jnp.bfloat16


def flip(value, z=0, y=0, xl=0, core=0, xh=0):
    masks = (z, y, xl, core, xh)
    pairs = []
    for source in range(128):
        rest, digits = source, []
        for size in reversed(SIZES):
            digits.append(rest % size)
            rest //= size
        target = 0
        for digit, size, mask in zip(reversed(digits), SIZES, masks):
            target = target * size + (digit ^ mask)
        pairs.append((source, target))
    return lax.ppermute(value, AXES, pairs)


def remap(value, rule):
    pairs = []
    for source in range(128):
        rest, digits = source, []
        for size in reversed(SIZES):
            digits.append(rest % size)
            rest //= size
        target = 0
        for digit, size in zip(rule(*reversed(digits)), SIZES):
            target = target * size + digit
        pairs.append((source, target))
    return lax.ppermute(value, AXES, pairs)


def pick(stack, index):
    return lax.dynamic_index_in_dim(stack, index, 0, keepdims=False)


def ring_gather(block, axes):
    near, far = axes
    half = block.shape[0] // 2
    one = flip(block, **near)
    three = flip(block, **far)
    upper = flip(three[:half], **near)
    lower = flip(one[half:], **far)
    return one, three, jnp.concatenate((upper, lower))


def dot(a, b):
    return jnp.dot(a, b, preferred_element_type=f32)


def shards(dens_resp, density, fock, fock_resp, pattern):
    z, y, xl, core, xh = (lax.axis_index(name) for name in AXES)

    with jax.named_scope("left_columns"):
        keep = jnp.where(core == 0, dens_resp, density)
        send = jnp.where(core == 0, density, dens_resp)
        came = flip(send, core=1)
    with jax.named_scope("right_columns"):
        at = jnp.arange(1280, dtype=jnp.int32)
        to = at // 160 % 2 * 640 + at // 40 % 2 * 320 + at // 320 * 80 + at // 80 % 2 * 40 + at % 40
        order = (to[:, None] == at[None, :]).astype(bf16)
        both_right = jnp.concatenate((fock, fock_resp))
        parts = [
            dot(both_right, order[:, j * 320 : (j + 1) * 320]).astype(bf16).reshape(2, 1, 160, 320)
            for j in range(4)
        ]
        parts = jnp.concatenate(
            [jnp.concatenate((parts[2 * j], parts[2 * j + 1]), axis=1) for j in range(2)]
        )
        parts, _ = lax.optimization_barrier((parts, send))
        rounds = lax.all_to_all(
            parts.reshape(8, 160, 320), ("xl", "core", "xh"), split_axis=0, concat_axis=0, tiled=True
        )
    with jax.named_scope("density_turn"):
        halves, _ = lax.optimization_barrier((density.reshape(2, 2, 40, 1280), send))
        same = lax.dynamic_index_in_dim(halves, xh, 1, keepdims=False).reshape(80, 4, 320)
        other = lax.dynamic_index_in_dim(halves, 1 - xh, 1, keepdims=False).reshape(80, 1280)
        other = flip(other, xh=1).reshape(80, 4, 320)
    with jax.named_scope("left_columns"):
        low = jnp.where(core == 0, keep, came).reshape(160, 4, 320)
        high = jnp.where(core == 0, came, keep).reshape(160, 4, 320)
        pieces = jnp.stack(
            [jnp.concatenate((low[:, j], high[:, j]), axis=1) for j in range(4)]
        )
        left = jnp.concatenate(
            [pick(pieces, y)] + [flip(pick(pieces, y ^ q), y=q) for q in (1, 2, 3)]
        )
    with jax.named_scope("right_gather"):
        right = rounds.reshape(2, 4, 160, 320).transpose(0, 2, 1, 3).reshape(320, 1280)
        right, left = lax.optimization_barrier((right, left))
        one, three, two = ring_gather(right, ({"z": 1}, {"z": 3}))
        rights = [right, one, two, three]
    with jax.named_scope("left_gather"):
        one, three, two = ring_gather(left, ({"xl": 1}, {"xl": 1, "xh": 1}))
        lefts = {(0, 0): left, (1, 0): one, (0, 1): two, (1, 1): three}

    with jax.named_scope("density_columns"):
        same, other, rights[2] = lax.optimization_barrier((same, other, rights[2]))
        first = jnp.where(xh == 0, same, other)
        second = jnp.where(xh == 0, other, same)
        cols = jnp.stack(
            [jnp.concatenate((first[:, j], second[:, j]), axis=1) for j in range(4)]
        )
        dslots = lax.all_to_all(cols, "y", split_axis=0, concat_axis=0, tiled=True)
        dslots = dslots.reshape(320, 640)

    with jax.named_scope("swap_matrix"):
        at = jnp.arange(1280, dtype=jnp.int32)
        to = at // 40 % 4 * 320 + at // 160 * 40 + at % 40
        swap = (to[:, None] == at[None, :]).astype(bf16)

    with jax.named_scope("first_product"):
        rights, dslots, swap = lax.optimization_barrier((rights, dslots, swap))
        rights = jnp.stack(rights)
        rsel = jnp.concatenate(
            [
                pick(rights, z ^ (nzh * 2 + (xh ^ r)))
                for r in range(2)
                for nzh in range(2)
            ]
        )
        theirs = [jnp.where(core == 0, lefts[1, r], lefts[0, r]) for r in range(2)]
        mine = [jnp.where(core == 0, lefts[0, r], lefts[1, r]) for r in range(2)]
        theirs = dot(jnp.concatenate(theirs, axis=1), rsel).reshape(4, 160, 1280)
        mine = dot(jnp.concatenate(mine, axis=1), rsel).reshape(4, 160, 1280)
    with jax.named_scope("mixed_sum"):
        both = [None] * 4
        for q in (2, 1, 3, 0):
            both[q] = mine[q] + flip(theirs[q], core=1)
        upper = flip(both[2][:80], y=1)
        lower = flip(both[2][80:], y=3)
        third = jnp.concatenate((both[3][:80] + upper, both[3][80:]))
        first = jnp.concatenate((both[1][:80], both[1][80:] + lower))
        sums = [flip(first, y=1), flip(third, y=3)]

    with jax.named_scope("density_gather"):
        dslots, _ = lax.optimization_barrier((dslots, both))
        dparts = [dslots] + [flip(dslots, z=q) for q in (1, 2, 3)]

    with jax.named_scope("mixed_sum"):
        sums, dparts = lax.optimization_barrier((sums, dparts))
        total = both[0] + sums[0] + sums[1]
        mixed = total.astype(bf16)

    with jax.named_scope("density_rows"):
        dparts = jnp.stack(dparts)
        dfull = jnp.concatenate([pick(dparts, z ^ nz) for nz in range(4)])

    with jax.named_scope("mixed_gather"):
        mslots = jnp.concatenate([mixed] + [flip(mixed, y=q) for q in (1, 2, 3)])
        mother = flip(mslots, core=1)

    with jax.named_scope("second_product"):
        near = dot(mslots, dfull).reshape(4, 160, 640)
        far = dot(mother, dfull).reshape(4, 160, 640)

        def piece(h, r):
            rows = jnp.where(core == h, near, far).reshape(8, 2, 40, 640)
            return lax.dynamic_index_in_dim(rows, xh ^ r, 1, keepdims=False).reshape(320, 640)

        total = piece(0, 0)
        for h, r in ((0, 1), (1, 0), (1, 1)):
            came = flip(piece(h, r).astype(bf16), xl=h, xh=r)
            total = total + came.astype(f32)
        total = total.reshape(4, 2, 40, 640)
        stay = lax.dynamic_index_in_dim(total, core, 1, keepdims=False)
        away = flip(lax.dynamic_index_in_dim(total, 1 - core, 1, keepdims=False), core=1)
        rows = jnp.where(
            core == 0,
            jnp.concatenate((stay, away), axis=2),
            jnp.concatenate((away, stay), axis=2),
        )

    with jax.named_scope("transposed"):
        sorted_rows = jnp.concatenate([pick(rows, y ^ ny) for ny in range(4)])
        turned = sorted_rows.astype(bf16).T.reshape(32, 40, 160)
        turned = lax.all_to_all(
            turned, ("z", "xl", "core", "xh"), split_axis=0, concat_axis=0, tiled=True
        )
        turned = turned.reshape(4, 8, 40, 160).transpose(0, 2, 1, 3).reshape(160, 1280)
        flipped = dot(turned, swap).reshape(4, 40, 1280)
        flipped = flipped.transpose(1, 0, 2).reshape(40, 5120)
    with jax.named_scope("direct"):
        direct = jnp.stack([rows[0]] + [flip(rows[q], y=q) for q in (1, 2, 3)])
        direct = direct.reshape(4, 40, 4, 320)
        long_rows = jnp.stack([pick(direct, y ^ ny) for ny in range(4)], axis=2)
        long_rows = long_rows.reshape(40, 5120)

    symmetric = 0.5 * (long_rows + flipped)
    first_row = ((((z * 4 + y) * 2 + xl) * 2 + core) * 2 + xh) * 40
    block_rows = (first_row + jnp.arange(40, dtype=jnp.int32)) // BLK
    block_count = pattern.shape[0]
    onehot = (
        block_rows[:, None] == jnp.arange(block_count, dtype=jnp.int32)[None, :]
    ).astype(f32)
    kept_blocks = jnp.dot(onehot, pattern.astype(f32), preferred_element_type=f32)
    kept_full = jnp.repeat(kept_blocks, BLK, axis=1)
    return symmetric * kept_full


def solution(mesh):
    fine = Mesh(mesh.devices.reshape(SIZES), AXES)
    split = P(("z", "y", "xl"), ("core", "xh"))
    return jax.shard_map(
        shards,
        mesh=fine,
        in_specs=(split, split, split, split, P()),
        out_specs=P(AXES, None),
        check_vma=False,
    )
```

```python
import jax
import jax.numpy as jnp
from jax import lax
from jax.experimental import pallas as pl
from jax.experimental.pallas import tpu as pltpu
from jax.sharding import Mesh
from jax.sharding import PartitionSpec as P

BLK = 128
AXES = ("z", "y", "xl", "core", "xh")
SIZES = (4, 4, 2, 2, 2)
f32 = jnp.float32
bf16 = jnp.bfloat16


def flip(value, z=0, y=0, xl=0, core=0, xh=0):
    masks = (z, y, xl, core, xh)
    pairs = []
    for source in range(128):
        rest, digits = source, []
        for size in reversed(SIZES):
            digits.append(rest % size)
            rest //= size
        target = 0
        for digit, size, mask in zip(reversed(digits), SIZES, masks):
            target = target * size + (digit ^ mask)
        pairs.append((source, target))
    return lax.ppermute(value, AXES, pairs)


def remap(value, rule):
    pairs = []
    for source in range(128):
        rest, digits = source, []
        for size in reversed(SIZES):
            digits.append(rest % size)
            rest //= size
        target = 0
        for digit, size in zip(rule(*reversed(digits)), SIZES):
            target = target * size + digit
        pairs.append((source, target))
    return lax.ppermute(value, AXES, pairs)


def pick(stack, index):
    return lax.dynamic_index_in_dim(stack, index, 0, keepdims=False)


def dot(a, b):
    return jnp.dot(a, b, preferred_element_type=f32)


VMEM = pl.BlockSpec(memory_space=pltpu.VMEM)
SMEM = pl.BlockSpec(memory_space=pltpu.SMEM)


def local_call(kernel, name, outs, coords, *operands, scratch=()):
    return pl.pallas_call(
        kernel,
        out_shape=outs,
        in_specs=[SMEM] + [VMEM] * len(operands),
        out_specs=jax.tree.map(lambda _: VMEM, outs),
        scratch_shapes=list(scratch),
        name=name,
    )(coords, *operands)


def shape(dtype, *dims):
    return jax.ShapeDtypeStruct(dims, dtype)


def left_kernel(at_ref, keep_ref, came_ref, *outs):
    y, core = at_ref[1], at_ref[3]
    low = jnp.where(core == 0, keep_ref[...], came_ref[...])
    high = jnp.where(core == 0, came_ref[...], keep_ref[...])
    for ny in range(4):
        cut = slice(ny * 320, ny * 320 + 320)
        piece = jnp.concatenate((low[:, cut], high[:, cut]), axis=1)
        for q in range(4):

            @pl.when((y ^ q) == ny)
            def _():
                outs[q][...] = piece


def right_kernel(at_ref, first_ref, second_ref, out_ref):
    for m, ref in enumerate((first_ref, second_ref)):
        whole = ref[...]
        for xl in range(2):
            for xh in range(2):
                out_ref[xl * 4 + m * 2 + xh] = jnp.concatenate(
                    [
                        whole[:, start : start + 40]
                        for ny in range(4)
                        for start in (
                            ny * 320 + xl * 160 + xh * 40,
                            ny * 320 + xl * 160 + 80 + xh * 40,
                        )
                    ],
                    axis=1,
                )


def density_kernel(at_ref, same_ref, other_ref, out_ref):
    xh = at_ref[4]
    first = jnp.where(xh == 0, same_ref[...], other_ref[...])
    second = jnp.where(xh == 0, other_ref[...], same_ref[...])
    for ny in range(4):
        cut = slice(ny * 320, ny * 320 + 320)
        out_ref[ny] = jnp.concatenate((first[:, cut], second[:, cut]), axis=1)


def combine_kernel(at_ref, own_ref, a_ref, b_ref, c_ref, stay_ref, away_ref):
    core = at_ref[3]
    for q in range(4):
        halves = []
        for nc in range(2):
            rows = slice((q * 2 + nc) * 40, (q * 2 + nc) * 40 + 40)
            halves.append(
                own_ref[rows]
                + a_ref[q * 2 + nc].astype(f32)
                + b_ref[q * 2 + nc].astype(f32)
                + c_ref[q * 2 + nc].astype(f32)
            )
        stay_ref[q] = jnp.where(core == 0, halves[0], halves[1])
        away_ref[q] = jnp.where(core == 0, halves[1], halves[0])


def spread_kernel(at_ref, stay_ref, came_ref, turned_ref, d0, d1, d2, d3, slots):
    y, core = at_ref[1], at_ref[3]
    for q, ref in enumerate((d0, d1, d2, d3)):
        low = jnp.where(core == 0, stay_ref[q], came_ref[q])
        high = jnp.where(core == 0, came_ref[q], stay_ref[q])
        ref[:, :640] = low
        ref[:, 640:] = high
        slots[y ^ q, :, :640] = low
        slots[y ^ q, :, 640:] = high
    for nz in range(4):
        part = jnp.concatenate(
            [slots[ny, :, nz * 320 : nz * 320 + 320] for ny in range(4)], axis=0
        )
        part = part.T
        for j in range(8):
            turned_ref[nz * 8 + j] = part[j * 40 : j * 40 + 40].astype(bf16)


def finish_kernel(at_ref, d0, d1, d2, d3, t_ref, kept_ref, out_ref, slots):
    for q, ref in enumerate((d0, d1, d2, d3)):
        slots[q] = ref[...]
    y = at_ref[1]
    for nz in range(4):
        blocks = []
        for ny in range(4):
            other = jnp.concatenate(
                [
                    t_ref[nz * 8 + s, :, ny * 40 : (ny + 1) * 40].astype(f32)
                    for s in range(8)
                ],
                axis=1,
            )
            blocks.append(slots[y ^ ny, :, nz * 320 : (nz + 1) * 320] + other)
        block = 0.5 * jnp.concatenate(blocks, axis=1)
        kept = jnp.concatenate(
            [
                jnp.broadcast_to(kept_ref[:, j : j + 1], (40, BLK))
                for j in range(nz * 10, nz * 10 + 10)
            ],
            axis=1,
        )
        out_ref[:, nz * 1280 : (nz + 1) * 1280] = block * kept


def shards(dens_resp, density, fock, fock_resp, pattern):
    z, y, xl, core, xh = (lax.axis_index(name) for name in AXES)
    coords = jnp.stack((z, y, xl, core, xh)).astype(jnp.int32)

    with jax.named_scope("left_columns"):
        keep = jnp.where(core == 0, dens_resp, density)
        send = jnp.where(core == 0, density, dens_resp)
        came = flip(send, core=1)
    with jax.named_scope("right_columns"):
        first, second, _ = lax.optimization_barrier((fock, fock_resp, send))
        parts = local_call(
            right_kernel, "right_columns", shape(bf16, 8, 160, 320), coords, first, second
        )
        rounds = lax.all_to_all(
            parts, ("xl", "core", "xh"), split_axis=0, concat_axis=0, tiled=True
        )
    with jax.named_scope("density_turn"):
        halves, _ = lax.optimization_barrier((density.reshape(2, 2, 40, 1280), send))
        same = lax.dynamic_index_in_dim(halves, xh, 1, keepdims=False).reshape(80, 1280)
        other = lax.dynamic_index_in_dim(halves, 1 - xh, 1, keepdims=False).reshape(80, 1280)
        other = flip(other, xh=1)
    with jax.named_scope("left_columns"):
        pieces = local_call(
            left_kernel, "left_columns", [shape(bf16, 160, 640)] * 4, coords, keep, came
        )
        left = jnp.concatenate([pieces[0]] + [flip(pieces[q], y=q) for q in (1, 2, 3)])
    with jax.named_scope("right_gather"):
        right = rounds.reshape(2, 4, 160, 320).transpose(0, 2, 1, 3).reshape(320, 1280)
        right, left = lax.optimization_barrier((right, left))
        rights = [right] + [flip(right, z=q) for q in (1, 2, 3)]
    with jax.named_scope("left_gather"):
        lefts = {
            (0, 0): left,
            (1, 0): flip(left, xl=1),
            (0, 1): flip(left, xh=1),
            (1, 1): flip(left, xl=1, xh=1),
        }

    with jax.named_scope("density_columns"):
        same, other, lefts[1, 0], lefts[1, 1] = lax.optimization_barrier(
            (same, other, lefts[1, 0], lefts[1, 1])
        )
        cols = local_call(
            density_kernel, "density_columns", shape(bf16, 4, 80, 640), coords, same, other
        )
        dslots = lax.all_to_all(cols, "y", split_axis=0, concat_axis=0, tiled=True)
        dslots = dslots.reshape(320, 640)

    with jax.named_scope("first_product"):
        rights, dslots = lax.optimization_barrier((rights, dslots))
        rights = jnp.stack(rights)
        rsel = jnp.concatenate(
            [
                pick(rights, z ^ (nzh * 2 + (xh ^ r)))
                for r in range(2)
                for nzh in range(2)
            ]
        )
        theirs = [jnp.where(core == 0, lefts[1, r], lefts[0, r]) for r in range(2)]
        mine = [jnp.where(core == 0, lefts[0, r], lefts[1, r]) for r in range(2)]
        theirs = dot(jnp.concatenate(theirs, axis=1), rsel).reshape(4, 160, 1280)
        mine = dot(jnp.concatenate(mine, axis=1), rsel).reshape(4, 160, 1280)
    with jax.named_scope("mixed_sum"):
        both = [None] * 4
        for q in (2, 1, 3, 0):
            both[q] = mine[q] + flip(theirs[q], core=1)
        upper = flip(both[2][:80], y=1)
        lower = flip(both[2][80:], y=3)
        third = jnp.concatenate((both[3][:80] + upper, both[3][80:]))
        first = jnp.concatenate((both[1][:80], both[1][80:] + lower))
        sums = [flip(first, y=1), flip(third, y=3)]

    with jax.named_scope("density_gather"):
        dslots, _ = lax.optimization_barrier((dslots, both))
        dparts = [dslots] + [flip(dslots, z=q) for q in (1, 2, 3)]

    with jax.named_scope("mixed_sum"):
        sums, dparts = lax.optimization_barrier((sums, dparts))
        total = both[0] + sums[0] + sums[1]
        mixed = total.astype(bf16)

    with jax.named_scope("density_rows"):
        dparts = jnp.stack(dparts)
        dfull = jnp.concatenate([pick(dparts, z ^ nz) for nz in range(4)])

    with jax.named_scope("mixed_gather"):
        mslots = jnp.concatenate([mixed] + [flip(mixed, y=q) for q in (1, 2, 3)])
        mother = flip(mslots, core=1)

    with jax.named_scope("second_product"):
        near = dot(mslots, dfull).reshape(4, 160, 640)
        far = dot(mother, dfull).reshape(4, 160, 640)

        def piece(h, r):
            rows = jnp.where(core == h, near, far).reshape(8, 2, 40, 640)
            return lax.dynamic_index_in_dim(rows, xh ^ r, 1, keepdims=False).reshape(320, 640)

        came = [
            flip(piece(h, r).astype(bf16), xl=h, xh=r).reshape(8, 40, 640)
            for h, r in ((0, 1), (1, 0), (1, 1))
        ]
        stay, away = local_call(
            combine_kernel, "combine", [shape(f32, 4, 40, 640)] * 2, coords, piece(0, 0), *came
        )
        away = flip(away, core=1)
        turned, *rows = local_call(
            spread_kernel,
            "spread",
            [shape(bf16, 32, 40, 160)] + [shape(f32, 40, 1280)] * 4,
            coords,
            stay,
            away,
            scratch=[pltpu.VMEM((4, 40, 1280), f32)],
        )

    with jax.named_scope("transposed"):
        turned = lax.all_to_all(
            turned, ("z", "xl", "core", "xh"), split_axis=0, concat_axis=0, tiled=True
        )
    with jax.named_scope("direct"):
        direct = [rows[0]] + [flip(rows[q], y=q) for q in (1, 2, 3)]

    first_row = ((((z * 4 + y) * 2 + xl) * 2 + core) * 2 + xh) * 40
    block_rows = (first_row + jnp.arange(40, dtype=jnp.int32)) // BLK
    block_count = pattern.shape[0]
    onehot = (
        block_rows[:, None] == jnp.arange(block_count, dtype=jnp.int32)[None, :]
    ).astype(f32)
    kept_blocks = jnp.dot(onehot, pattern.astype(f32), preferred_element_type=f32)
    return local_call(
        finish_kernel,
        "finish",
        shape(f32, 40, 5120),
        coords,
        *direct,
        turned,
        kept_blocks,
        scratch=[pltpu.VMEM((4, 40, 1280), f32)],
    )


def solution(mesh):
    fine = Mesh(mesh.devices.reshape(SIZES), AXES)
    split = P(("z", "y", "xl"), ("core", "xh"))
    return jax.shard_map(
        shards,
        mesh=fine,
        in_specs=(split, split, split, split, P()),
        out_specs=P(AXES, None),
        check_vma=False,
    )
```

```python
import jax
import jax.numpy as jnp
from jax import lax
from jax.experimental import pallas as pl
from jax.experimental.pallas import tpu as pltpu
from jax.sharding import Mesh
from jax.sharding import PartitionSpec as P

BLK = 128
AXES = ("z", "y", "xl", "core", "xh")
SIZES = (4, 4, 2, 2, 2)
f32 = jnp.float32
bf16 = jnp.bfloat16


def flip(value, z=0, y=0, xl=0, core=0, xh=0):
    masks = (z, y, xl, core, xh)
    pairs = []
    for source in range(128):
        rest, digits = source, []
        for size in reversed(SIZES):
            digits.append(rest % size)
            rest //= size
        target = 0
        for digit, size, mask in zip(reversed(digits), SIZES, masks):
            target = target * size + (digit ^ mask)
        pairs.append((source, target))
    return lax.ppermute(value, AXES, pairs)


def remap(value, rule):
    pairs = []
    for source in range(128):
        rest, digits = source, []
        for size in reversed(SIZES):
            digits.append(rest % size)
            rest //= size
        target = 0
        for digit, size in zip(rule(*reversed(digits)), SIZES):
            target = target * size + digit
        pairs.append((source, target))
    return lax.ppermute(value, AXES, pairs)


def pick(stack, index):
    return lax.dynamic_index_in_dim(stack, index, 0, keepdims=False)


def dot(a, b):
    return jnp.dot(a, b, preferred_element_type=f32)


VMEM = pl.BlockSpec(memory_space=pltpu.VMEM)
SMEM = pl.BlockSpec(memory_space=pltpu.SMEM)


def local_call(kernel, name, outs, coords, *operands, scratch=()):
    return pl.pallas_call(
        kernel,
        out_shape=outs,
        in_specs=[SMEM] + [VMEM] * len(operands),
        out_specs=jax.tree.map(lambda _: VMEM, outs),
        scratch_shapes=list(scratch),
        name=name,
    )(coords, *operands)


def shape(dtype, *dims):
    return jax.ShapeDtypeStruct(dims, dtype)


def left_kernel(at_ref, keep_ref, came_ref, *outs):
    y, core = at_ref[1], at_ref[3]
    low = jnp.where(core == 0, keep_ref[...], came_ref[...])
    high = jnp.where(core == 0, came_ref[...], keep_ref[...])
    for ny in range(4):
        cut = slice(ny * 320, ny * 320 + 320)
        piece = jnp.concatenate((low[:, cut], high[:, cut]), axis=1)
        for q in range(4):

            @pl.when((y ^ q) == ny)
            def _():
                outs[q][...] = piece


def right_kernel(at_ref, first_ref, second_ref, out_ref):
    for m, ref in enumerate((first_ref, second_ref)):
        whole = ref[...]
        for xl in range(2):
            for xh in range(2):
                out_ref[xl * 4 + m * 2 + xh] = jnp.concatenate(
                    [
                        whole[:, start : start + 40]
                        for ny in range(4)
                        for start in (
                            ny * 320 + xl * 160 + xh * 40,
                            ny * 320 + xl * 160 + 80 + xh * 40,
                        )
                    ],
                    axis=1,
                )


def density_kernel(at_ref, same_ref, other_ref, out_ref):
    xh = at_ref[4]
    first = jnp.where(xh == 0, same_ref[...], other_ref[...])
    second = jnp.where(xh == 0, other_ref[...], same_ref[...])
    for ny in range(4):
        cut = slice(ny * 320, ny * 320 + 320)
        out_ref[ny] = jnp.concatenate((first[:, cut], second[:, cut]), axis=1)


def combine_kernel(at_ref, own_ref, a_ref, b_ref, c_ref, stay_ref, away_ref):
    core = at_ref[3]
    for q in range(4):
        halves = []
        for nc in range(2):
            rows = slice((q * 2 + nc) * 40, (q * 2 + nc) * 40 + 40)
            halves.append(
                own_ref[rows]
                + a_ref[q * 2 + nc].astype(f32)
                + b_ref[q * 2 + nc].astype(f32)
                + c_ref[q * 2 + nc].astype(f32)
            )
        stay_ref[q] = jnp.where(core == 0, halves[0], halves[1])
        away_ref[q] = jnp.where(core == 0, halves[1], halves[0])


def spread_kernel(at_ref, stay_ref, came_ref, turned_ref, d0, d1, d2, d3, slots):
    y, core = at_ref[1], at_ref[3]
    for q, ref in enumerate((d0, d1, d2, d3)):
        low = jnp.where(core == 0, stay_ref[q], came_ref[q])
        high = jnp.where(core == 0, came_ref[q], stay_ref[q])
        ref[:, :640] = low
        ref[:, 640:] = high
        slots[y ^ q, :, :640] = low
        slots[y ^ q, :, 640:] = high
    for nz in range(4):
        part = jnp.concatenate(
            [slots[ny, :, nz * 320 : nz * 320 + 320] for ny in range(4)], axis=0
        )
        part = part.T
        for j in range(8):
            turned_ref[nz * 8 + j] = part[j * 40 : j * 40 + 40].astype(bf16)


def finish_kernel(at_ref, d0, d1, d2, d3, t_ref, kept_ref, out_ref, slots):
    for q, ref in enumerate((d0, d1, d2, d3)):
        slots[q] = ref[...]
    y = at_ref[1]
    for nz in range(4):
        blocks = []
        for ny in range(4):
            other = jnp.concatenate(
                [
                    t_ref[nz * 8 + s, :, ny * 40 : (ny + 1) * 40].astype(f32)
                    for s in range(8)
                ],
                axis=1,
            )
            blocks.append(slots[y ^ ny, :, nz * 320 : (nz + 1) * 320] + other)
        block = 0.5 * jnp.concatenate(blocks, axis=1)
        kept = jnp.concatenate(
            [
                jnp.broadcast_to(kept_ref[:, j : j + 1], (40, BLK))
                for j in range(nz * 10, nz * 10 + 10)
            ],
            axis=1,
        )
        out_ref[:, nz * 1280 : (nz + 1) * 1280] = block * kept


def shards(dens_resp, density, fock, fock_resp, pattern):
    z, y, xl, core, xh = (lax.axis_index(name) for name in AXES)
    coords = jnp.stack((z, y, xl, core, xh)).astype(jnp.int32)

    with jax.named_scope("left_columns"):
        keep = jnp.where(core == 0, dens_resp, density)
        send = jnp.where(core == 0, density, dens_resp)
        came = flip(send, core=1)
    with jax.named_scope("right_columns"):
        first, second, _ = lax.optimization_barrier((fock, fock_resp, send))
        parts = local_call(
            right_kernel, "right_columns", shape(bf16, 8, 160, 320), coords, first, second
        )
        rounds = lax.all_to_all(
            parts, ("xl", "core", "xh"), split_axis=0, concat_axis=0, tiled=True
        )
    with jax.named_scope("density_turn"):
        halves, _ = lax.optimization_barrier((density.reshape(2, 2, 40, 1280), send))
        same = lax.dynamic_index_in_dim(halves, xh, 1, keepdims=False).reshape(80, 1280)
        other = lax.dynamic_index_in_dim(halves, 1 - xh, 1, keepdims=False).reshape(80, 1280)
        other = flip(other, xh=1)
    with jax.named_scope("left_columns"):
        pieces = local_call(
            left_kernel, "left_columns", [shape(bf16, 160, 640)] * 4, coords, keep, came
        )
        left = jnp.concatenate([pieces[0]] + [flip(pieces[q], y=q) for q in (1, 2, 3)])
    with jax.named_scope("right_gather"):
        right = rounds.reshape(2, 4, 160, 320).transpose(0, 2, 1, 3).reshape(320, 1280)
        right, left, other = lax.optimization_barrier((right, left, other))
        rights = [right] + [flip(right, z=q) for q in (1, 2, 3)]
    with jax.named_scope("left_gather"):
        lefts = {
            (0, 0): left,
            (1, 0): flip(left, xl=1),
            (0, 1): flip(left, xh=1),
            (1, 1): flip(left, xl=1, xh=1),
        }

    with jax.named_scope("density_columns"):
        same, other, lefts[1, 0], lefts[1, 1] = lax.optimization_barrier(
            (same, other, lefts[1, 0], lefts[1, 1])
        )
        cols = local_call(
            density_kernel, "density_columns", shape(bf16, 4, 80, 640), coords, same, other
        )
        dslots = lax.all_to_all(cols, "y", split_axis=0, concat_axis=0, tiled=True)
        dslots = dslots.reshape(320, 640)

    with jax.named_scope("first_product"):
        rights, dslots = lax.optimization_barrier((rights, dslots))
        rights = jnp.stack(rights)
        rsel = jnp.concatenate(
            [
                pick(rights, z ^ (nzh * 2 + (xh ^ r)))
                for r in range(2)
                for nzh in range(2)
            ]
        )
        theirs = [jnp.where(core == 0, lefts[1, r], lefts[0, r]) for r in range(2)]
        mine = [jnp.where(core == 0, lefts[0, r], lefts[1, r]) for r in range(2)]
        theirs = dot(jnp.concatenate(theirs, axis=1), rsel).reshape(4, 160, 1280)
        mine = dot(jnp.concatenate(mine, axis=1), rsel).reshape(4, 160, 1280)
    with jax.named_scope("mixed_sum"):
        both = [None] * 4
        for q in (2, 1, 3, 0):
            both[q] = mine[q] + flip(theirs[q], core=1)
        upper = flip(both[2][:80], y=1)
        lower = flip(both[2][80:], y=3)
        third = jnp.concatenate((both[3][:80] + upper, both[3][80:]))
        first = jnp.concatenate((both[1][:80], both[1][80:] + lower))
        sums = [flip(first, y=1), flip(third, y=3)]

    with jax.named_scope("density_gather"):
        dslots, _ = lax.optimization_barrier((dslots, both))
        dparts = [dslots] + [flip(dslots, z=q) for q in (1, 2, 3)]

    with jax.named_scope("mixed_sum"):
        sums, dparts = lax.optimization_barrier((sums, dparts))
        total = both[0] + sums[0] + sums[1]
        mixed = total.astype(bf16)

    with jax.named_scope("density_rows"):
        dparts = jnp.stack(dparts)
        dfull = jnp.concatenate([pick(dparts, z ^ nz) for nz in range(4)])

    with jax.named_scope("mixed_gather"):
        mslots = jnp.concatenate([mixed] + [flip(mixed, y=q) for q in (1, 2, 3)])
        mother = flip(mslots, core=1)

    with jax.named_scope("second_product"):
        near = dot(mslots, dfull).reshape(4, 160, 640)
        far = dot(mother, dfull).reshape(4, 160, 640)

        def piece(h, r):
            rows = jnp.where(core == h, near, far).reshape(8, 2, 40, 640)
            return lax.dynamic_index_in_dim(rows, xh ^ r, 1, keepdims=False).reshape(320, 640)

        came = [
            flip(piece(h, r).astype(bf16), xl=h, xh=r).reshape(8, 40, 640)
            for h, r in ((0, 1), (1, 0), (1, 1))
        ]
        stay, away = local_call(
            combine_kernel, "combine", [shape(f32, 4, 40, 640)] * 2, coords, piece(0, 0), *came
        )
        away = flip(away, core=1)
        turned, *rows = local_call(
            spread_kernel,
            "spread",
            [shape(bf16, 32, 40, 160)] + [shape(f32, 40, 1280)] * 4,
            coords,
            stay,
            away,
            scratch=[pltpu.VMEM((4, 40, 1280), f32)],
        )

    with jax.named_scope("transposed"):
        turned = lax.all_to_all(
            turned, ("z", "xl", "core", "xh"), split_axis=0, concat_axis=0, tiled=True
        )
    with jax.named_scope("direct"):
        direct = [rows[0]] + [flip(rows[q], y=q) for q in (1, 2, 3)]

    first_row = ((((z * 4 + y) * 2 + xl) * 2 + core) * 2 + xh) * 40
    block_rows = (first_row + jnp.arange(40, dtype=jnp.int32)) // BLK
    block_count = pattern.shape[0]
    onehot = (
        block_rows[:, None] == jnp.arange(block_count, dtype=jnp.int32)[None, :]
    ).astype(f32)
    kept_blocks = jnp.dot(onehot, pattern.astype(f32), preferred_element_type=f32)
    return local_call(
        finish_kernel,
        "finish",
        shape(f32, 40, 5120),
        coords,
        *direct,
        turned,
        kept_blocks,
        scratch=[pltpu.VMEM((4, 40, 1280), f32)],
    )


def solution(mesh):
    fine = Mesh(mesh.devices.reshape(SIZES), AXES)
    split = P(("z", "y", "xl"), ("core", "xh"))
    return jax.shard_map(
        shards,
        mesh=fine,
        in_specs=(split, split, split, split, P()),
        out_specs=P(AXES, None),
        check_vma=False,
    )
```

```python
import jax
import jax.numpy as jnp
from jax import lax
from jax.experimental import pallas as pl
from jax.experimental.pallas import tpu as pltpu
from jax.sharding import Mesh
from jax.sharding import PartitionSpec as P

BLK = 128
AXES = ("z", "y", "xl", "core", "xh")
SIZES = (4, 4, 2, 2, 2)
f32 = jnp.float32
bf16 = jnp.bfloat16


def flip(value, z=0, y=0, xl=0, core=0, xh=0):
    masks = (z, y, xl, core, xh)
    pairs = []
    for source in range(128):
        rest, digits = source, []
        for size in reversed(SIZES):
            digits.append(rest % size)
            rest //= size
        target = 0
        for digit, size, mask in zip(reversed(digits), SIZES, masks):
            target = target * size + (digit ^ mask)
        pairs.append((source, target))
    return lax.ppermute(value, AXES, pairs)


def remap(value, rule):
    pairs = []
    for source in range(128):
        rest, digits = source, []
        for size in reversed(SIZES):
            digits.append(rest % size)
            rest //= size
        target = 0
        for digit, size in zip(rule(*reversed(digits)), SIZES):
            target = target * size + digit
        pairs.append((source, target))
    return lax.ppermute(value, AXES, pairs)


def pick(stack, index):
    return lax.dynamic_index_in_dim(stack, index, 0, keepdims=False)


def dot(a, b):
    return jnp.dot(a, b, preferred_element_type=f32)


VMEM = pl.BlockSpec(memory_space=pltpu.VMEM)
SMEM = pl.BlockSpec(memory_space=pltpu.SMEM)


def local_call(kernel, name, outs, coords, *operands, scratch=()):
    return pl.pallas_call(
        kernel,
        out_shape=outs,
        in_specs=[SMEM] + [VMEM] * len(operands),
        out_specs=jax.tree.map(lambda _: VMEM, outs),
        scratch_shapes=list(scratch),
        name=name,
    )(coords, *operands)


def shape(dtype, *dims):
    return jax.ShapeDtypeStruct(dims, dtype)


def left_kernel(at_ref, keep_ref, came_ref, *outs):
    y, core = at_ref[1], at_ref[3]
    low = jnp.where(core == 0, keep_ref[...], came_ref[...])
    high = jnp.where(core == 0, came_ref[...], keep_ref[...])
    for ny in range(4):
        cut = slice(ny * 320, ny * 320 + 320)
        piece = jnp.concatenate((low[:, cut], high[:, cut]), axis=1)
        for q in range(4):

            @pl.when((y ^ q) == ny)
            def _():
                outs[q][...] = piece


def right_kernel(at_ref, first_ref, second_ref, out_ref):
    for m, ref in enumerate((first_ref, second_ref)):
        whole = ref[...]
        for xl in range(2):
            for xh in range(2):
                out_ref[xl * 4 + m * 2 + xh] = jnp.concatenate(
                    [
                        whole[:, start : start + 40]
                        for ny in range(4)
                        for start in (
                            ny * 320 + xl * 160 + xh * 40,
                            ny * 320 + xl * 160 + 80 + xh * 40,
                        )
                    ],
                    axis=1,
                )


def density_kernel(at_ref, same_ref, other_ref, out_ref):
    xh = at_ref[4]
    first = jnp.where(xh == 0, same_ref[...], other_ref[...])
    second = jnp.where(xh == 0, other_ref[...], same_ref[...])
    for ny in range(4):
        cut = slice(ny * 320, ny * 320 + 320)
        out_ref[ny] = jnp.concatenate((first[:, cut], second[:, cut]), axis=1)


def spread_kernel(at_ref, *refs):
    many, last = refs[:4], refs[4:8]
    turned_ref, outs, slots = refs[8], refs[9:13], refs[13]
    y = at_ref[1]
    for q in range(4):
        parts = last if q == 2 else many
        place = 0 if q == 2 else (0, 1, None, 2)[q]
        total = parts[0][place].astype(f32)
        for ref in parts[1:]:
            total = total + ref[place].astype(f32)
        outs[q][...] = total
        slots[y ^ q] = total
    for nz in range(4):
        part = jnp.concatenate(
            [slots[ny, :, nz * 320 : nz * 320 + 320] for ny in range(4)], axis=0
        )
        part = part.T
        for j in range(8):
            turned_ref[nz * 8 + j] = part[j * 40 : j * 40 + 40].astype(bf16)


def finish_kernel(at_ref, d0, d1, d2, d3, t_ref, kept_ref, out_ref, slots):
    for q, ref in enumerate((d0, d1, d2, d3)):
        slots[q] = ref[...]
    y = at_ref[1]
    for nz in range(4):
        blocks = []
        for ny in range(4):
            other = jnp.concatenate(
                [
                    t_ref[nz * 8 + s, :, ny * 40 : (ny + 1) * 40].astype(f32)
                    for s in range(8)
                ],
                axis=1,
            )
            blocks.append(slots[y ^ ny, :, nz * 320 : (nz + 1) * 320] + other)
        block = 0.5 * jnp.concatenate(blocks, axis=1)
        kept = jnp.concatenate(
            [
                jnp.broadcast_to(kept_ref[:, j : j + 1], (40, BLK))
                for j in range(nz * 10, nz * 10 + 10)
            ],
            axis=1,
        )
        out_ref[:, nz * 1280 : (nz + 1) * 1280] = block * kept


def shards(dens_resp, density, fock, fock_resp, pattern):
    z, y, xl, core, xh = (lax.axis_index(name) for name in AXES)
    coords = jnp.stack((z, y, xl, core, xh)).astype(jnp.int32)

    with jax.named_scope("left_columns"):
        keep = jnp.where(core == 0, dens_resp, density)
        send = jnp.where(core == 0, density, dens_resp)
        came = flip(send, core=1)
    with jax.named_scope("right_columns"):
        first, second, _ = lax.optimization_barrier((fock, fock_resp, send))
        parts = local_call(
            right_kernel, "right_columns", shape(bf16, 8, 160, 320), coords, first, second
        )
        rounds = lax.all_to_all(
            parts, ("xl", "core", "xh"), split_axis=0, concat_axis=0, tiled=True
        )
    with jax.named_scope("density_turn"):
        halves, _ = lax.optimization_barrier((density.reshape(2, 2, 40, 1280), send))
        same = lax.dynamic_index_in_dim(halves, xh, 1, keepdims=False).reshape(80, 1280)
        other = lax.dynamic_index_in_dim(halves, 1 - xh, 1, keepdims=False).reshape(80, 1280)
        other = flip(other, xh=1)
    with jax.named_scope("left_columns"):
        pieces = local_call(
            left_kernel, "left_columns", [shape(bf16, 160, 640)] * 4, coords, keep, came
        )
        left = jnp.concatenate([pieces[0]] + [flip(pieces[q], y=q) for q in (1, 2, 3)])
    with jax.named_scope("right_gather"):
        right = rounds.reshape(2, 4, 160, 320).transpose(0, 2, 1, 3).reshape(320, 1280)
        right, left, other = lax.optimization_barrier((right, left, other))
        rights = [right] + [flip(right, z=q) for q in (1, 2, 3)]
    with jax.named_scope("left_gather"):
        lefts = {
            (0, 0): left,
            (1, 0): flip(left, xl=1),
            (0, 1): flip(left, xh=1),
            (1, 1): flip(left, xl=1, xh=1),
        }

    with jax.named_scope("density_columns"):
        same, other, lefts[1, 0] = lax.optimization_barrier((same, other, lefts[1, 0]))
        cols = local_call(
            density_kernel, "density_columns", shape(bf16, 4, 80, 640), coords, same, other
        )
        dslots = lax.all_to_all(cols, "y", split_axis=0, concat_axis=0, tiled=True)
        dslots = dslots.reshape(320, 640)

    with jax.named_scope("first_product"):
        rights, dslots = lax.optimization_barrier((rights, dslots))
        rights = jnp.stack(rights)
        rsel = jnp.concatenate(
            [
                pick(rights, z ^ (nzh * 2 + (xh ^ r)))
                for r in range(2)
                for nzh in range(2)
            ]
        )
        theirs = [jnp.where(core == 0, lefts[1, r], lefts[0, r]) for r in range(2)]
        mine = [jnp.where(core == 0, lefts[0, r], lefts[1, r]) for r in range(2)]
        theirs = dot(jnp.concatenate(theirs, axis=1), rsel).reshape(4, 160, 1280)
        mine = dot(jnp.concatenate(mine, axis=1), rsel).reshape(4, 160, 1280)
    with jax.named_scope("mixed_sum"):
        both = [None] * 4
        for q in (2, 1, 3, 0):
            both[q] = mine[q] + flip(theirs[q], core=1)
        upper = flip(both[2][:80], y=1)
        lower = flip(both[2][80:], y=3)
        third = jnp.concatenate((both[3][:80] + upper, both[3][80:]))
        first = jnp.concatenate((both[1][:80], both[1][80:] + lower))
        sums = [flip(first, y=1), flip(third, y=3)]

    with jax.named_scope("density_gather"):
        dslots, _ = lax.optimization_barrier((dslots, both))
        dparts = [dslots] + [flip(dslots, z=q) for q in (1, 2, 3)]

    with jax.named_scope("mixed_sum"):
        sums, dparts = lax.optimization_barrier((sums, dparts))
        total = both[0] + sums[0] + sums[1]
        mixed = total.astype(bf16)

    with jax.named_scope("density_rows"):
        mixed, dparts = lax.optimization_barrier((mixed, dparts))
        dmine = jnp.concatenate([pick(jnp.stack(dparts), z ^ nz) for nz in range(4)])
        dother = flip(dmine, core=1)
        dfull = jnp.where(
            core == 0,
            jnp.concatenate((dmine, dother), axis=1),
            jnp.concatenate((dother, dmine), axis=1),
        )

    with jax.named_scope("mixed_gather"):
        mslots = [mixed] + [flip(mixed, y=q) for q in (1, 2, 3)]

    with jax.named_scope("second_product"):
        turns = [(r, t) for r in range(2) for t in range(2)]

        def pieces_of(rows, count):
            resp = dot(rows, dfull).reshape(count, 2, 2, 40, 1280)
            cut = []
            for r, t in turns:
                piece = lax.dynamic_index_in_dim(resp, core ^ t, 1, keepdims=False)
                piece = lax.dynamic_index_in_dim(piece, xh ^ r, 1, keepdims=False)
                cut.append(piece.astype(bf16))
            return cut

        def scatter(cut):
            return [
                remap(piece, lambda a, b, c, d, e: (a, b, c ^ d, d ^ t, e ^ r))
                for piece, (r, t) in zip(cut, turns)
            ]

        many = pieces_of(jnp.concatenate((mslots[0], mslots[1], mslots[3])), 3)
        many = scatter(many)
        many[0], mslots[2] = lax.optimization_barrier((many[0], mslots[2]))
        last = scatter(pieces_of(mslots[2], 1))
        turned, *rows = local_call(
            spread_kernel,
            "spread",
            [shape(bf16, 32, 40, 160)] + [shape(f32, 40, 1280)] * 4,
            coords,
            *many,
            *last,
            scratch=[pltpu.VMEM((4, 40, 1280), f32)],
        )

    with jax.named_scope("transposed"):
        turned = lax.all_to_all(
            turned, ("z", "xl", "core", "xh"), split_axis=0, concat_axis=0, tiled=True
        )
    with jax.named_scope("direct"):
        direct = [rows[0]] + [flip(rows[q], y=q) for q in (1, 2, 3)]

    first_row = ((((z * 4 + y) * 2 + xl) * 2 + core) * 2 + xh) * 40
    block_rows = (first_row + jnp.arange(40, dtype=jnp.int32)) // BLK
    block_count = pattern.shape[0]
    onehot = (
        block_rows[:, None] == jnp.arange(block_count, dtype=jnp.int32)[None, :]
    ).astype(f32)
    kept_blocks = jnp.dot(onehot, pattern.astype(f32), preferred_element_type=f32)
    return local_call(
        finish_kernel,
        "finish",
        shape(f32, 40, 5120),
        coords,
        *direct,
        turned,
        kept_blocks,
        scratch=[pltpu.VMEM((4, 40, 1280), f32)],
    )


def solution(mesh):
    fine = Mesh(mesh.devices.reshape(SIZES), AXES)
    split = P(("z", "y", "xl"), ("core", "xh"))
    return jax.shard_map(
        shards,
        mesh=fine,
        in_specs=(split, split, split, split, P()),
        out_specs=P(AXES, None),
        check_vma=False,
    )
```

```python
import jax
import jax.numpy as jnp
from jax import lax
from jax.experimental import pallas as pl
from jax.experimental.pallas import tpu as pltpu
from jax.sharding import Mesh
from jax.sharding import PartitionSpec as P

BLK = 128
AXES = ("z", "y", "xl", "core", "xh")
SIZES = (4, 4, 2, 2, 2)
f32 = jnp.float32
bf16 = jnp.bfloat16


def flip(value, z=0, y=0, xl=0, core=0, xh=0):
    masks = (z, y, xl, core, xh)
    pairs = []
    for source in range(128):
        rest, digits = source, []
        for size in reversed(SIZES):
            digits.append(rest % size)
            rest //= size
        target = 0
        for digit, size, mask in zip(reversed(digits), SIZES, masks):
            target = target * size + (digit ^ mask)
        pairs.append((source, target))
    return lax.ppermute(value, AXES, pairs)


def remap(value, rule):
    pairs = []
    for source in range(128):
        rest, digits = source, []
        for size in reversed(SIZES):
            digits.append(rest % size)
            rest //= size
        target = 0
        for digit, size in zip(rule(*reversed(digits)), SIZES):
            target = target * size + digit
        pairs.append((source, target))
    return lax.ppermute(value, AXES, pairs)


def pick(stack, index):
    return lax.dynamic_index_in_dim(stack, index, 0, keepdims=False)


def dot(a, b):
    return jnp.dot(a, b, preferred_element_type=f32)


VMEM = pl.BlockSpec(memory_space=pltpu.VMEM)
SMEM = pl.BlockSpec(memory_space=pltpu.SMEM)


def local_call(kernel, name, outs, coords, *operands, scratch=()):
    return pl.pallas_call(
        kernel,
        out_shape=outs,
        in_specs=[SMEM] + [VMEM] * len(operands),
        out_specs=jax.tree.map(lambda _: VMEM, outs),
        scratch_shapes=list(scratch),
        name=name,
    )(coords, *operands)


def shape(dtype, *dims):
    return jax.ShapeDtypeStruct(dims, dtype)


def left_kernel(at_ref, first_ref, second_ref, came_ref, *outs):
    y, core = at_ref[1], at_ref[3]
    low = jnp.where(core == 0, first_ref[...], came_ref[...])
    high = jnp.where(core == 0, came_ref[...], second_ref[...])
    for ny in range(4):
        cut = slice(ny * 320, ny * 320 + 320)
        piece = jnp.concatenate((low[:, cut], high[:, cut]), axis=1)
        for q in range(4):

            @pl.when((y ^ q) == ny)
            def _():
                outs[q][...] = piece


def right_kernel(at_ref, first_ref, second_ref, out_ref):
    for m, ref in enumerate((first_ref, second_ref)):
        whole = ref[...]
        for xl in range(2):
            for xh in range(2):
                out_ref[xl * 4 + m * 2 + xh] = jnp.concatenate(
                    [
                        whole[:, start : start + 40]
                        for ny in range(4)
                        for start in (
                            ny * 320 + xl * 160 + xh * 40,
                            ny * 320 + xl * 160 + 80 + xh * 40,
                        )
                    ],
                    axis=1,
                )


def density_kernel(at_ref, same_ref, other_ref, out_ref):
    xh = at_ref[4]
    first = jnp.where(xh == 0, same_ref[...], other_ref[...])
    second = jnp.where(xh == 0, other_ref[...], same_ref[...])
    for ny in range(4):
        cut = slice(ny * 320, ny * 320 + 320)
        out_ref[ny] = jnp.concatenate((first[:, cut], second[:, cut]), axis=1)


def rows_kernel(at_ref, *refs):
    out_ref = refs[4]
    z = at_ref[0]
    for q in range(4):
        out_ref[pl.ds(pl.multiple_of((z ^ q) * 320, 320), 320), :] = refs[q][...]


def join_kernel(at_ref, mine_ref, other_ref, out_ref):
    core = at_ref[3]
    out_ref[:, :640] = jnp.where(core == 0, mine_ref[...], other_ref[...])
    out_ref[:, 640:] = jnp.where(core == 0, other_ref[...], mine_ref[...])


def spread_kernel(at_ref, *refs):
    many, last = refs[:4], refs[4:8]
    turned_ref, outs, slots = refs[8], refs[9:13], refs[13]
    y = at_ref[1]
    for q in range(4):
        parts = last if q == 2 else many
        place = 0 if q == 2 else (0, 1, None, 2)[q]
        total = parts[0][place].astype(f32)
        for ref in parts[1:]:
            total = total + ref[place].astype(f32)
        outs[q][...] = total
        slots[y ^ q] = total
    for nz in range(4):
        part = jnp.concatenate(
            [slots[ny, :, nz * 320 : nz * 320 + 320] for ny in range(4)], axis=0
        )
        part = part.T
        for j in range(8):
            turned_ref[nz * 8 + j] = part[j * 40 : j * 40 + 40].astype(bf16)


def finish_kernel(at_ref, d0, d1, d2, d3, t_ref, kept_ref, out_ref, slots):
    for q, ref in enumerate((d0, d1, d2, d3)):
        slots[q] = ref[...]
    y = at_ref[1]
    for nz in range(4):
        blocks = []
        for ny in range(4):
            other = jnp.concatenate(
                [
                    t_ref[nz * 8 + s, :, ny * 40 : (ny + 1) * 40].astype(f32)
                    for s in range(8)
                ],
                axis=1,
            )
            blocks.append(slots[y ^ ny, :, nz * 320 : (nz + 1) * 320] + other)
        block = 0.5 * jnp.concatenate(blocks, axis=1)
        kept = jnp.concatenate(
            [
                jnp.broadcast_to(kept_ref[:, j : j + 1], (40, BLK))
                for j in range(nz * 10, nz * 10 + 10)
            ],
            axis=1,
        )
        out_ref[:, nz * 1280 : (nz + 1) * 1280] = block * kept


def shards(dens_resp, density, fock, fock_resp, pattern):
    z, y, xl, core, xh = (lax.axis_index(name) for name in AXES)
    coords = jnp.stack((z, y, xl, core, xh)).astype(jnp.int32)

    with jax.named_scope("left_columns"):
        send = jnp.where(core == 0, density, dens_resp)
        came = flip(send, core=1)
    with jax.named_scope("right_columns"):
        first, second, _ = lax.optimization_barrier((fock, fock_resp, send))
        parts = local_call(
            right_kernel, "right_columns", shape(bf16, 8, 160, 320), coords, first, second
        )
    with jax.named_scope("density_turn"):
        halves, _ = lax.optimization_barrier((density.reshape(2, 2, 40, 1280), send))
        same = lax.dynamic_index_in_dim(halves, xh, 1, keepdims=False).reshape(80, 1280)
        other = lax.dynamic_index_in_dim(halves, 1 - xh, 1, keepdims=False).reshape(80, 1280)
        other = flip(other, xh=1)
    with jax.named_scope("left_columns"):
        pieces = local_call(
            left_kernel, "left_columns", [shape(bf16, 160, 640)] * 4, coords, dens_resp, density, came
        )
        parts, pieces = lax.optimization_barrier((parts, pieces))
        left = jnp.concatenate([pieces[0]] + [flip(pieces[q], y=q) for q in (1, 2, 3)])
        left, other = lax.optimization_barrier((left, other))
    with jax.named_scope("right_gather"):
        rounds = lax.all_to_all(
            parts, ("xl", "core", "xh"), split_axis=0, concat_axis=0, tiled=True
        )
        right = rounds.reshape(2, 4, 160, 320).transpose(0, 2, 1, 3).reshape(320, 1280)
        right, left = lax.optimization_barrier((right, left))
        rights = [right] + [flip(right, z=q) for q in (1, 2, 3)]
    with jax.named_scope("left_gather"):
        lefts = {
            (0, 0): left,
            (1, 0): flip(left, xl=1),
            (0, 1): flip(left, xh=1),
            (1, 1): flip(left, xl=1, xh=1),
        }

    with jax.named_scope("density_columns"):
        same, other, lefts[1, 0] = lax.optimization_barrier((same, other, lefts[1, 0]))
        cols = local_call(
            density_kernel, "density_columns", shape(bf16, 4, 80, 640), coords, same, other
        )
        dslots = lax.all_to_all(cols, "y", split_axis=0, concat_axis=0, tiled=True)
        dslots = dslots.reshape(320, 640)

    with jax.named_scope("first_product"):
        rights, dslots = lax.optimization_barrier((rights, dslots))
        rights = jnp.stack(rights)
        rsel = jnp.concatenate(
            [
                pick(rights, z ^ (nzh * 2 + (xh ^ r)))
                for r in range(2)
                for nzh in range(2)
            ]
        )
        theirs = [jnp.where(core == 0, lefts[1, r], lefts[0, r]) for r in range(2)]
        mine = [jnp.where(core == 0, lefts[0, r], lefts[1, r]) for r in range(2)]
        theirs = dot(jnp.concatenate(theirs, axis=1), rsel).reshape(4, 160, 1280)
        mine = dot(jnp.concatenate(mine, axis=1), rsel).reshape(4, 160, 1280)
    with jax.named_scope("mixed_sum"):
        both = [None] * 4
        for q in (2, 1, 3, 0):
            both[q] = mine[q] + flip(theirs[q], core=1)
        upper = flip(both[2][:80], y=1)
        lower = flip(both[2][80:], y=3)
        third = jnp.concatenate((both[3][:80] + upper, both[3][80:]))
        first = jnp.concatenate((both[1][:80], both[1][80:] + lower))
        sums = [flip(first, y=1), flip(third, y=3)]

    with jax.named_scope("density_gather"):
        dslots, _ = lax.optimization_barrier((dslots, both))
        dparts = [dslots] + [flip(dslots, z=q) for q in (1, 2, 3)]

    with jax.named_scope("mixed_sum"):
        sums, dparts = lax.optimization_barrier((sums, dparts))
        total = both[0] + sums[0] + sums[1]
        mixed = total.astype(bf16)

    with jax.named_scope("density_rows"):
        dmine = local_call(rows_kernel, "density_rows", shape(bf16, 1280, 640), coords, *dparts)
        dfull = local_call(
            join_kernel, "density_join", shape(bf16, 1280, 1280), coords, dmine, flip(dmine, core=1)
        )
    with jax.named_scope("mixed_gather"):
        mslots = [mixed] + [flip(mixed, y=q) for q in (1, 2, 3)]

    with jax.named_scope("second_product"):
        turns = [(r, t) for r in range(2) for t in range(2)]

        def pieces_of(rows, count):
            resp = dot(rows, dfull).reshape(count, 2, 2, 40, 1280)
            cut = []
            for r, t in turns:
                piece = lax.dynamic_index_in_dim(resp, core ^ t, 1, keepdims=False)
                piece = lax.dynamic_index_in_dim(piece, xh ^ r, 1, keepdims=False)
                cut.append(piece.astype(bf16))
            return cut

        def scatter(cut):
            return [
                remap(piece, lambda a, b, c, d, e: (a, b, c ^ d, d ^ t, e ^ r))
                for piece, (r, t) in zip(cut, turns)
            ]

        many = pieces_of(jnp.concatenate((mslots[0], mslots[1], mslots[3])), 3)
        many = scatter(many)
        many[0], mslots[2] = lax.optimization_barrier((many[0], mslots[2]))
        last = scatter(pieces_of(mslots[2], 1))
        turned, *rows = local_call(
            spread_kernel,
            "spread",
            [shape(bf16, 32, 40, 160)] + [shape(f32, 40, 1280)] * 4,
            coords,
            *many,
            *last,
            scratch=[pltpu.VMEM((4, 40, 1280), f32)],
        )

    with jax.named_scope("transposed"):
        turned = lax.all_to_all(
            turned, ("z", "xl", "core", "xh"), split_axis=0, concat_axis=0, tiled=True
        )
    with jax.named_scope("direct"):
        direct = [rows[0]] + [flip(rows[q], y=q) for q in (1, 2, 3)]

    first_row = ((((z * 4 + y) * 2 + xl) * 2 + core) * 2 + xh) * 40
    block_rows = (first_row + jnp.arange(40, dtype=jnp.int32)) // BLK
    block_count = pattern.shape[0]
    onehot = (
        block_rows[:, None] == jnp.arange(block_count, dtype=jnp.int32)[None, :]
    ).astype(f32)
    kept_blocks = jnp.dot(onehot, pattern.astype(f32), preferred_element_type=f32)
    return local_call(
        finish_kernel,
        "finish",
        shape(f32, 40, 5120),
        coords,
        *direct,
        turned,
        kept_blocks,
        scratch=[pltpu.VMEM((4, 40, 1280), f32)],
    )


def solution(mesh):
    fine = Mesh(mesh.devices.reshape(SIZES), AXES)
    split = P(("z", "y", "xl"), ("core", "xh"))
    return jax.shard_map(
        shards,
        mesh=fine,
        in_specs=(split, split, split, split, P()),
        out_specs=P(AXES, None),
        check_vma=False,
    )
```

```python
import jax
import jax.numpy as jnp
from jax import lax
from jax.experimental import pallas as pl
from jax.experimental.pallas import tpu as pltpu
from jax.sharding import Mesh
from jax.sharding import PartitionSpec as P

BLK = 128
AXES = ("z", "y", "xl", "core", "xh")
SIZES = (4, 4, 2, 2, 2)
f32 = jnp.float32
bf16 = jnp.bfloat16


def flip(value, z=0, y=0, xl=0, core=0, xh=0):
    masks = (z, y, xl, core, xh)
    pairs = []
    for source in range(128):
        rest, digits = source, []
        for size in reversed(SIZES):
            digits.append(rest % size)
            rest //= size
        target = 0
        for digit, size, mask in zip(reversed(digits), SIZES, masks):
            target = target * size + (digit ^ mask)
        pairs.append((source, target))
    return lax.ppermute(value, AXES, pairs)


def remap(value, rule):
    pairs = []
    for source in range(128):
        rest, digits = source, []
        for size in reversed(SIZES):
            digits.append(rest % size)
            rest //= size
        target = 0
        for digit, size in zip(rule(*reversed(digits)), SIZES):
            target = target * size + digit
        pairs.append((source, target))
    return lax.ppermute(value, AXES, pairs)


def pick(stack, index):
    return lax.dynamic_index_in_dim(stack, index, 0, keepdims=False)


def dot(a, b):
    return jnp.dot(a, b, preferred_element_type=f32)


VMEM = pl.BlockSpec(memory_space=pltpu.VMEM)
SMEM = pl.BlockSpec(memory_space=pltpu.SMEM)


def local_call(kernel, name, outs, coords, *operands, scratch=()):
    return pl.pallas_call(
        kernel,
        out_shape=outs,
        in_specs=[SMEM] + [VMEM] * len(operands),
        out_specs=jax.tree.map(lambda _: VMEM, outs),
        scratch_shapes=list(scratch),
        name=name,
    )(coords, *operands)


def shape(dtype, *dims):
    return jax.ShapeDtypeStruct(dims, dtype)


def left_kernel(at_ref, first_ref, second_ref, came_ref, *outs):
    y, core = at_ref[1], at_ref[3]
    low = jnp.where(core == 0, first_ref[...], came_ref[...])
    high = jnp.where(core == 0, came_ref[...], second_ref[...])
    for ny in range(4):
        cut = slice(ny * 320, ny * 320 + 320)
        piece = jnp.concatenate((low[:, cut], high[:, cut]), axis=1)
        for q in range(4):

            @pl.when((y ^ q) == ny)
            def _():
                outs[q][...] = piece


def right_kernel(at_ref, first_ref, second_ref, out_ref):
    for m, ref in enumerate((first_ref, second_ref)):
        whole = ref[...]
        for xl in range(2):
            for xh in range(2):
                out_ref[xl * 4 + m * 2 + xh] = jnp.concatenate(
                    [
                        whole[:, start : start + 40]
                        for ny in range(4)
                        for start in (
                            ny * 320 + xl * 160 + xh * 40,
                            ny * 320 + xl * 160 + 80 + xh * 40,
                        )
                    ],
                    axis=1,
                )


def density_kernel(at_ref, same_ref, other_ref, out_ref):
    xh = at_ref[4]
    first = jnp.where(xh == 0, same_ref[...], other_ref[...])
    second = jnp.where(xh == 0, other_ref[...], same_ref[...])
    for ny in range(4):
        cut = slice(ny * 320, ny * 320 + 320)
        out_ref[ny] = jnp.concatenate((first[:, cut], second[:, cut]), axis=1)


def rows_kernel(at_ref, own_ref, one_ref, upper_ref, lower_ref, three_ref, out_ref):
    z = at_ref[0]

    def place(q, start, count, ref):
        first = pl.multiple_of((z ^ q) * 320 + start, 160)
        out_ref[pl.ds(first, count), :] = ref[...]

    place(0, 0, 320, own_ref)
    place(1, 0, 320, one_ref)
    place(2, 0, 160, upper_ref)
    place(2, 160, 160, lower_ref)
    place(3, 0, 320, three_ref)


def second_kernel(at_ref, mine_ref, other_ref, *refs):
    rows, outs, whole = refs[:-5], refs[-5:-1], refs[-1]
    core, xh = at_ref[3], at_ref[4]
    for side, right in enumerate((mine_ref, other_ref)):
        first = 0
        for ref in rows:
            count = ref.shape[0] // 80
            whole[side, first : first + count] = dot(ref[...], right[...]).reshape(
                count, 2, 40, 640
            )
            first += count
    for i, out in enumerate(outs):
        r, t = i // 2, i % 2
        for side in range(2):
            for slot in range(out.shape[1]):
                out[side, slot] = whole[side, slot * 2 + (core ^ t), xh ^ r].astype(bf16)


def spread_kernel(at_ref, *refs):
    many, last = refs[:4], refs[4:8]
    turned_ref, outs, slots = refs[8], refs[9:13], refs[13]
    y, core = at_ref[1], at_ref[3]
    for q in range(4):
        parts = last if q == 2 else many
        place = 0 if q == 2 else (0, 1, None, 2)[q]

        def total(side):
            terms = [parts[i][side ^ (i % 2), place].astype(f32) for i in range(4)]
            return (terms[0] + terms[1]) + (terms[2] + terms[3])

        mine, other = total(0), total(1)
        low = jnp.where(core == 0, mine, other)
        high = jnp.where(core == 0, other, mine)
        outs[q][:, :640] = low
        outs[q][:, 640:] = high
        slots[y ^ q, :, :640] = low
        slots[y ^ q, :, 640:] = high
    for nz in range(4):
        part = jnp.concatenate(
            [slots[ny, :, nz * 320 : nz * 320 + 320] for ny in range(4)], axis=0
        )
        part = part.T
        for j in range(8):
            turned_ref[nz * 8 + j] = part[j * 40 : j * 40 + 40].astype(bf16)


def finish_kernel(at_ref, d0, d1, d2, d3, t_ref, kept_ref, out_ref, slots):
    for q, ref in enumerate((d0, d1, d2, d3)):
        slots[q] = ref[...]
    y = at_ref[1]
    for nz in range(4):
        blocks = []
        for ny in range(4):
            other = jnp.concatenate(
                [
                    t_ref[nz * 8 + s, :, ny * 40 : (ny + 1) * 40].astype(f32)
                    for s in range(8)
                ],
                axis=1,
            )
            blocks.append(slots[y ^ ny, :, nz * 320 : (nz + 1) * 320] + other)
        block = 0.5 * jnp.concatenate(blocks, axis=1)
        kept = jnp.concatenate(
            [
                jnp.broadcast_to(kept_ref[:, j : j + 1], (40, BLK))
                for j in range(nz * 10, nz * 10 + 10)
            ],
            axis=1,
        )
        out_ref[:, nz * 1280 : (nz + 1) * 1280] = block * kept


def shards(dens_resp, density, fock, fock_resp, pattern):
    z, y, xl, core, xh = (lax.axis_index(name) for name in AXES)
    coords = jnp.stack((z, y, xl, core, xh)).astype(jnp.int32)

    with jax.named_scope("left_columns"):
        send = jnp.where(core == 0, density, dens_resp)
        came = flip(send, core=1)
    with jax.named_scope("right_columns"):
        first, second, _ = lax.optimization_barrier((fock, fock_resp, send))
        parts = local_call(
            right_kernel, "right_columns", shape(bf16, 8, 160, 320), coords, first, second
        )
    with jax.named_scope("density_turn"):
        halves, _ = lax.optimization_barrier((density.reshape(2, 2, 40, 1280), send))
        same = lax.dynamic_index_in_dim(halves, xh, 1, keepdims=False).reshape(80, 1280)
        other = lax.dynamic_index_in_dim(halves, 1 - xh, 1, keepdims=False).reshape(80, 1280)
        other = flip(other, xh=1)
    with jax.named_scope("left_columns"):
        pieces = local_call(
            left_kernel, "left_columns", [shape(bf16, 160, 640)] * 4, coords, dens_resp, density, came
        )
        parts, pieces = lax.optimization_barrier((parts, pieces))
        left = jnp.concatenate([pieces[0]] + [flip(pieces[q], y=q) for q in (1, 2, 3)])
        left, other = lax.optimization_barrier((left, other))
    with jax.named_scope("right_gather"):
        rounds = lax.all_to_all(
            parts, ("xl", "core", "xh"), split_axis=0, concat_axis=0, tiled=True
        )
        right = rounds.reshape(2, 4, 160, 320).transpose(0, 2, 1, 3).reshape(320, 1280)
        right, left = lax.optimization_barrier((right, left))
        rights = [right] + [flip(right, z=q) for q in (1, 2, 3)]
    with jax.named_scope("left_gather"):
        lefts = {
            (0, 0): left,
            (1, 0): flip(left, xl=1),
            (0, 1): flip(left, xh=1),
            (1, 1): flip(left, xl=1, xh=1),
        }

    with jax.named_scope("density_columns"):
        same, other, lefts[1, 0] = lax.optimization_barrier((same, other, lefts[1, 0]))
        cols = local_call(
            density_kernel, "density_columns", shape(bf16, 4, 80, 640), coords, same, other
        )
        dslots = lax.all_to_all(cols, "y", split_axis=0, concat_axis=0, tiled=True)
        dslots = dslots.reshape(320, 640)

    with jax.named_scope("first_product"):
        rights, dslots = lax.optimization_barrier((rights, dslots))
        rights = jnp.stack(rights)
        rsel = jnp.concatenate(
            [
                pick(rights, z ^ (nzh * 2 + (xh ^ r)))
                for r in range(2)
                for nzh in range(2)
            ]
        )
        theirs = [jnp.where(core == 0, lefts[1, r], lefts[0, r]) for r in range(2)]
        mine = [jnp.where(core == 0, lefts[0, r], lefts[1, r]) for r in range(2)]
        theirs = dot(jnp.concatenate(theirs, axis=1), rsel).reshape(4, 160, 1280)
        mine = dot(jnp.concatenate(mine, axis=1), rsel).reshape(4, 160, 1280)
    with jax.named_scope("mixed_sum"):
        both = [None] * 4
        for q in (2, 1, 3, 0):
            both[q] = mine[q] + flip(theirs[q], core=1)
        upper = flip(both[2][:80], y=1)
        lower = flip(both[2][80:], y=3)

    with jax.named_scope("density_gather"):
        done = flip(dslots, z=1)
        dthree = flip(dslots, z=3)
        upper, lower, done, dthree = lax.optimization_barrier((upper, lower, done, dthree))
        dtwo = (flip(dthree[:160], z=1), flip(done[160:], z=3))

    with jax.named_scope("mixed_sum"):
        third = jnp.concatenate((both[3][:80] + upper, both[3][80:]))
        first = jnp.concatenate((both[1][:80], both[1][80:] + lower))
        sums = [flip(first, y=1), flip(third, y=3)]

    with jax.named_scope("density_rows"):
        dmine = local_call(
            rows_kernel, "density_rows", shape(bf16, 1280, 640), coords, dslots, done, *dtwo, dthree
        )

    with jax.named_scope("mixed_sum"):
        sums, dmine = lax.optimization_barrier((sums, dmine))
        total = both[0] + sums[0] + sums[1]
        mixed = total.astype(bf16)

    with jax.named_scope("mixed_gather"):
        one, three = flip(mixed, y=1), flip(mixed, y=3)
        dother = flip(dmine, core=1)
        two = (three[:80], one[80:])
        two, one, three = lax.optimization_barrier((two, one, three))
        two = (flip(two[0], y=1), flip(two[1], y=3))

    with jax.named_scope("second_product"):

        def scatter(count, *rows):
            cut = local_call(
                second_kernel,
                "second_product",
                [shape(bf16, 2, count, 40, 640)] * 4,
                coords,
                dmine,
                dother,
                *rows,
                scratch=[pltpu.VMEM((2, count * 2, 2, 40, 640), f32)],
            )
            turns = [(r, t) for r in range(2) for t in range(2)]
            return [
                remap(piece, lambda a, b, c, d, e: (a, b, c ^ d, d ^ t, e ^ r))
                for piece, (r, t) in zip(cut, turns)
            ]

        many = scatter(3, mixed, one, three)
        many[0], two = lax.optimization_barrier((many[0], two))
        last = scatter(1, *two)
        turned, *rows = local_call(
            spread_kernel,
            "spread",
            [shape(bf16, 32, 40, 160)] + [shape(f32, 40, 1280)] * 4,
            coords,
            *many,
            *last,
            scratch=[pltpu.VMEM((4, 40, 1280), f32)],
        )

    with jax.named_scope("transposed"):
        turned = lax.all_to_all(
            turned, ("z", "xl", "core", "xh"), split_axis=0, concat_axis=0, tiled=True
        )
    with jax.named_scope("direct"):
        direct = [rows[0]] + [flip(rows[q], y=q) for q in (1, 2, 3)]

    first_row = ((((z * 4 + y) * 2 + xl) * 2 + core) * 2 + xh) * 40
    block_rows = (first_row + jnp.arange(40, dtype=jnp.int32)) // BLK
    block_count = pattern.shape[0]
    onehot = (
        block_rows[:, None] == jnp.arange(block_count, dtype=jnp.int32)[None, :]
    ).astype(f32)
    kept_blocks = jnp.dot(onehot, pattern.astype(f32), preferred_element_type=f32)
    return local_call(
        finish_kernel,
        "finish",
        shape(f32, 40, 5120),
        coords,
        *direct,
        turned,
        kept_blocks,
        scratch=[pltpu.VMEM((4, 40, 1280), f32)],
    )


def solution(mesh):
    fine = Mesh(mesh.devices.reshape(SIZES), AXES)
    split = P(("z", "y", "xl"), ("core", "xh"))
    return jax.shard_map(
        shards,
        mesh=fine,
        in_specs=(split, split, split, split, P()),
        out_specs=P(AXES, None),
        check_vma=False,
    )
```

```python
import jax
import jax.numpy as jnp
from jax import lax
from jax.experimental import pallas as pl
from jax.experimental.pallas import tpu as pltpu
from jax.sharding import Mesh
from jax.sharding import PartitionSpec as P

BLK = 128
AXES = ("z", "y", "xl", "core", "xh")
SIZES = (4, 4, 2, 2, 2)
f32 = jnp.float32
bf16 = jnp.bfloat16


def flip(value, z=0, y=0, xl=0, core=0, xh=0):
    masks = (z, y, xl, core, xh)
    pairs = []
    for source in range(128):
        rest, digits = source, []
        for size in reversed(SIZES):
            digits.append(rest % size)
            rest //= size
        target = 0
        for digit, size, mask in zip(reversed(digits), SIZES, masks):
            target = target * size + (digit ^ mask)
        pairs.append((source, target))
    return lax.ppermute(value, AXES, pairs)


def remap(value, rule):
    pairs = []
    for source in range(128):
        rest, digits = source, []
        for size in reversed(SIZES):
            digits.append(rest % size)
            rest //= size
        target = 0
        for digit, size in zip(rule(*reversed(digits)), SIZES):
            target = target * size + digit
        pairs.append((source, target))
    return lax.ppermute(value, AXES, pairs)


def pick(stack, index):
    return lax.dynamic_index_in_dim(stack, index, 0, keepdims=False)


def dot(a, b):
    return jnp.dot(a, b, preferred_element_type=f32)


VMEM = pl.BlockSpec(memory_space=pltpu.VMEM)
SMEM = pl.BlockSpec(memory_space=pltpu.SMEM)


def local_call(kernel, name, outs, coords, *operands, scratch=()):
    return pl.pallas_call(
        kernel,
        out_shape=outs,
        in_specs=[SMEM] + [VMEM] * len(operands),
        out_specs=jax.tree.map(lambda _: VMEM, outs),
        scratch_shapes=list(scratch),
        name=name,
    )(coords, *operands)


def shape(dtype, *dims):
    return jax.ShapeDtypeStruct(dims, dtype)


def left_kernel(at_ref, first_ref, second_ref, came_ref, *outs):
    y, core = at_ref[1], at_ref[3]
    low = jnp.where(core == 0, first_ref[...], came_ref[...])
    high = jnp.where(core == 0, came_ref[...], second_ref[...])
    for ny in range(4):
        cut = slice(ny * 320, ny * 320 + 320)
        piece = jnp.concatenate((low[:, cut], high[:, cut]), axis=1)
        for q in range(4):

            @pl.when((y ^ q) == ny)
            def _():
                outs[q][...] = piece


def right_kernel(at_ref, first_ref, second_ref, out_ref):
    for m, ref in enumerate((first_ref, second_ref)):
        whole = ref[...]
        for xl in range(2):
            for xh in range(2):
                out_ref[xl * 4 + m * 2 + xh] = jnp.concatenate(
                    [
                        whole[:, start : start + 40]
                        for ny in range(4)
                        for start in (
                            ny * 320 + xl * 160 + xh * 40,
                            ny * 320 + xl * 160 + 80 + xh * 40,
                        )
                    ],
                    axis=1,
                )


def density_kernel(at_ref, same_ref, other_ref, out_ref):
    xh = at_ref[4]
    first = jnp.where(xh == 0, same_ref[...], other_ref[...])
    second = jnp.where(xh == 0, other_ref[...], same_ref[...])
    for ny in range(4):
        cut = slice(ny * 320, ny * 320 + 320)
        out_ref[ny] = jnp.concatenate((first[:, cut], second[:, cut]), axis=1)


def rows_kernel(at_ref, own_ref, one_ref, upper_ref, lower_ref, three_ref, out_ref):
    z = at_ref[0]

    def place(q, start, count, ref):
        first = pl.multiple_of((z ^ q) * 320 + start, 160)
        out_ref[pl.ds(first, count), :] = ref[...]

    place(0, 0, 320, own_ref)
    place(1, 0, 320, one_ref)
    place(2, 0, 160, upper_ref)
    place(2, 160, 160, lower_ref)
    place(3, 0, 320, three_ref)


def second_kernel(at_ref, mine_ref, other_ref, *refs):
    rows, outs, stack, whole = refs[:-6], refs[-6:-2], refs[-2], refs[-1]
    core, xh = at_ref[3], at_ref[4]
    first = 0
    for ref in rows:
        stack[first : first + ref.shape[0]] = ref[...]
        first += ref.shape[0]
    for side, right in enumerate((mine_ref, other_ref)):
        whole[side] = dot(stack[...], right[...]).reshape(first // 80, 2, 40, 640)
    for i, out in enumerate(outs):
        r, t = i // 2, i % 2
        for side in range(2):
            for slot in range(out.shape[1]):
                out[side, slot] = whole[side, slot * 2 + (core ^ t), xh ^ r].astype(bf16)


def spread_kernel(at_ref, *refs):
    many, last = refs[:4], refs[4:8]
    turned_ref, outs, slots = refs[8], refs[9:13], refs[13]
    y, core = at_ref[1], at_ref[3]
    for q in range(4):
        parts = last if q == 2 else many
        place = 0 if q == 2 else (0, 1, None, 2)[q]

        def total(side):
            terms = [parts[i][side ^ (i % 2), place].astype(f32) for i in range(4)]
            return (terms[0] + terms[1]) + (terms[2] + terms[3])

        mine, other = total(0), total(1)
        low = jnp.where(core == 0, mine, other)
        high = jnp.where(core == 0, other, mine)
        outs[q][:, :640] = low
        outs[q][:, 640:] = high
        slots[y ^ q, :, :640] = low
        slots[y ^ q, :, 640:] = high
    for nz in range(4):
        part = jnp.concatenate(
            [slots[ny, :, nz * 320 : nz * 320 + 320] for ny in range(4)], axis=0
        )
        part = part.T
        for j in range(8):
            turned_ref[nz * 8 + j] = part[j * 40 : j * 40 + 40].astype(bf16)


def finish_kernel(at_ref, d0, d1, d2, d3, t_ref, kept_ref, out_ref, slots):
    for q, ref in enumerate((d0, d1, d2, d3)):
        slots[q] = ref[...]
    y = at_ref[1]
    for nz in range(4):
        blocks = []
        for ny in range(4):
            other = jnp.concatenate(
                [
                    t_ref[nz * 8 + s, :, ny * 40 : (ny + 1) * 40].astype(f32)
                    for s in range(8)
                ],
                axis=1,
            )
            blocks.append(slots[y ^ ny, :, nz * 320 : (nz + 1) * 320] + other)
        block = 0.5 * jnp.concatenate(blocks, axis=1)
        kept = jnp.concatenate(
            [
                jnp.broadcast_to(kept_ref[:, j : j + 1], (40, BLK))
                for j in range(nz * 10, nz * 10 + 10)
            ],
            axis=1,
        )
        out_ref[:, nz * 1280 : (nz + 1) * 1280] = block * kept


def shards(dens_resp, density, fock, fock_resp, pattern):
    z, y, xl, core, xh = (lax.axis_index(name) for name in AXES)
    coords = jnp.stack((z, y, xl, core, xh)).astype(jnp.int32)

    with jax.named_scope("left_columns"):
        send = jnp.where(core == 0, density, dens_resp)
        came = flip(send, core=1)
    with jax.named_scope("right_columns"):
        first, second, _ = lax.optimization_barrier((fock, fock_resp, send))
        parts = local_call(
            right_kernel, "right_columns", shape(bf16, 8, 160, 320), coords, first, second
        )
    with jax.named_scope("density_turn"):
        halves, _ = lax.optimization_barrier((density.reshape(2, 2, 40, 1280), send))
        same = lax.dynamic_index_in_dim(halves, xh, 1, keepdims=False).reshape(80, 1280)
        other = lax.dynamic_index_in_dim(halves, 1 - xh, 1, keepdims=False).reshape(80, 1280)
        other = flip(other, xh=1)
    with jax.named_scope("left_columns"):
        pieces = local_call(
            left_kernel, "left_columns", [shape(bf16, 160, 640)] * 4, coords, dens_resp, density, came
        )
        parts, pieces = lax.optimization_barrier((parts, pieces))
        left = jnp.concatenate([pieces[0]] + [flip(pieces[q], y=q) for q in (1, 2, 3)])
        left, other = lax.optimization_barrier((left, other))
    with jax.named_scope("right_gather"):
        rounds = lax.all_to_all(
            parts, ("xl", "core", "xh"), split_axis=0, concat_axis=0, tiled=True
        )
        right = rounds.reshape(2, 4, 160, 320).transpose(0, 2, 1, 3).reshape(320, 1280)
        right, left = lax.optimization_barrier((right, left))
        rights = [right] + [flip(right, z=q) for q in (1, 2, 3)]
    with jax.named_scope("left_gather"):
        lefts = {
            (0, 0): left,
            (1, 0): flip(left, xl=1),
            (0, 1): flip(left, xh=1),
            (1, 1): flip(left, xl=1, xh=1),
        }

    with jax.named_scope("density_columns"):
        same, other, lefts[1, 0] = lax.optimization_barrier((same, other, lefts[1, 0]))
        cols = local_call(
            density_kernel, "density_columns", shape(bf16, 4, 80, 640), coords, same, other
        )
        dslots = lax.all_to_all(cols, "y", split_axis=0, concat_axis=0, tiled=True)
        dslots = dslots.reshape(320, 640)

    with jax.named_scope("first_product"):
        rights, dslots = lax.optimization_barrier((rights, dslots))
        rights = jnp.stack(rights)
        rsel = jnp.concatenate(
            [
                pick(rights, z ^ (nzh * 2 + (xh ^ r)))
                for r in range(2)
                for nzh in range(2)
            ]
        )
        theirs = [jnp.where(core == 0, lefts[1, r], lefts[0, r]) for r in range(2)]
        mine = [jnp.where(core == 0, lefts[0, r], lefts[1, r]) for r in range(2)]
        theirs = dot(jnp.concatenate(theirs, axis=1), rsel).reshape(4, 160, 1280)
        mine = dot(jnp.concatenate(mine, axis=1), rsel).reshape(4, 160, 1280)
    with jax.named_scope("mixed_sum"):
        both = [None] * 4
        for q in (2, 1, 3, 0):
            both[q] = mine[q] + flip(theirs[q], core=1)
        upper = flip(both[2][:80], y=1)
        lower = flip(both[2][80:], y=3)

    with jax.named_scope("density_gather"):
        done = flip(dslots, z=1)
        dthree = flip(dslots, z=3)
        upper, lower, done, dthree = lax.optimization_barrier((upper, lower, done, dthree))
        dtwo = (flip(dthree[:160], z=1), flip(done[160:], z=3))

    with jax.named_scope("mixed_sum"):
        third = jnp.concatenate((both[3][:80] + upper, both[3][80:]))
        first = jnp.concatenate((both[1][:80], both[1][80:] + lower))
        sums = [flip(first, y=1), flip(third, y=3)]

    with jax.named_scope("density_rows"):
        dmine = local_call(
            rows_kernel, "density_rows", shape(bf16, 1280, 640), coords, dslots, done, *dtwo, dthree
        )

    with jax.named_scope("mixed_sum"):
        sums, dmine = lax.optimization_barrier((sums, dmine))
        total = both[0] + sums[0] + sums[1]
        mixed = total.astype(bf16)

    with jax.named_scope("mixed_gather"):
        one, three = flip(mixed, y=1), flip(mixed, y=3)
        dother = flip(dmine, core=1)
        two = (three[:80], one[80:])
        two, one, three = lax.optimization_barrier((two, one, three))
        two = (flip(two[0], y=1), flip(two[1], y=3))

    with jax.named_scope("second_product"):

        def pieces_of(count, *rows):
            return local_call(
                second_kernel,
                "second_product",
                [shape(bf16, 2, count, 40, 640)] * 4,
                coords,
                dmine,
                dother,
                *rows,
                scratch=[
                    pltpu.VMEM((count * 160, 1280), bf16),
                    pltpu.VMEM((2, count * 2, 2, 40, 640), f32),
                ],
            )

        def scatter(cut):
            turns = [(r, t) for r in range(2) for t in range(2)]
            return [
                remap(piece, lambda a, b, c, d, e: (a, b, c ^ d, d ^ t, e ^ r))
                for piece, (r, t) in zip(cut, turns)
            ]

        cut = list(pieces_of(3, mixed, one, three))
        cut[3], two = lax.optimization_barrier((cut[3], two))
        many = scatter(cut)
        many[0], two = lax.optimization_barrier((many[0], two))
        last = scatter(pieces_of(1, *two))
        turned, *rows = local_call(
            spread_kernel,
            "spread",
            [shape(bf16, 32, 40, 160)] + [shape(f32, 40, 1280)] * 4,
            coords,
            *many,
            *last,
            scratch=[pltpu.VMEM((4, 40, 1280), f32)],
        )

    with jax.named_scope("transposed"):
        turned = lax.all_to_all(
            turned, ("z", "xl", "core", "xh"), split_axis=0, concat_axis=0, tiled=True
        )
    with jax.named_scope("direct"):
        direct = [rows[0]] + [flip(rows[q], y=q) for q in (1, 2, 3)]

    first_row = ((((z * 4 + y) * 2 + xl) * 2 + core) * 2 + xh) * 40
    block_rows = (first_row + jnp.arange(40, dtype=jnp.int32)) // BLK
    block_count = pattern.shape[0]
    onehot = (
        block_rows[:, None] == jnp.arange(block_count, dtype=jnp.int32)[None, :]
    ).astype(f32)
    kept_blocks = jnp.dot(onehot, pattern.astype(f32), preferred_element_type=f32)
    return local_call(
        finish_kernel,
        "finish",
        shape(f32, 40, 5120),
        coords,
        *direct,
        turned,
        kept_blocks,
        scratch=[pltpu.VMEM((4, 40, 1280), f32)],
    )


def solution(mesh):
    fine = Mesh(mesh.devices.reshape(SIZES), AXES)
    split = P(("z", "y", "xl"), ("core", "xh"))
    return jax.shard_map(
        shards,
        mesh=fine,
        in_specs=(split, split, split, split, P()),
        out_specs=P(AXES, None),
        check_vma=False,
    )
```

```python
import jax
import jax.numpy as jnp
from jax import lax
from jax.experimental import pallas as pl
from jax.experimental.pallas import tpu as pltpu
from jax.sharding import Mesh
from jax.sharding import PartitionSpec as P

BLK = 128
AXES = ("z", "y", "xl", "core", "xh")
SIZES = (4, 4, 2, 2, 2)
f32 = jnp.float32
bf16 = jnp.bfloat16


def flip(value, z=0, y=0, xl=0, core=0, xh=0):
    masks = (z, y, xl, core, xh)
    pairs = []
    for source in range(128):
        rest, digits = source, []
        for size in reversed(SIZES):
            digits.append(rest % size)
            rest //= size
        target = 0
        for digit, size, mask in zip(reversed(digits), SIZES, masks):
            target = target * size + (digit ^ mask)
        pairs.append((source, target))
    return lax.ppermute(value, AXES, pairs)


def remap(value, rule):
    pairs = []
    for source in range(128):
        rest, digits = source, []
        for size in reversed(SIZES):
            digits.append(rest % size)
            rest //= size
        target = 0
        for digit, size in zip(rule(*reversed(digits)), SIZES):
            target = target * size + digit
        pairs.append((source, target))
    return lax.ppermute(value, AXES, pairs)


def pick(stack, index):
    return lax.dynamic_index_in_dim(stack, index, 0, keepdims=False)


def dot(a, b):
    return jnp.dot(a, b, preferred_element_type=f32)


VMEM = pl.BlockSpec(memory_space=pltpu.VMEM)
SMEM = pl.BlockSpec(memory_space=pltpu.SMEM)


def local_call(kernel, name, outs, coords, *operands, scratch=()):
    return pl.pallas_call(
        kernel,
        out_shape=outs,
        in_specs=[SMEM] + [VMEM] * len(operands),
        out_specs=jax.tree.map(lambda _: VMEM, outs),
        scratch_shapes=list(scratch),
        name=name,
    )(coords, *operands)


def shape(dtype, *dims):
    return jax.ShapeDtypeStruct(dims, dtype)


def left_kernel(at_ref, first_ref, second_ref, came_ref, *outs):
    y, core = at_ref[1], at_ref[3]
    low = jnp.where(core == 0, first_ref[...], came_ref[...])
    high = jnp.where(core == 0, came_ref[...], second_ref[...])
    for ny in range(4):
        cut = slice(ny * 320, ny * 320 + 320)
        piece = jnp.concatenate((low[:, cut], high[:, cut]), axis=1)
        for q in range(4):

            @pl.when((y ^ q) == ny)
            def _():
                outs[q][...] = piece


def right_kernel(at_ref, first_ref, second_ref, out_ref):
    for m, ref in enumerate((first_ref, second_ref)):
        whole = ref[...]
        for xl in range(2):
            for xh in range(2):
                out_ref[xl * 4 + m * 2 + xh] = jnp.concatenate(
                    [
                        whole[:, start : start + 40]
                        for ny in range(4)
                        for start in (
                            ny * 320 + xl * 160 + xh * 40,
                            ny * 320 + xl * 160 + 80 + xh * 40,
                        )
                    ],
                    axis=1,
                )


def density_kernel(at_ref, same_ref, other_ref, out_ref):
    xh = at_ref[4]
    first = jnp.where(xh == 0, same_ref[...], other_ref[...])
    second = jnp.where(xh == 0, other_ref[...], same_ref[...])
    for ny in range(4):
        cut = slice(ny * 320, ny * 320 + 320)
        out_ref[ny] = jnp.concatenate((first[:, cut], second[:, cut]), axis=1)


def rows_kernel(at_ref, own_ref, one_ref, upper_ref, lower_ref, three_ref, out_ref):
    z = at_ref[0]

    def place(q, start, count, ref):
        first = pl.multiple_of((z ^ q) * 320 + start, 160)
        out_ref[pl.ds(first, count), :] = ref[...]

    place(0, 0, 320, own_ref)
    place(1, 0, 320, one_ref)
    place(2, 0, 160, upper_ref)
    place(2, 160, 160, lower_ref)
    place(3, 0, 320, three_ref)


def cut_kernel(at_ref, mine_ref, other_ref, *outs):
    core, xh = at_ref[3], at_ref[4]
    for i, out in enumerate(outs):
        r, t = i // 2, i % 2
        for side, ref in enumerate((mine_ref, other_ref)):
            for slot in range(out.shape[1]):
                out[side, slot] = ref[slot * 2 + (core ^ t), xh ^ r]


def spread_kernel(at_ref, *refs):
    many, last = refs[:4], refs[4:8]
    turned_ref, outs, slots = refs[8], refs[9:13], refs[13]
    y, core = at_ref[1], at_ref[3]
    for q in range(4):
        parts = last if q == 2 else many
        place = 0 if q == 2 else (0, 1, None, 2)[q]

        def total(side):
            terms = [parts[i][side ^ (i % 2), place].astype(f32) for i in range(4)]
            return (terms[0] + terms[1]) + (terms[2] + terms[3])

        mine, other = total(0), total(1)
        low = jnp.where(core == 0, mine, other)
        high = jnp.where(core == 0, other, mine)
        outs[q][:, :640] = low
        outs[q][:, 640:] = high
        slots[y ^ q, :, :640] = low
        slots[y ^ q, :, 640:] = high
    for nz in range(4):
        part = jnp.concatenate(
            [slots[ny, :, nz * 320 : nz * 320 + 320] for ny in range(4)], axis=0
        )
        part = part.T
        for j in range(8):
            turned_ref[nz * 8 + j] = part[j * 40 : j * 40 + 40].astype(bf16)


def finish_kernel(at_ref, d0, d1, d2, d3, t_ref, kept_ref, out_ref, slots):
    for q, ref in enumerate((d0, d1, d2, d3)):
        slots[q] = ref[...]
    y = at_ref[1]
    for nz in range(4):
        blocks = []
        for ny in range(4):
            other = jnp.concatenate(
                [
                    t_ref[nz * 8 + s, :, ny * 40 : (ny + 1) * 40].astype(f32)
                    for s in range(8)
                ],
                axis=1,
            )
            blocks.append(slots[y ^ ny, :, nz * 320 : (nz + 1) * 320] + other)
        block = 0.5 * jnp.concatenate(blocks, axis=1)
        kept = jnp.concatenate(
            [
                jnp.broadcast_to(kept_ref[:, j : j + 1], (40, BLK))
                for j in range(nz * 10, nz * 10 + 10)
            ],
            axis=1,
        )
        out_ref[:, nz * 1280 : (nz + 1) * 1280] = block * kept


def shards(dens_resp, density, fock, fock_resp, pattern):
    z, y, xl, core, xh = (lax.axis_index(name) for name in AXES)
    coords = jnp.stack((z, y, xl, core, xh)).astype(jnp.int32)

    with jax.named_scope("left_columns"):
        send = jnp.where(core == 0, density, dens_resp)
        came = flip(send, core=1)
    with jax.named_scope("right_columns"):
        first, second, _ = lax.optimization_barrier((fock, fock_resp, send))
        parts = local_call(
            right_kernel, "right_columns", shape(bf16, 8, 160, 320), coords, first, second
        )
    with jax.named_scope("density_turn"):
        halves, _ = lax.optimization_barrier((density.reshape(2, 2, 40, 1280), send))
        same = lax.dynamic_index_in_dim(halves, xh, 1, keepdims=False).reshape(80, 1280)
        other = lax.dynamic_index_in_dim(halves, 1 - xh, 1, keepdims=False).reshape(80, 1280)
        other = flip(other, xh=1)
    with jax.named_scope("left_columns"):
        pieces = local_call(
            left_kernel, "left_columns", [shape(bf16, 160, 640)] * 4, coords, dens_resp, density, came
        )
        parts, pieces = lax.optimization_barrier((parts, pieces))
        slots = [pieces[0]] + [flip(pieces[q], y=q) for q in (1, 2, 3)]
        left = jnp.concatenate(
            (
                slots[2][:80],
                slots[1][:80],
                slots[2][80:],
                slots[3][80:],
                slots[3][:80],
                slots[1][80:],
                slots[0],
            )
        )
        left, other = lax.optimization_barrier((left, other))
    with jax.named_scope("right_gather"):
        rounds = lax.all_to_all(
            parts, ("xl", "core", "xh"), split_axis=0, concat_axis=0, tiled=True
        )
        right = rounds.reshape(2, 4, 160, 320).transpose(0, 2, 1, 3).reshape(320, 1280)
        right, left = lax.optimization_barrier((right, left))
        rights = [right] + [flip(right, z=q) for q in (1, 2, 3)]
    with jax.named_scope("left_gather"):
        lefts = {
            (0, 0): left,
            (1, 0): flip(left, xl=1),
            (0, 1): flip(left, xh=1),
            (1, 1): flip(left, xl=1, xh=1),
        }

    with jax.named_scope("density_columns"):
        same, other, lefts[1, 0] = lax.optimization_barrier((same, other, lefts[1, 0]))
        cols = local_call(
            density_kernel, "density_columns", shape(bf16, 4, 80, 640), coords, same, other
        )
        dslots = lax.all_to_all(cols, "y", split_axis=0, concat_axis=0, tiled=True)
        dslots = dslots.reshape(320, 640)

    with jax.named_scope("first_product"):
        rights, dslots = lax.optimization_barrier((rights, dslots))
        rights = jnp.stack(rights)
        rsel = jnp.concatenate(
            [
                pick(rights, z ^ (nzh * 2 + (xh ^ r)))
                for r in range(2)
                for nzh in range(2)
            ]
        )
        theirs = [jnp.where(core == 0, lefts[1, r], lefts[0, r]) for r in range(2)]
        mine = [jnp.where(core == 0, lefts[0, r], lefts[1, r]) for r in range(2)]
        theirs = dot(jnp.concatenate(theirs, axis=1), rsel).reshape(4, 160, 1280)
        mine = dot(jnp.concatenate(mine, axis=1), rsel).reshape(4, 160, 1280)
    with jax.named_scope("mixed_sum"):
        both = [mine[g] + flip(theirs[g], core=1) for g in range(4)]
        upper = flip(both[0], y=1)
        lower = flip(both[1], y=3)

    with jax.named_scope("density_gather"):
        done = flip(dslots, z=1)
        dthree = flip(dslots, z=3)
        upper, lower, done, dthree = lax.optimization_barrier((upper, lower, done, dthree))
        dtwo = (flip(dthree[:160], z=1), flip(done[160:], z=3))

    with jax.named_scope("mixed_sum"):
        sums = [
            flip(both[2][:80] + upper[:80], y=3),
            flip(both[2][80:] + lower[:80], y=1),
        ]

    with jax.named_scope("density_rows"):
        dmine = local_call(
            rows_kernel, "density_rows", shape(bf16, 1280, 640), coords, dslots, done, *dtwo, dthree
        )

    with jax.named_scope("mixed_sum"):
        sums, dmine = lax.optimization_barrier((sums, dmine))
        total = both[3] + jnp.concatenate((upper[80:] + sums[0], lower[80:] + sums[1]))
        mixed = total.astype(bf16)

    with jax.named_scope("mixed_gather"):
        one, three = flip(mixed, y=1), flip(mixed, y=3)
        dother = flip(dmine, core=1)
        two = (three[:80], one[80:])
        two, one, three = lax.optimization_barrier((two, one, three))
        two = (flip(two[0], y=1), flip(two[1], y=3))

    with jax.named_scope("second_product"):

        def pieces_of(count, *rows):
            rows = jnp.concatenate(rows)
            parts = [
                dot(rows, right).astype(bf16).reshape(count * 2, 2, 40, 640)
                for right in (dmine, dother)
            ]
            return local_call(
                cut_kernel, "cut", [shape(bf16, 2, count, 40, 640)] * 4, coords, *parts
            )

        def scatter(cut):
            turns = [(r, t) for r in range(2) for t in range(2)]
            return [
                remap(piece, lambda a, b, c, d, e: (a, b, c ^ d, d ^ t, e ^ r))
                for piece, (r, t) in zip(cut, turns)
            ]

        cut = list(pieces_of(3, mixed, one, three))
        cut, two = lax.optimization_barrier((cut, two))
        many = scatter(cut)
        many[0], two = lax.optimization_barrier((many[0], two))
        last = scatter(pieces_of(1, *two))
        turned, *rows = local_call(
            spread_kernel,
            "spread",
            [shape(bf16, 32, 40, 160)] + [shape(f32, 40, 1280)] * 4,
            coords,
            *many,
            *last,
            scratch=[pltpu.VMEM((4, 40, 1280), f32)],
        )

    with jax.named_scope("transposed"):
        turned = lax.all_to_all(
            turned, ("z", "xl", "core", "xh"), split_axis=0, concat_axis=0, tiled=True
        )
    with jax.named_scope("direct"):
        direct = [rows[0]] + [flip(rows[q], y=q) for q in (1, 2, 3)]

    first_row = ((((z * 4 + y) * 2 + xl) * 2 + core) * 2 + xh) * 40
    block_rows = (first_row + jnp.arange(40, dtype=jnp.int32)) // BLK
    block_count = pattern.shape[0]
    onehot = (
        block_rows[:, None] == jnp.arange(block_count, dtype=jnp.int32)[None, :]
    ).astype(f32)
    kept_blocks = jnp.dot(onehot, pattern.astype(f32), preferred_element_type=f32)
    return local_call(
        finish_kernel,
        "finish",
        shape(f32, 40, 5120),
        coords,
        *direct,
        turned,
        kept_blocks,
        scratch=[pltpu.VMEM((4, 40, 1280), f32)],
    )


def solution(mesh):
    fine = Mesh(mesh.devices.reshape(SIZES), AXES)
    split = P(("z", "y", "xl"), ("core", "xh"))
    return jax.shard_map(
        shards,
        mesh=fine,
        in_specs=(split, split, split, split, P()),
        out_specs=P(AXES, None),
        check_vma=False,
    )
```

```python
import jax
import jax.numpy as jnp
from jax import lax
from jax.experimental import pallas as pl
from jax.experimental.pallas import tpu as pltpu
from jax.sharding import Mesh
from jax.sharding import PartitionSpec as P

BLK = 128
AXES = ("z", "y", "xl", "core", "xh")
SIZES = (4, 4, 2, 2, 2)
f32 = jnp.float32
bf16 = jnp.bfloat16


def flip(value, z=0, y=0, xl=0, core=0, xh=0):
    masks = (z, y, xl, core, xh)
    pairs = []
    for source in range(128):
        rest, digits = source, []
        for size in reversed(SIZES):
            digits.append(rest % size)
            rest //= size
        target = 0
        for digit, size, mask in zip(reversed(digits), SIZES, masks):
            target = target * size + (digit ^ mask)
        pairs.append((source, target))
    return lax.ppermute(value, AXES, pairs)


def remap(value, rule):
    pairs = []
    for source in range(128):
        rest, digits = source, []
        for size in reversed(SIZES):
            digits.append(rest % size)
            rest //= size
        target = 0
        for digit, size in zip(rule(*reversed(digits)), SIZES):
            target = target * size + digit
        pairs.append((source, target))
    return lax.ppermute(value, AXES, pairs)


def pick(stack, index):
    return lax.dynamic_index_in_dim(stack, index, 0, keepdims=False)


def dot(a, b):
    return jnp.dot(a, b, preferred_element_type=f32)


VMEM = pl.BlockSpec(memory_space=pltpu.VMEM)
SMEM = pl.BlockSpec(memory_space=pltpu.SMEM)


def local_call(kernel, name, outs, coords, *operands, scratch=()):
    return pl.pallas_call(
        kernel,
        out_shape=outs,
        in_specs=[SMEM] + [VMEM] * len(operands),
        out_specs=jax.tree.map(lambda _: VMEM, outs),
        scratch_shapes=list(scratch),
        name=name,
    )(coords, *operands)


def shape(dtype, *dims):
    return jax.ShapeDtypeStruct(dims, dtype)


def left_kernel(at_ref, first_ref, second_ref, *outs):
    y = at_ref[1]
    first, second = first_ref[...], second_ref[...]
    pieces = []
    for ny in range(4):
        cut = slice(ny * 320, ny * 320 + 320)
        pieces.append(jnp.concatenate((first[:, cut], second[:, cut]), axis=1))
    for q in range(4):
        low = jnp.where((y & 1) == 0, pieces[q], pieces[q ^ 1])
        high = jnp.where((y & 1) == 0, pieces[q ^ 2], pieces[q ^ 3])
        outs[q][...] = jnp.where((y & 2) == 0, low, high)


def pass_kernel(at_ref, *refs):
    core, out = at_ref[3], refs[4]
    for c in range(2):

        @pl.when(core == c)
        def _():
            for q in range(4):
                cut = slice(320 - c * 320, 640 - c * 320)
                out[q * 160 : q * 160 + 160] = refs[q][:, cut]


def pair_kernel(at_ref, *refs):
    core, came_ref, out = at_ref[3], refs[4], refs[5]
    for c in range(2):

        @pl.when(core == c)
        def _():
            for q in range(4):
                rows = slice(q * 160, q * 160 + 160)
                pair = [came_ref[rows], came_ref[rows]]
                pair[c] = refs[q][:, c * 320 : c * 320 + 320]
                out[rows] = jnp.concatenate(pair, axis=1)


def right_kernel(at_ref, first_ref, second_ref, out_ref):
    for m, ref in enumerate((first_ref, second_ref)):
        whole = ref[...]
        for xl in range(2):
            for xh in range(2):
                out_ref[xl * 4 + m * 2 + xh] = jnp.concatenate(
                    [
                        whole[:, start : start + 40]
                        for ny in range(4)
                        for start in (
                            ny * 320 + xl * 160 + xh * 40,
                            ny * 320 + xl * 160 + 80 + xh * 40,
                        )
                    ],
                    axis=1,
                )


def density_kernel(at_ref, same_ref, other_ref, out_ref):
    xh = at_ref[4]
    first = jnp.where(xh == 0, same_ref[...], other_ref[...])
    second = jnp.where(xh == 0, other_ref[...], same_ref[...])
    for ny in range(4):
        cut = slice(ny * 320, ny * 320 + 320)
        out_ref[ny] = jnp.concatenate((first[:, cut], second[:, cut]), axis=1)


def rows_kernel(at_ref, own_ref, one_ref, upper_ref, lower_ref, three_ref, out_ref):
    z = at_ref[0]

    def place(q, start, count, ref):
        first = pl.multiple_of((z ^ q) * 320 + start, 160)
        out_ref[pl.ds(first, count), :] = ref[...]

    place(0, 0, 320, own_ref)
    place(1, 0, 320, one_ref)
    place(2, 0, 160, upper_ref)
    place(2, 160, 160, lower_ref)
    place(3, 0, 320, three_ref)


def second_kernel(at_ref, mine_ref, other_ref, *refs):
    rows, outs, stack, whole = refs[:-6], refs[-6:-2], refs[-2], refs[-1]
    core, xh = at_ref[3], at_ref[4]
    first = 0
    for ref in rows:
        stack[first : first + ref.shape[0]] = ref[...]
        first += ref.shape[0]
    for side, right in enumerate((mine_ref, other_ref)):
        whole[side] = dot(stack[...], right[...]).reshape(first // 80, 2, 40, 640)
    for i, out in enumerate(outs):
        r, t = i // 2, i % 2
        for side in range(2):
            for slot in range(out.shape[1]):
                out[side, slot] = whole[side, slot * 2 + (core ^ t), xh ^ r].astype(bf16)


def spread_kernel(at_ref, *refs):
    many, last = refs[:4], refs[4:8]
    turned_ref, outs, slots = refs[8], refs[9:13], refs[13]
    y, core = at_ref[1], at_ref[3]
    for q in range(4):
        parts = last if q == 2 else many
        place = 0 if q == 2 else (0, 1, None, 2)[q]

        def total(side):
            terms = [parts[i][side ^ (i % 2), place].astype(f32) for i in range(4)]
            return (terms[0] + terms[1]) + (terms[2] + terms[3])

        mine, other = total(0), total(1)
        low = jnp.where(core == 0, mine, other)
        high = jnp.where(core == 0, other, mine)
        outs[q][:, :640] = low
        outs[q][:, 640:] = high
        slots[y ^ q, :, :640] = low
        slots[y ^ q, :, 640:] = high
    for nz in range(4):
        part = jnp.concatenate(
            [slots[ny, :, nz * 320 : nz * 320 + 320] for ny in range(4)], axis=0
        )
        part = part.T
        for j in range(8):
            turned_ref[nz * 8 + j] = part[j * 40 : j * 40 + 40].astype(bf16)


def finish_kernel(at_ref, d0, d1, d2, d3, t_ref, kept_ref, out_ref, slots):
    for q, ref in enumerate((d0, d1, d2, d3)):
        slots[q] = ref[...]
    y = at_ref[1]
    for nz in range(4):
        blocks = []
        for ny in range(4):
            other = jnp.concatenate(
                [
                    t_ref[nz * 8 + s, :, ny * 40 : (ny + 1) * 40].astype(f32)
                    for s in range(8)
                ],
                axis=1,
            )
            blocks.append(slots[y ^ ny, :, nz * 320 : (nz + 1) * 320] + other)
        block = 0.5 * jnp.concatenate(blocks, axis=1)
        kept = jnp.concatenate(
            [
                jnp.broadcast_to(kept_ref[:, j : j + 1], (40, BLK))
                for j in range(nz * 10, nz * 10 + 10)
            ],
            axis=1,
        )
        out_ref[:, nz * 1280 : (nz + 1) * 1280] = block * kept


def shards(dens_resp, density, fock, fock_resp, pattern):
    z, y, xl, core, xh = (lax.axis_index(name) for name in AXES)
    coords = jnp.stack((z, y, xl, core, xh)).astype(jnp.int32)

    with jax.named_scope("left_columns"):
        pieces = local_call(
            left_kernel, "left_columns", [shape(bf16, 160, 640)] * 4, coords, dens_resp, density
        )
        slots = [pieces[0]] + [flip(pieces[q], y=q) for q in (1, 2, 3)]
    with jax.named_scope("density_turn"):
        halves = density.reshape(2, 2, 40, 1280)
        same = lax.dynamic_index_in_dim(halves, xh, 1, keepdims=False).reshape(80, 1280)
        other = lax.dynamic_index_in_dim(halves, 1 - xh, 1, keepdims=False).reshape(80, 1280)
        other = flip(other, xh=1)
    with jax.named_scope("right_columns"):
        first, second, _ = lax.optimization_barrier((fock, fock_resp, pieces))
        parts = local_call(
            right_kernel, "right_columns", shape(bf16, 8, 160, 320), coords, first, second
        )
        parts, other = lax.optimization_barrier((parts, other))
    with jax.named_scope("left_pair"):
        came = local_call(pass_kernel, "left_pass", shape(bf16, 640, 320), coords, *slots)
        came = flip(came, core=1)
        left = local_call(pair_kernel, "left_pair", shape(bf16, 640, 640), coords, *slots, came)
    with jax.named_scope("right_gather"):
        rounds = lax.all_to_all(
            parts, ("xl", "core", "xh"), split_axis=0, concat_axis=0, tiled=True
        )
        right = rounds.reshape(2, 4, 160, 320).transpose(0, 2, 1, 3).reshape(320, 1280)
        right, left = lax.optimization_barrier((right, left))
        rights = [right] + [flip(right, z=q) for q in (1, 2, 3)]
    with jax.named_scope("left_gather"):
        lefts = {
            (0, 0): left,
            (1, 0): flip(left, xl=1),
            (0, 1): flip(left, xh=1),
            (1, 1): flip(left, xl=1, xh=1),
        }

    with jax.named_scope("density_columns"):
        same, other, lefts[1, 0] = lax.optimization_barrier((same, other, lefts[1, 0]))
        cols = local_call(
            density_kernel, "density_columns", shape(bf16, 4, 80, 640), coords, same, other
        )
        dslots = lax.all_to_all(cols, "y", split_axis=0, concat_axis=0, tiled=True)
        dslots = dslots.reshape(320, 640)

    with jax.named_scope("first_product"):
        rights, dslots = lax.optimization_barrier((rights, dslots))
        rights = jnp.stack(rights)
        rsel = jnp.concatenate(
            [
                pick(rights, z ^ (nzh * 2 + (xh ^ r)))
                for r in range(2)
                for nzh in range(2)
            ]
        )
        theirs = [jnp.where(core == 0, lefts[1, r], lefts[0, r]) for r in range(2)]
        mine = [jnp.where(core == 0, lefts[0, r], lefts[1, r]) for r in range(2)]
        theirs = dot(jnp.concatenate(theirs, axis=1), rsel).reshape(4, 160, 1280)
        mine = dot(jnp.concatenate(mine, axis=1), rsel).reshape(4, 160, 1280)
    with jax.named_scope("mixed_sum"):
        both = [None] * 4
        for q in (2, 1, 3, 0):
            both[q] = mine[q] + flip(theirs[q], core=1)
        upper = flip(both[2][:80], y=1)
        lower = flip(both[2][80:], y=3)

    with jax.named_scope("density_gather"):
        done = flip(dslots, z=1)
        dthree = flip(dslots, z=3)
        upper, lower, done, dthree = lax.optimization_barrier((upper, lower, done, dthree))
        dtwo = (flip(dthree[:160], z=1), flip(done[160:], z=3))

    with jax.named_scope("mixed_sum"):
        third = jnp.concatenate((both[3][:80] + upper, both[3][80:]))
        first = jnp.concatenate((both[1][:80], both[1][80:] + lower))
        sums = [flip(first, y=1), flip(third, y=3)]

    with jax.named_scope("density_rows"):
        dmine = local_call(
            rows_kernel, "density_rows", shape(bf16, 1280, 640), coords, dslots, done, *dtwo, dthree
        )

    with jax.named_scope("mixed_sum"):
        sums, dmine = lax.optimization_barrier((sums, dmine))
        total = both[0] + sums[0] + sums[1]
        mixed = total.astype(bf16)

    with jax.named_scope("mixed_gather"):
        one, three = flip(mixed, y=1), flip(mixed, y=3)
        dother = flip(dmine, core=1)
        two = (three[:80], one[80:])
        two, one, three = lax.optimization_barrier((two, one, three))
        two = (flip(two[0], y=1), flip(two[1], y=3))

    with jax.named_scope("second_product"):

        def pieces_of(count, *rows):
            return local_call(
                second_kernel,
                "second_product",
                [shape(bf16, 2, count, 40, 640)] * 4,
                coords,
                dmine,
                dother,
                *rows,
                scratch=[
                    pltpu.VMEM((count * 160, 1280), bf16),
                    pltpu.VMEM((2, count * 2, 2, 40, 640), f32),
                ],
            )

        def scatter(cut):
            turns = [(r, t) for r in range(2) for t in range(2)]
            return [
                remap(piece, lambda a, b, c, d, e: (a, b, c ^ d, d ^ t, e ^ r))
                for piece, (r, t) in zip(cut, turns)
            ]

        cut = list(pieces_of(3, mixed, one, three))
        cut[3], two = lax.optimization_barrier((cut[3], two))
        many = scatter(cut)
        many[0], two = lax.optimization_barrier((many[0], two))
        last = scatter(pieces_of(1, *two))
        turned, *rows = local_call(
            spread_kernel,
            "spread",
            [shape(bf16, 32, 40, 160)] + [shape(f32, 40, 1280)] * 4,
            coords,
            *many,
            *last,
            scratch=[pltpu.VMEM((4, 40, 1280), f32)],
        )

    with jax.named_scope("transposed"):
        turned = lax.all_to_all(
            turned, ("z", "xl", "core", "xh"), split_axis=0, concat_axis=0, tiled=True
        )
    with jax.named_scope("direct"):
        direct = [rows[0]] + [flip(rows[q], y=q) for q in (1, 2, 3)]

    first_row = ((((z * 4 + y) * 2 + xl) * 2 + core) * 2 + xh) * 40
    block_rows = (first_row + jnp.arange(40, dtype=jnp.int32)) // BLK
    block_count = pattern.shape[0]
    onehot = (
        block_rows[:, None] == jnp.arange(block_count, dtype=jnp.int32)[None, :]
    ).astype(f32)
    kept_blocks = jnp.dot(onehot, pattern.astype(f32), preferred_element_type=f32)
    return local_call(
        finish_kernel,
        "finish",
        shape(f32, 40, 5120),
        coords,
        *direct,
        turned,
        kept_blocks,
        scratch=[pltpu.VMEM((4, 40, 1280), f32)],
    )


def solution(mesh):
    fine = Mesh(mesh.devices.reshape(SIZES), AXES)
    split = P(("z", "y", "xl"), ("core", "xh"))
    return jax.shard_map(
        shards,
        mesh=fine,
        in_specs=(split, split, split, split, P()),
        out_specs=P(AXES, None),
        check_vma=False,
    )
```

```python
import jax
import jax.numpy as jnp
from jax import lax
from jax.experimental import pallas as pl
from jax.experimental.pallas import tpu as pltpu
from jax.sharding import Mesh
from jax.sharding import PartitionSpec as P

BLK = 128
AXES = ("z", "y", "xl", "core", "xh")
SIZES = (4, 4, 2, 2, 2)
f32 = jnp.float32
bf16 = jnp.bfloat16


def flip(value, z=0, y=0, xl=0, core=0, xh=0):
    masks = (z, y, xl, core, xh)
    pairs = []
    for source in range(128):
        rest, digits = source, []
        for size in reversed(SIZES):
            digits.append(rest % size)
            rest //= size
        target = 0
        for digit, size, mask in zip(reversed(digits), SIZES, masks):
            target = target * size + (digit ^ mask)
        pairs.append((source, target))
    return lax.ppermute(value, AXES, pairs)


def remap(value, rule):
    pairs = []
    for source in range(128):
        rest, digits = source, []
        for size in reversed(SIZES):
            digits.append(rest % size)
            rest //= size
        target = 0
        for digit, size in zip(rule(*reversed(digits)), SIZES):
            target = target * size + digit
        pairs.append((source, target))
    return lax.ppermute(value, AXES, pairs)


def pick(stack, index):
    return lax.dynamic_index_in_dim(stack, index, 0, keepdims=False)


def dot(a, b):
    return jnp.dot(a, b, preferred_element_type=f32)


VMEM = pl.BlockSpec(memory_space=pltpu.VMEM)
SMEM = pl.BlockSpec(memory_space=pltpu.SMEM)


def local_call(kernel, name, outs, coords, *operands, scratch=()):
    return pl.pallas_call(
        kernel,
        out_shape=outs,
        in_specs=[SMEM] + [VMEM] * len(operands),
        out_specs=jax.tree.map(lambda _: VMEM, outs),
        scratch_shapes=list(scratch),
        name=name,
    )(coords, *operands)


def shape(dtype, *dims):
    return jax.ShapeDtypeStruct(dims, dtype)


def left_kernel(at_ref, first_ref, second_ref, *outs):
    y = at_ref[1]
    first, second = first_ref[...], second_ref[...]
    pieces = []
    for ny in range(4):
        cut = slice(ny * 320, ny * 320 + 320)
        pieces.append(jnp.concatenate((first[:, cut], second[:, cut]), axis=1))
    for q in range(4):
        low = jnp.where((y & 1) == 0, pieces[q], pieces[q ^ 1])
        high = jnp.where((y & 1) == 0, pieces[q ^ 2], pieces[q ^ 3])
        outs[q][...] = jnp.where((y & 2) == 0, low, high)


def pass_kernel(at_ref, *refs):
    core, out = at_ref[3], refs[4]
    for c in range(2):

        @pl.when(core == c)
        def _():
            for q in range(4):
                cut = slice(320 - c * 320, 640 - c * 320)
                out[q * 160 : q * 160 + 160] = refs[q][:, cut]


def pair_kernel(at_ref, *refs):
    core, came_ref, out = at_ref[3], refs[4], refs[5]
    for c in range(2):

        @pl.when(core == c)
        def _():
            for q in range(4):
                rows = slice(q * 160, q * 160 + 160)
                pair = [came_ref[rows], came_ref[rows]]
                pair[c] = refs[q][:, c * 320 : c * 320 + 320]
                out[rows] = jnp.concatenate(pair, axis=1)


def right_kernel(at_ref, first_ref, second_ref, out_ref):
    for m, ref in enumerate((first_ref, second_ref)):
        whole = ref[...]
        for xl in range(2):
            for xh in range(2):
                out_ref[xl * 4 + m * 2 + xh] = jnp.concatenate(
                    [
                        whole[:, start : start + 40]
                        for ny in range(4)
                        for start in (
                            ny * 320 + xl * 160 + xh * 40,
                            ny * 320 + xl * 160 + 80 + xh * 40,
                        )
                    ],
                    axis=1,
                )


def density_kernel(at_ref, same_ref, other_ref, out_ref):
    xh = at_ref[4]
    first = jnp.where(xh == 0, same_ref[...], other_ref[...])
    second = jnp.where(xh == 0, other_ref[...], same_ref[...])
    for ny in range(4):
        cut = slice(ny * 320, ny * 320 + 320)
        out_ref[ny] = jnp.concatenate((first[:, cut], second[:, cut]), axis=1)


def rows_kernel(at_ref, own_ref, one_ref, upper_ref, lower_ref, three_ref, out_ref):
    z = at_ref[0]

    def place(q, start, count, ref):
        first = pl.multiple_of((z ^ q) * 320 + start, 160)
        out_ref[pl.ds(first, count), :] = ref[...]

    place(0, 0, 320, own_ref)
    place(1, 0, 320, one_ref)
    place(2, 0, 160, upper_ref)
    place(2, 160, 160, lower_ref)
    place(3, 0, 320, three_ref)


def second_kernel(at_ref, mine_ref, other_ref, *refs):
    rows, outs, stack, whole = refs[:-6], refs[-6:-2], refs[-2], refs[-1]
    core, xh = at_ref[3], at_ref[4]
    first = 0
    for ref in rows:
        stack[first : first + ref.shape[0]] = ref[...]
        first += ref.shape[0]
    for side, right in enumerate((mine_ref, other_ref)):
        whole[side] = dot(stack[...], right[...]).reshape(first // 80, 2, 40, 640)
    for i, out in enumerate(outs):
        r, t = i // 2, i % 2
        for side in range(2):
            for slot in range(out.shape[1]):
                out[side, slot] = whole[side, slot * 2 + (core ^ t), xh ^ r].astype(bf16)


def spread_kernel(at_ref, *refs):
    many, last = refs[:4], refs[4:8]
    turned_ref, outs, slots = refs[8], refs[9:13], refs[13]
    y, core = at_ref[1], at_ref[3]
    for q in range(4):
        parts = last if q == 2 else many
        place = 0 if q == 2 else (0, 1, None, 2)[q]

        def total(side):
            terms = [parts[i][side ^ (i % 2), place].astype(f32) for i in range(4)]
            return (terms[0] + terms[1]) + (terms[2] + terms[3])

        mine, other = total(0), total(1)
        low = jnp.where(core == 0, mine, other)
        high = jnp.where(core == 0, other, mine)
        outs[q][:, :640] = low
        outs[q][:, 640:] = high
        slots[y ^ q, :, :640] = low
        slots[y ^ q, :, 640:] = high
    for nz in range(4):
        part = jnp.concatenate(
            [slots[ny, :, nz * 320 : nz * 320 + 320] for ny in range(4)], axis=0
        )
        part = part.T
        for j in range(8):
            turned_ref[nz * 8 + j] = part[j * 40 : j * 40 + 40].astype(bf16)


def finish_kernel(at_ref, d0, d1, d2, d3, t_ref, kept_ref, out_ref, slots):
    for q, ref in enumerate((d0, d1, d2, d3)):
        slots[q] = ref[...]
    y = at_ref[1]
    for nz in range(4):
        blocks = []
        for ny in range(4):
            other = jnp.concatenate(
                [
                    t_ref[nz * 8 + s, :, ny * 40 : (ny + 1) * 40].astype(f32)
                    for s in range(8)
                ],
                axis=1,
            )
            blocks.append(slots[y ^ ny, :, nz * 320 : (nz + 1) * 320] + other)
        block = 0.5 * jnp.concatenate(blocks, axis=1)
        kept = jnp.concatenate(
            [
                jnp.broadcast_to(kept_ref[:, j : j + 1], (40, BLK))
                for j in range(nz * 10, nz * 10 + 10)
            ],
            axis=1,
        )
        out_ref[:, nz * 1280 : (nz + 1) * 1280] = block * kept


def shards(dens_resp, density, fock, fock_resp, pattern):
    z, y, xl, core, xh = (lax.axis_index(name) for name in AXES)
    coords = jnp.stack((z, y, xl, core, xh)).astype(jnp.int32)

    with jax.named_scope("left_columns"):
        pieces = local_call(
            left_kernel, "left_columns", [shape(bf16, 160, 640)] * 4, coords, dens_resp, density
        )
        slots = [pieces[0]] + [flip(pieces[q], y=q) for q in (1, 2, 3)]
    with jax.named_scope("density_turn"):
        halves, _ = lax.optimization_barrier((density.reshape(2, 2, 40, 1280), pieces))
        same = lax.dynamic_index_in_dim(halves, xh, 1, keepdims=False).reshape(80, 1280)
        other = lax.dynamic_index_in_dim(halves, 1 - xh, 1, keepdims=False).reshape(80, 1280)
        other = flip(other, xh=1)
    with jax.named_scope("right_columns"):
        first, second, _ = lax.optimization_barrier((fock, fock_resp, pieces))
        parts = local_call(
            right_kernel, "right_columns", shape(bf16, 8, 160, 320), coords, first, second
        )
        parts, slots[1] = lax.optimization_barrier((parts, slots[1]))
    with jax.named_scope("left_pair"):
        slots[2], other = lax.optimization_barrier((slots[2], other))
        came = local_call(pass_kernel, "left_pass", shape(bf16, 640, 320), coords, *slots)
        came = flip(came, core=1)
        left = local_call(pair_kernel, "left_pair", shape(bf16, 640, 640), coords, *slots, came)
    with jax.named_scope("right_gather"):
        rounds = lax.all_to_all(
            parts, ("xl", "core", "xh"), split_axis=0, concat_axis=0, tiled=True
        )
        right = rounds.reshape(2, 4, 160, 320).transpose(0, 2, 1, 3).reshape(320, 1280)
        right, left = lax.optimization_barrier((right, left))
        rights = [right] + [flip(right, z=q) for q in (1, 2, 3)]
    with jax.named_scope("left_gather"):
        lefts = {
            (0, 0): left,
            (1, 0): flip(left, xl=1),
            (0, 1): flip(left, xh=1),
            (1, 1): flip(left, xl=1, xh=1),
        }

    with jax.named_scope("density_columns"):
        same, other, lefts[1, 0] = lax.optimization_barrier((same, other, lefts[1, 0]))
        cols = local_call(
            density_kernel, "density_columns", shape(bf16, 4, 80, 640), coords, same, other
        )
        dslots = lax.all_to_all(cols, "y", split_axis=0, concat_axis=0, tiled=True)
        dslots = dslots.reshape(320, 640)

    with jax.named_scope("first_product"):
        rights, dslots = lax.optimization_barrier((rights, dslots))
        rights = jnp.stack(rights)
        rsel = jnp.concatenate(
            [
                pick(rights, z ^ (nzh * 2 + (xh ^ r)))
                for r in range(2)
                for nzh in range(2)
            ]
        )
        theirs = [jnp.where(core == 0, lefts[1, r], lefts[0, r]) for r in range(2)]
        mine = [jnp.where(core == 0, lefts[0, r], lefts[1, r]) for r in range(2)]
        theirs = dot(jnp.concatenate(theirs, axis=1), rsel).reshape(4, 160, 1280)
        mine = dot(jnp.concatenate(mine, axis=1), rsel).reshape(4, 160, 1280)
    with jax.named_scope("mixed_sum"):
        both = [None] * 4
        for q in (2, 1, 3, 0):
            both[q] = mine[q] + flip(theirs[q], core=1)
        upper = flip(both[2][:80], y=1)
        lower = flip(both[2][80:], y=3)

    with jax.named_scope("density_gather"):
        done = flip(dslots, z=1)
        dthree = flip(dslots, z=3)
        upper, lower, done, dthree = lax.optimization_barrier((upper, lower, done, dthree))
        dtwo = (flip(dthree[:160], z=1), flip(done[160:], z=3))

    with jax.named_scope("mixed_sum"):
        third = jnp.concatenate((both[3][:80] + upper, both[3][80:]))
        first = jnp.concatenate((both[1][:80], both[1][80:] + lower))
        sums = [flip(first, y=1), flip(third, y=3)]

    with jax.named_scope("density_rows"):
        dmine = local_call(
            rows_kernel, "density_rows", shape(bf16, 1280, 640), coords, dslots, done, *dtwo, dthree
        )

    with jax.named_scope("mixed_sum"):
        sums, dmine = lax.optimization_barrier((sums, dmine))
        total = both[0] + sums[0] + sums[1]
        mixed = total.astype(bf16)

    with jax.named_scope("mixed_gather"):
        one, three = flip(mixed, y=1), flip(mixed, y=3)
        dother = flip(dmine, core=1)
        two = (three[:80], one[80:])
        two, one, three = lax.optimization_barrier((two, one, three))
        two = (flip(two[0], y=1), flip(two[1], y=3))

    with jax.named_scope("second_product"):

        def pieces_of(count, *rows):
            return local_call(
                second_kernel,
                "second_product",
                [shape(bf16, 2, count, 40, 640)] * 4,
                coords,
                dmine,
                dother,
                *rows,
                scratch=[
                    pltpu.VMEM((count * 160, 1280), bf16),
                    pltpu.VMEM((2, count * 2, 2, 40, 640), f32),
                ],
            )

        def scatter(cut):
            turns = [(r, t) for r in range(2) for t in range(2)]
            return [
                remap(piece, lambda a, b, c, d, e: (a, b, c ^ d, d ^ t, e ^ r))
                for piece, (r, t) in zip(cut, turns)
            ]

        cut = list(pieces_of(3, mixed, one, three))
        cut[3], two = lax.optimization_barrier((cut[3], two))
        many = scatter(cut)
        many[0], two = lax.optimization_barrier((many[0], two))
        last = scatter(pieces_of(1, *two))
        turned, *rows = local_call(
            spread_kernel,
            "spread",
            [shape(bf16, 32, 40, 160)] + [shape(f32, 40, 1280)] * 4,
            coords,
            *many,
            *last,
            scratch=[pltpu.VMEM((4, 40, 1280), f32)],
        )

    with jax.named_scope("transposed"):
        turned = lax.all_to_all(
            turned, ("z", "xl", "core", "xh"), split_axis=0, concat_axis=0, tiled=True
        )
    with jax.named_scope("direct"):
        direct = [rows[0]] + [flip(rows[q], y=q) for q in (1, 2, 3)]

    first_row = ((((z * 4 + y) * 2 + xl) * 2 + core) * 2 + xh) * 40
    block_rows = (first_row + jnp.arange(40, dtype=jnp.int32)) // BLK
    block_count = pattern.shape[0]
    onehot = (
        block_rows[:, None] == jnp.arange(block_count, dtype=jnp.int32)[None, :]
    ).astype(f32)
    kept_blocks = jnp.dot(onehot, pattern.astype(f32), preferred_element_type=f32)
    return local_call(
        finish_kernel,
        "finish",
        shape(f32, 40, 5120),
        coords,
        *direct,
        turned,
        kept_blocks,
        scratch=[pltpu.VMEM((4, 40, 1280), f32)],
    )


def solution(mesh):
    fine = Mesh(mesh.devices.reshape(SIZES), AXES)
    split = P(("z", "y", "xl"), ("core", "xh"))
    return jax.shard_map(
        shards,
        mesh=fine,
        in_specs=(split, split, split, split, P()),
        out_specs=P(AXES, None),
        check_vma=False,
    )
```

```python
import jax
import jax.numpy as jnp
from jax import lax
from jax.experimental import pallas as pl
from jax.experimental.pallas import tpu as pltpu
from jax.sharding import Mesh
from jax.sharding import PartitionSpec as P

BLK = 128
AXES = ("z", "y", "xl", "core", "xh")
SIZES = (4, 4, 2, 2, 2)
f32 = jnp.float32
bf16 = jnp.bfloat16


def flip(value, z=0, y=0, xl=0, core=0, xh=0):
    masks = (z, y, xl, core, xh)
    pairs = []
    for source in range(128):
        rest, digits = source, []
        for size in reversed(SIZES):
            digits.append(rest % size)
            rest //= size
        target = 0
        for digit, size, mask in zip(reversed(digits), SIZES, masks):
            target = target * size + (digit ^ mask)
        pairs.append((source, target))
    return lax.ppermute(value, AXES, pairs)


def remap(value, rule):
    pairs = []
    for source in range(128):
        rest, digits = source, []
        for size in reversed(SIZES):
            digits.append(rest % size)
            rest //= size
        target = 0
        for digit, size in zip(rule(*reversed(digits)), SIZES):
            target = target * size + digit
        pairs.append((source, target))
    return lax.ppermute(value, AXES, pairs)


def pick(stack, index):
    return lax.dynamic_index_in_dim(stack, index, 0, keepdims=False)


def dot(a, b):
    return jnp.dot(a, b, preferred_element_type=f32)


VMEM = pl.BlockSpec(memory_space=pltpu.VMEM)
SMEM = pl.BlockSpec(memory_space=pltpu.SMEM)


def local_call(kernel, name, outs, coords, *operands, scratch=()):
    return pl.pallas_call(
        kernel,
        out_shape=outs,
        in_specs=[SMEM] + [VMEM] * len(operands),
        out_specs=jax.tree.map(lambda _: VMEM, outs),
        scratch_shapes=list(scratch),
        name=name,
    )(coords, *operands)


def shape(dtype, *dims):
    return jax.ShapeDtypeStruct(dims, dtype)


def left_kernel(at_ref, first_ref, second_ref, came_ref, *outs):
    y, core = at_ref[1], at_ref[3]
    low = jnp.where(core == 0, first_ref[...], came_ref[...])
    high = jnp.where(core == 0, came_ref[...], second_ref[...])
    for ny in range(4):
        cut = slice(ny * 320, ny * 320 + 320)
        piece = jnp.concatenate((low[:, cut], high[:, cut]), axis=1)
        for q in range(4):

            @pl.when((y ^ q) == ny)
            def _():
                outs[q][...] = piece


def right_kernel(at_ref, first_ref, second_ref, out_ref):
    for m, ref in enumerate((first_ref, second_ref)):
        whole = ref[...]
        for xl in range(2):
            for xh in range(2):
                out_ref[xl * 4 + m * 2 + xh] = jnp.concatenate(
                    [
                        whole[:, start : start + 40]
                        for ny in range(4)
                        for start in (
                            ny * 320 + xl * 160 + xh * 40,
                            ny * 320 + xl * 160 + 80 + xh * 40,
                        )
                    ],
                    axis=1,
                )


def density_kernel(at_ref, same_ref, other_ref, out_ref):
    xh = at_ref[4]
    first = jnp.where(xh == 0, same_ref[...], other_ref[...])
    second = jnp.where(xh == 0, other_ref[...], same_ref[...])
    for ny in range(4):
        cut = slice(ny * 320, ny * 320 + 320)
        out_ref[ny] = jnp.concatenate((first[:, cut], second[:, cut]), axis=1)


def rows_kernel(at_ref, own_ref, one_ref, upper_ref, lower_ref, three_ref, out_ref):
    z = at_ref[0]

    def place(q, start, count, ref):
        first = pl.multiple_of((z ^ q) * 320 + start, 160)
        out_ref[pl.ds(first, count), :] = ref[...]

    place(0, 0, 320, own_ref)
    place(1, 0, 320, one_ref)
    place(2, 0, 160, upper_ref)
    place(2, 160, 160, lower_ref)
    place(3, 0, 320, three_ref)


def join_kernel(at_ref, mine_ref, other_ref, out_ref):
    core = at_ref[3]
    out_ref[:, :640] = jnp.where(core == 0, mine_ref[...], other_ref[...])
    out_ref[:, 640:] = jnp.where(core == 0, other_ref[...], mine_ref[...])


def spread_kernel(at_ref, *refs):
    many, last = refs[:4], refs[4:8]
    turned_ref, outs, slots = refs[8], refs[9:13], refs[13]
    y = at_ref[1]
    for q in range(4):
        parts = last if q == 2 else many
        place = 0 if q == 2 else (0, 1, None, 2)[q]
        total = parts[0][place].astype(f32)
        for ref in parts[1:]:
            total = total + ref[place].astype(f32)
        outs[q][...] = total
        slots[y ^ q] = total
    for nz in range(4):
        part = jnp.concatenate(
            [slots[ny, :, nz * 320 : nz * 320 + 320] for ny in range(4)], axis=0
        )
        part = part.T
        for j in range(8):
            turned_ref[nz * 8 + j] = part[j * 40 : j * 40 + 40].astype(bf16)


def finish_kernel(at_ref, d0, d1, d2, d3, t_ref, kept_ref, out_ref, slots):
    for q, ref in enumerate((d0, d1, d2, d3)):
        slots[q] = ref[...]
    y = at_ref[1]
    for nz in range(4):
        blocks = []
        for ny in range(4):
            other = jnp.concatenate(
                [
                    t_ref[nz * 8 + s, :, ny * 40 : (ny + 1) * 40].astype(f32)
                    for s in range(8)
                ],
                axis=1,
            )
            blocks.append(slots[y ^ ny, :, nz * 320 : (nz + 1) * 320] + other)
        block = 0.5 * jnp.concatenate(blocks, axis=1)
        kept = jnp.concatenate(
            [
                jnp.broadcast_to(kept_ref[:, j : j + 1], (40, BLK))
                for j in range(nz * 10, nz * 10 + 10)
            ],
            axis=1,
        )
        out_ref[:, nz * 1280 : (nz + 1) * 1280] = block * kept


def shards(dens_resp, density, fock, fock_resp, pattern):
    z, y, xl, core, xh = (lax.axis_index(name) for name in AXES)
    coords = jnp.stack((z, y, xl, core, xh)).astype(jnp.int32)

    with jax.named_scope("left_columns"):
        send = jnp.where(core == 0, density, dens_resp)
        came = flip(send, core=1)
    with jax.named_scope("right_columns"):
        first, second, _ = lax.optimization_barrier((fock, fock_resp, send))
        parts = local_call(
            right_kernel, "right_columns", shape(bf16, 8, 160, 320), coords, first, second
        )
    with jax.named_scope("density_turn"):
        halves, _ = lax.optimization_barrier((density.reshape(2, 2, 40, 1280), send))
        same = lax.dynamic_index_in_dim(halves, xh, 1, keepdims=False).reshape(80, 1280)
        other = lax.dynamic_index_in_dim(halves, 1 - xh, 1, keepdims=False).reshape(80, 1280)
        other = flip(other, xh=1)
    with jax.named_scope("left_columns"):
        pieces = local_call(
            left_kernel, "left_columns", [shape(bf16, 160, 640)] * 4, coords, dens_resp, density, came
        )
        parts, pieces = lax.optimization_barrier((parts, pieces))
        left = jnp.concatenate([pieces[0]] + [flip(pieces[q], y=q) for q in (1, 2, 3)])
        left, other = lax.optimization_barrier((left, other))
    with jax.named_scope("right_gather"):
        rounds = lax.all_to_all(
            parts, ("xl", "core", "xh"), split_axis=0, concat_axis=0, tiled=True
        )
        right = rounds.reshape(2, 4, 160, 320).transpose(0, 2, 1, 3).reshape(320, 1280)
        right, left = lax.optimization_barrier((right, left))
        rights = [right] + [flip(right, z=q) for q in (1, 2, 3)]
    with jax.named_scope("left_gather"):
        lefts = {
            (0, 0): left,
            (1, 0): flip(left, xl=1),
            (0, 1): flip(left, xh=1),
            (1, 1): flip(left, xl=1, xh=1),
        }

    with jax.named_scope("density_columns"):
        same, other, lefts[1, 0] = lax.optimization_barrier((same, other, lefts[1, 0]))
        cols = local_call(
            density_kernel, "density_columns", shape(bf16, 4, 80, 640), coords, same, other
        )
        dslots = lax.all_to_all(cols, "y", split_axis=0, concat_axis=0, tiled=True)
        dslots = dslots.reshape(320, 640)

    with jax.named_scope("first_product"):
        rights, dslots = lax.optimization_barrier((rights, dslots))
        rights = jnp.stack(rights)
        rsel = jnp.concatenate(
            [
                pick(rights, z ^ (nzh * 2 + (xh ^ r)))
                for r in range(2)
                for nzh in range(2)
            ]
        )
        theirs = [jnp.where(core == 0, lefts[1, r], lefts[0, r]) for r in range(2)]
        mine = [jnp.where(core == 0, lefts[0, r], lefts[1, r]) for r in range(2)]
        theirs = dot(jnp.concatenate(theirs, axis=1), rsel).reshape(4, 160, 1280)
        mine = dot(jnp.concatenate(mine, axis=1), rsel).reshape(4, 160, 1280)
    with jax.named_scope("mixed_sum"):
        both = [None] * 4
        for q in (2, 1, 3, 0):
            both[q] = mine[q] + flip(theirs[q], core=1)
        upper = flip(both[2][:80], y=1)
        lower = flip(both[2][80:], y=3)

    with jax.named_scope("density_gather"):
        done = flip(dslots, z=1)
        dthree = flip(dslots, z=3)
        upper, lower, done, dthree = lax.optimization_barrier((upper, lower, done, dthree))
        dtwo = (flip(dthree[:160], z=1), flip(done[160:], z=3))

    with jax.named_scope("mixed_sum"):
        third = jnp.concatenate((both[3][:80] + upper, both[3][80:]))
        first = jnp.concatenate((both[1][:80], both[1][80:] + lower))
        sums = [flip(first, y=1), flip(third, y=3)]

    with jax.named_scope("density_rows"):
        dmine = local_call(
            rows_kernel, "density_rows", shape(bf16, 1280, 640), coords, dslots, done, *dtwo, dthree
        )

    with jax.named_scope("mixed_sum"):
        sums, dmine = lax.optimization_barrier((sums, dmine))
        total = both[0] + sums[0] + sums[1]
        mixed = total.astype(bf16)

    with jax.named_scope("mixed_gather"):
        one, three = flip(mixed, y=1), flip(mixed, y=3)
        dother = flip(dmine, core=1)
        two = (three[:80], one[80:])
        dfull = local_call(
            join_kernel, "density_join", shape(bf16, 1280, 1280), coords, dmine, dother
        )
        two, one, three, dfull = lax.optimization_barrier((two, one, three, dfull))
        two = (flip(two[0], y=1), flip(two[1], y=3))

    with jax.named_scope("second_product"):

        turns = [(r, t) for r in range(2) for t in range(2)]

        def pieces_of(count, *rows):
            resp = dot(jnp.concatenate(rows), dfull).reshape(count, 2, 2, 40, 1280)
            cut = []
            for r, t in turns:
                piece = lax.dynamic_index_in_dim(resp, core ^ t, 1, keepdims=False)
                piece = lax.dynamic_index_in_dim(piece, xh ^ r, 1, keepdims=False)
                cut.append(piece.astype(bf16))
            return cut

        def scatter(cut):
            return [
                remap(piece, lambda a, b, c, d, e: (a, b, c ^ d, d ^ t, e ^ r))
                for piece, (r, t) in zip(cut, turns)
            ]

        cut = list(pieces_of(3, mixed, one, three))
        many = scatter(cut)
        many[0], two = lax.optimization_barrier((many[0], two))
        last = scatter(pieces_of(1, *two))
        turned, *rows = local_call(
            spread_kernel,
            "spread",
            [shape(bf16, 32, 40, 160)] + [shape(f32, 40, 1280)] * 4,
            coords,
            *many,
            *last,
            scratch=[pltpu.VMEM((4, 40, 1280), f32)],
        )

    with jax.named_scope("transposed"):
        turned = lax.all_to_all(
            turned, ("z", "xl", "core", "xh"), split_axis=0, concat_axis=0, tiled=True
        )
    with jax.named_scope("direct"):
        direct = [rows[0]] + [flip(rows[q], y=q) for q in (1, 2, 3)]

    first_row = ((((z * 4 + y) * 2 + xl) * 2 + core) * 2 + xh) * 40
    block_rows = (first_row + jnp.arange(40, dtype=jnp.int32)) // BLK
    block_count = pattern.shape[0]
    onehot = (
        block_rows[:, None] == jnp.arange(block_count, dtype=jnp.int32)[None, :]
    ).astype(f32)
    kept_blocks = jnp.dot(onehot, pattern.astype(f32), preferred_element_type=f32)
    return local_call(
        finish_kernel,
        "finish",
        shape(f32, 40, 5120),
        coords,
        *direct,
        turned,
        kept_blocks,
        scratch=[pltpu.VMEM((4, 40, 1280), f32)],
    )


def solution(mesh):
    fine = Mesh(mesh.devices.reshape(SIZES), AXES)
    split = P(("z", "y", "xl"), ("core", "xh"))
    return jax.shard_map(
        shards,
        mesh=fine,
        in_specs=(split, split, split, split, P()),
        out_specs=P(AXES, None),
        check_vma=False,
    )
```

```python
import jax
import jax.numpy as jnp
from jax import lax
from jax.experimental import pallas as pl
from jax.experimental.pallas import tpu as pltpu
from jax.sharding import Mesh
from jax.sharding import PartitionSpec as P

BLK = 128
AXES = ("z", "y", "xl", "core", "xh")
SIZES = (4, 4, 2, 2, 2)
f32 = jnp.float32
bf16 = jnp.bfloat16


def flip(value, z=0, y=0, xl=0, core=0, xh=0):
    masks = (z, y, xl, core, xh)
    pairs = []
    for source in range(128):
        rest, digits = source, []
        for size in reversed(SIZES):
            digits.append(rest % size)
            rest //= size
        target = 0
        for digit, size, mask in zip(reversed(digits), SIZES, masks):
            target = target * size + (digit ^ mask)
        pairs.append((source, target))
    return lax.ppermute(value, AXES, pairs)


def remap(value, rule):
    pairs = []
    for source in range(128):
        rest, digits = source, []
        for size in reversed(SIZES):
            digits.append(rest % size)
            rest //= size
        target = 0
        for digit, size in zip(rule(*reversed(digits)), SIZES):
            target = target * size + digit
        pairs.append((source, target))
    return lax.ppermute(value, AXES, pairs)


def pick(stack, index):
    return lax.dynamic_index_in_dim(stack, index, 0, keepdims=False)


def dot(a, b):
    return jnp.dot(a, b, preferred_element_type=f32)


VMEM = pl.BlockSpec(memory_space=pltpu.VMEM)
SMEM = pl.BlockSpec(memory_space=pltpu.SMEM)


def local_call(kernel, name, outs, coords, *operands, scratch=()):
    return pl.pallas_call(
        kernel,
        out_shape=outs,
        in_specs=[SMEM] + [VMEM] * len(operands),
        out_specs=jax.tree.map(lambda _: VMEM, outs),
        scratch_shapes=list(scratch),
        name=name,
    )(coords, *operands)


def shape(dtype, *dims):
    return jax.ShapeDtypeStruct(dims, dtype)


def left_kernel(at_ref, first_ref, second_ref, came_ref, *outs):
    y, core = at_ref[1], at_ref[3]
    low = jnp.where(core == 0, first_ref[...], came_ref[...])
    high = jnp.where(core == 0, came_ref[...], second_ref[...])
    for ny in range(4):
        cut = slice(ny * 320, ny * 320 + 320)
        piece = jnp.concatenate((low[:, cut], high[:, cut]), axis=1)
        for q in range(4):

            @pl.when((y ^ q) == ny)
            def _():
                outs[q][...] = piece


def right_kernel(at_ref, first_ref, second_ref, out_ref):
    for m, ref in enumerate((first_ref, second_ref)):
        whole = ref[...]
        for xl in range(2):
            for xh in range(2):
                out_ref[xl * 4 + m * 2 + xh] = jnp.concatenate(
                    [
                        whole[:, start : start + 40]
                        for ny in range(4)
                        for start in (
                            ny * 320 + xl * 160 + xh * 40,
                            ny * 320 + xl * 160 + 80 + xh * 40,
                        )
                    ],
                    axis=1,
                )


def density_kernel(at_ref, same_ref, other_ref, out_ref):
    xh = at_ref[4]
    first = jnp.where(xh == 0, same_ref[...], other_ref[...])
    second = jnp.where(xh == 0, other_ref[...], same_ref[...])
    for ny in range(4):
        cut = slice(ny * 320, ny * 320 + 320)
        out_ref[ny] = jnp.concatenate((first[:, cut], second[:, cut]), axis=1)


def rows_kernel(at_ref, own_ref, one_ref, upper_ref, lower_ref, three_ref, out_ref):
    z = at_ref[0]

    def place(q, start, count, ref):
        first = pl.multiple_of((z ^ q) * 320 + start, 160)
        out_ref[pl.ds(first, count), :] = ref[...]

    place(0, 0, 320, own_ref)
    place(1, 0, 320, one_ref)
    place(2, 0, 160, upper_ref)
    place(2, 160, 160, lower_ref)
    place(3, 0, 320, three_ref)


def second_kernel(at_ref, mine_ref, other_ref, *refs):
    rows, outs, stack, whole = refs[:-6], refs[-6:-2], refs[-2], refs[-1]
    core, xh = at_ref[3], at_ref[4]
    first = 0
    for ref in rows:
        stack[first : first + ref.shape[0]] = ref[...]
        first += ref.shape[0]
    for side, right in enumerate((mine_ref, other_ref)):
        whole[side] = dot(stack[...], right[...]).reshape(first // 80, 2, 40, 640)
    for i, out in enumerate(outs):
        r, t = i // 2, i % 2
        for side in range(2):
            for slot in range(out.shape[1]):
                out[side, slot] = whole[side, slot * 2 + (core ^ t), xh ^ r].astype(bf16)


def spread_kernel(at_ref, *refs):
    many, last = refs[:4], refs[4:8]
    turned_ref, outs, slots = refs[8], refs[9:13], refs[13]
    y, core = at_ref[1], at_ref[3]
    for q in range(4):
        parts = last if q == 2 else many
        place = 0 if q == 2 else (0, 1, None, 2)[q]

        def total(side):
            terms = [parts[i][side ^ (i % 2), place].astype(f32) for i in range(4)]
            return (terms[0] + terms[1]) + (terms[2] + terms[3])

        mine, other = total(0), total(1)
        low = jnp.where(core == 0, mine, other)
        high = jnp.where(core == 0, other, mine)
        outs[q][:, :640] = low.astype(outs[q].dtype)
        outs[q][:, 640:] = high.astype(outs[q].dtype)
        slots[y ^ q, :, :640] = low
        slots[y ^ q, :, 640:] = high
    for nz in range(4):
        part = jnp.concatenate(
            [slots[ny, :, nz * 320 : nz * 320 + 320] for ny in range(4)], axis=0
        )
        part = part.T
        for j in range(8):
            turned_ref[nz * 8 + j] = part[j * 40 : j * 40 + 40].astype(bf16)


def finish_kernel(at_ref, d0, d1, d2, d3, t_ref, kept_ref, out_ref, slots):
    for q, ref in enumerate((d0, d1, d2, d3)):
        slots[q] = ref[...].astype(f32)
    y = at_ref[1]
    for nz in range(4):
        blocks = []
        for ny in range(4):
            other = jnp.concatenate(
                [
                    t_ref[nz * 8 + s, :, ny * 40 : (ny + 1) * 40].astype(f32)
                    for s in range(8)
                ],
                axis=1,
            )
            blocks.append(slots[y ^ ny, :, nz * 320 : (nz + 1) * 320] + other)
        block = 0.5 * jnp.concatenate(blocks, axis=1)
        kept = jnp.concatenate(
            [
                jnp.broadcast_to(kept_ref[:, j : j + 1], (40, BLK))
                for j in range(nz * 10, nz * 10 + 10)
            ],
            axis=1,
        )
        out_ref[:, nz * 1280 : (nz + 1) * 1280] = block * kept


def shards(dens_resp, density, fock, fock_resp, pattern):
    z, y, xl, core, xh = (lax.axis_index(name) for name in AXES)
    coords = jnp.stack((z, y, xl, core, xh)).astype(jnp.int32)

    with jax.named_scope("left_columns"):
        send = jnp.where(core == 0, density, dens_resp)
        came = flip(send, core=1)
    with jax.named_scope("right_columns"):
        first, second, _ = lax.optimization_barrier((fock, fock_resp, send))
        parts = local_call(
            right_kernel, "right_columns", shape(bf16, 8, 160, 320), coords, first, second
        )
    with jax.named_scope("density_turn"):
        halves, _ = lax.optimization_barrier((density.reshape(2, 2, 40, 1280), send))
        same = lax.dynamic_index_in_dim(halves, xh, 1, keepdims=False).reshape(80, 1280)
        other = lax.dynamic_index_in_dim(halves, 1 - xh, 1, keepdims=False).reshape(80, 1280)
        other = flip(other, xh=1)
    with jax.named_scope("left_columns"):
        pieces = local_call(
            left_kernel, "left_columns", [shape(bf16, 160, 640)] * 4, coords, dens_resp, density, came
        )
        parts, pieces = lax.optimization_barrier((parts, pieces))
        left = jnp.concatenate([pieces[0]] + [flip(pieces[q], y=q) for q in (1, 2, 3)])
        left, other = lax.optimization_barrier((left, other))
    with jax.named_scope("right_gather"):
        rounds = lax.all_to_all(
            parts, ("xl", "core", "xh"), split_axis=0, concat_axis=0, tiled=True
        )
        right = rounds.reshape(2, 4, 160, 320).transpose(0, 2, 1, 3).reshape(320, 1280)
        right, left = lax.optimization_barrier((right, left))
        rights = [right] + [flip(right, z=q) for q in (1, 2, 3)]
    with jax.named_scope("left_gather"):
        lefts = {
            (0, 0): left,
            (1, 0): flip(left, xl=1),
            (0, 1): flip(left, xh=1),
            (1, 1): flip(left, xl=1, xh=1),
        }

    with jax.named_scope("density_columns"):
        same, other, lefts[1, 0] = lax.optimization_barrier((same, other, lefts[1, 0]))
        cols = local_call(
            density_kernel, "density_columns", shape(bf16, 4, 80, 640), coords, same, other
        )
        dslots = lax.all_to_all(cols, "y", split_axis=0, concat_axis=0, tiled=True)
        dslots = dslots.reshape(320, 640)

    with jax.named_scope("first_product"):
        rights, dslots = lax.optimization_barrier((rights, dslots))
        rights = jnp.stack(rights)
        rsel = jnp.concatenate(
            [
                pick(rights, z ^ (nzh * 2 + (xh ^ r)))
                for r in range(2)
                for nzh in range(2)
            ]
        )
        theirs = [jnp.where(core == 0, lefts[1, r], lefts[0, r]) for r in range(2)]
        mine = [jnp.where(core == 0, lefts[0, r], lefts[1, r]) for r in range(2)]
        theirs = dot(jnp.concatenate(theirs, axis=1), rsel).reshape(4, 160, 1280)
        mine = dot(jnp.concatenate(mine, axis=1), rsel).reshape(4, 160, 1280)
    with jax.named_scope("mixed_sum"):
        both = [None] * 4
        for q in (2, 1, 3, 0):
            both[q] = mine[q] + flip(theirs[q], core=1)
        upper = flip(both[2][:80], y=1)
        lower = flip(both[2][80:], y=3)

    with jax.named_scope("density_gather"):
        done = flip(dslots, z=1)
        dthree = flip(dslots, z=3)
        upper, lower, done, dthree = lax.optimization_barrier((upper, lower, done, dthree))
        dtwo = (flip(dthree[:160], z=1), flip(done[160:], z=3))

    with jax.named_scope("mixed_sum"):
        third = jnp.concatenate((both[3][:80] + upper, both[3][80:]))
        first = jnp.concatenate((both[1][:80], both[1][80:] + lower))
        sums = [flip(first, y=1), flip(third, y=3)]

    with jax.named_scope("density_rows"):
        dmine = local_call(
            rows_kernel, "density_rows", shape(bf16, 1280, 640), coords, dslots, done, *dtwo, dthree
        )

    with jax.named_scope("mixed_sum"):
        sums, dmine = lax.optimization_barrier((sums, dmine))
        total = both[0] + sums[0] + sums[1]
        mixed = total.astype(bf16)

    with jax.named_scope("mixed_gather"):
        one, three = flip(mixed, y=1), flip(mixed, y=3)
        dother = flip(dmine, core=1)
        two = (three[:80], one[80:])
        two, one, three = lax.optimization_barrier((two, one, three))
        two = (flip(two[0], y=1), flip(two[1], y=3))

    with jax.named_scope("second_product"):

        def pieces_of(count, *rows):
            return local_call(
                second_kernel,
                "second_product",
                [shape(bf16, 2, count, 40, 640)] * 4,
                coords,
                dmine,
                dother,
                *rows,
                scratch=[
                    pltpu.VMEM((count * 160, 1280), bf16),
                    pltpu.VMEM((2, count * 2, 2, 40, 640), f32),
                ],
            )

        def scatter(cut):
            turns = [(r, t) for r in range(2) for t in range(2)]
            return [
                remap(piece, lambda a, b, c, d, e: (a, b, c ^ d, d ^ t, e ^ r))
                for piece, (r, t) in zip(cut, turns)
            ]

        cut = list(pieces_of(3, mixed, one, three))
        cut[3], two = lax.optimization_barrier((cut[3], two))
        many = scatter(cut)
        many[0], two = lax.optimization_barrier((many[0], two))
        last = scatter(pieces_of(1, *two))
        turned, *rows = local_call(
            spread_kernel,
            "spread",
            [shape(bf16, 32, 40, 160), shape(f32, 40, 1280)] + [shape(bf16, 40, 1280)] * 3,
            coords,
            *many,
            *last,
            scratch=[pltpu.VMEM((4, 40, 1280), f32)],
        )

    with jax.named_scope("transposed"):
        turned = lax.all_to_all(
            turned, ("z", "xl", "core", "xh"), split_axis=0, concat_axis=0, tiled=True
        )
    with jax.named_scope("direct"):
        direct = [rows[0]] + [flip(rows[q], y=q) for q in (1, 2, 3)]

    first_row = ((((z * 4 + y) * 2 + xl) * 2 + core) * 2 + xh) * 40
    block_rows = (first_row + jnp.arange(40, dtype=jnp.int32)) // BLK
    block_count = pattern.shape[0]
    onehot = (
        block_rows[:, None] == jnp.arange(block_count, dtype=jnp.int32)[None, :]
    ).astype(f32)
    kept_blocks = jnp.dot(onehot, pattern.astype(f32), preferred_element_type=f32)
    return local_call(
        finish_kernel,
        "finish",
        shape(f32, 40, 5120),
        coords,
        *direct,
        turned,
        kept_blocks,
        scratch=[pltpu.VMEM((4, 40, 1280), f32)],
    )


def solution(mesh):
    fine = Mesh(mesh.devices.reshape(SIZES), AXES)
    split = P(("z", "y", "xl"), ("core", "xh"))
    return jax.shard_map(
        shards,
        mesh=fine,
        in_specs=(split, split, split, split, P()),
        out_specs=P(AXES, None),
        check_vma=False,
    )
```

```python
import jax
import jax.numpy as jnp
from jax import lax
from jax.experimental import pallas as pl
from jax.experimental.pallas import tpu as pltpu
from jax.sharding import Mesh
from jax.sharding import PartitionSpec as P

BLK = 128
AXES = ("z", "y", "xl", "core", "xh")
SIZES = (4, 4, 2, 2, 2)
f32 = jnp.float32
bf16 = jnp.bfloat16


def flip(value, z=0, y=0, xl=0, core=0, xh=0):
    masks = (z, y, xl, core, xh)
    pairs = []
    for source in range(128):
        rest, digits = source, []
        for size in reversed(SIZES):
            digits.append(rest % size)
            rest //= size
        target = 0
        for digit, size, mask in zip(reversed(digits), SIZES, masks):
            target = target * size + (digit ^ mask)
        pairs.append((source, target))
    return lax.ppermute(value, AXES, pairs)


def remap(value, rule):
    pairs = []
    for source in range(128):
        rest, digits = source, []
        for size in reversed(SIZES):
            digits.append(rest % size)
            rest //= size
        target = 0
        for digit, size in zip(rule(*reversed(digits)), SIZES):
            target = target * size + digit
        pairs.append((source, target))
    return lax.ppermute(value, AXES, pairs)


def pick(stack, index):
    return lax.dynamic_index_in_dim(stack, index, 0, keepdims=False)


def dot(a, b):
    return jnp.dot(a, b, preferred_element_type=f32)


VMEM = pl.BlockSpec(memory_space=pltpu.VMEM)
SMEM = pl.BlockSpec(memory_space=pltpu.SMEM)


def local_call(kernel, name, outs, coords, *operands, scratch=()):
    return pl.pallas_call(
        kernel,
        out_shape=outs,
        in_specs=[SMEM] + [VMEM] * len(operands),
        out_specs=jax.tree.map(lambda _: VMEM, outs),
        scratch_shapes=list(scratch),
        name=name,
    )(coords, *operands)


def shape(dtype, *dims):
    return jax.ShapeDtypeStruct(dims, dtype)


def left_kernel(at_ref, first_ref, second_ref, came_ref, *outs):
    y, core = at_ref[1], at_ref[3]
    low = jnp.where(core == 0, first_ref[...], came_ref[...])
    high = jnp.where(core == 0, came_ref[...], second_ref[...])
    for ny in range(4):
        cut = slice(ny * 320, ny * 320 + 320)
        piece = jnp.concatenate((low[:, cut], high[:, cut]), axis=1)
        for q in range(4):

            @pl.when((y ^ q) == ny)
            def _():
                outs[q][...] = piece


def right_kernel(at_ref, first_ref, second_ref, out_ref):
    for m, ref in enumerate((first_ref, second_ref)):
        whole = ref[...]
        for xl in range(2):
            for xh in range(2):
                out_ref[xl * 4 + m * 2 + xh] = jnp.concatenate(
                    [
                        whole[:, start : start + 40]
                        for ny in range(4)
                        for start in (
                            ny * 320 + xl * 160 + xh * 40,
                            ny * 320 + xl * 160 + 80 + xh * 40,
                        )
                    ],
                    axis=1,
                )


def density_kernel(at_ref, same_ref, other_ref, out_ref):
    xh = at_ref[4]
    first = jnp.where(xh == 0, same_ref[...], other_ref[...])
    second = jnp.where(xh == 0, other_ref[...], same_ref[...])
    for ny in range(4):
        cut = slice(ny * 320, ny * 320 + 320)
        out_ref[ny] = jnp.concatenate((first[:, cut], second[:, cut]), axis=1)


def rows_kernel(at_ref, own_ref, one_ref, upper_ref, lower_ref, three_ref, out_ref):
    z = at_ref[0]

    def place(q, start, count, ref):
        first = pl.multiple_of((z ^ q) * 320 + start, 160)
        out_ref[pl.ds(first, count), :] = ref[...]

    place(0, 0, 320, own_ref)
    place(1, 0, 320, one_ref)
    place(2, 0, 160, upper_ref)
    place(2, 160, 160, lower_ref)
    place(3, 0, 320, three_ref)


def second_kernel(at_ref, mine_ref, other_ref, *refs):
    rows, outs, stack, whole = refs[:-6], refs[-6:-2], refs[-2], refs[-1]
    core, xh = at_ref[3], at_ref[4]
    first = 0
    for ref in rows:
        stack[first : first + ref.shape[0]] = ref[...]
        first += ref.shape[0]
    for side, right in enumerate((mine_ref, other_ref)):
        whole[side] = dot(stack[...], right[...]).reshape(first // 80, 2, 40, 640)
    for i, out in enumerate(outs):
        r, t = i // 2, i % 2
        for side in range(2):
            for slot in range(out.shape[1]):
                out[side, slot] = whole[side, slot * 2 + (core ^ t), xh ^ r].astype(bf16)


def spread_kernel(at_ref, *refs):
    many, last = refs[:4], refs[4:8]
    turned_ref, outs, slots = refs[8], refs[9:13], refs[13]
    y, core = at_ref[1], at_ref[3]
    for q in range(4):
        parts = last if q == 2 else many
        place = 0 if q == 2 else (0, 1, None, 2)[q]

        def total(side):
            terms = [parts[i][side ^ (i % 2), place].astype(f32) for i in range(4)]
            return (terms[0] + terms[1]) + (terms[2] + terms[3])

        mine, other = total(0), total(1)
        low = jnp.where(core == 0, mine, other)
        high = jnp.where(core == 0, other, mine)
        outs[q][:, :640] = low.astype(outs[q].dtype)
        outs[q][:, 640:] = high.astype(outs[q].dtype)
        slots[y ^ q, :, :640] = low
        slots[y ^ q, :, 640:] = high
    for nz in range(4):
        part = jnp.concatenate(
            [slots[ny, :, nz * 320 : nz * 320 + 320] for ny in range(4)], axis=0
        )
        part = part.T
        for j in range(8):
            turned_ref[nz * 8 + j] = part[j * 40 : j * 40 + 40].astype(bf16)


def finish_kernel(at_ref, d0, d1, d2, d3, t_ref, kept_ref, out_ref, slots):
    for q, ref in enumerate((d0, d1, d2, d3)):
        slots[q] = ref[...].astype(f32)
    y = at_ref[1]
    for nz in range(4):
        blocks = []
        for ny in range(4):
            other = jnp.concatenate(
                [
                    t_ref[nz * 8 + s, :, ny * 40 : (ny + 1) * 40]
                    for s in range(8)
                ],
                axis=1,
            ).astype(f32)
            blocks.append(slots[y ^ ny, :, nz * 320 : (nz + 1) * 320] + other)
        block = 0.5 * jnp.concatenate(blocks, axis=1)
        kept = jnp.concatenate(
            [
                jnp.broadcast_to(kept_ref[:, j : j + 1], (40, BLK))
                for j in range(nz * 10, nz * 10 + 10)
            ],
            axis=1,
        )
        out_ref[:, nz * 1280 : (nz + 1) * 1280] = block * kept


def shards(dens_resp, density, fock, fock_resp, pattern):
    z, y, xl, core, xh = (lax.axis_index(name) for name in AXES)
    coords = jnp.stack((z, y, xl, core, xh)).astype(jnp.int32)

    with jax.named_scope("left_columns"):
        send = jnp.where(core == 0, density, dens_resp)
        came = flip(send, core=1)
    with jax.named_scope("right_columns"):
        first, second, _ = lax.optimization_barrier((fock, fock_resp, send))
        parts = local_call(
            right_kernel, "right_columns", shape(bf16, 8, 160, 320), coords, first, second
        )
    with jax.named_scope("density_turn"):
        halves, _ = lax.optimization_barrier((density.reshape(2, 2, 40, 1280), send))
        same = lax.dynamic_index_in_dim(halves, xh, 1, keepdims=False).reshape(80, 1280)
        other = lax.dynamic_index_in_dim(halves, 1 - xh, 1, keepdims=False).reshape(80, 1280)
        other = flip(other, xh=1)
    with jax.named_scope("left_columns"):
        pieces = local_call(
            left_kernel, "left_columns", [shape(bf16, 160, 640)] * 4, coords, dens_resp, density, came
        )
        parts, pieces = lax.optimization_barrier((parts, pieces))
        left = jnp.concatenate([pieces[0]] + [flip(pieces[q], y=q) for q in (1, 2, 3)])
        left, other = lax.optimization_barrier((left, other))
    with jax.named_scope("right_gather"):
        rounds = lax.all_to_all(
            parts, ("xl", "core", "xh"), split_axis=0, concat_axis=0, tiled=True
        )
        right = rounds.reshape(2, 4, 160, 320).transpose(0, 2, 1, 3).reshape(320, 1280)
        right, left = lax.optimization_barrier((right, left))
        rights = [right] + [flip(right, z=q) for q in (1, 2, 3)]
    with jax.named_scope("left_gather"):
        lefts = {
            (0, 0): left,
            (1, 0): flip(left, xl=1),
            (0, 1): flip(left, xh=1),
            (1, 1): flip(left, xl=1, xh=1),
        }

    with jax.named_scope("density_columns"):
        same, other, lefts[1, 0] = lax.optimization_barrier((same, other, lefts[1, 0]))
        cols = local_call(
            density_kernel, "density_columns", shape(bf16, 4, 80, 640), coords, same, other
        )
        dslots = lax.all_to_all(cols, "y", split_axis=0, concat_axis=0, tiled=True)
        dslots = dslots.reshape(320, 640)

    with jax.named_scope("first_product"):
        rights, dslots = lax.optimization_barrier((rights, dslots))
        rights = jnp.stack(rights)
        rsel = jnp.concatenate(
            [
                pick(rights, z ^ (nzh * 2 + (xh ^ r)))
                for r in range(2)
                for nzh in range(2)
            ]
        )
        theirs = [jnp.where(core == 0, lefts[1, r], lefts[0, r]) for r in range(2)]
        mine = [jnp.where(core == 0, lefts[0, r], lefts[1, r]) for r in range(2)]
        theirs = dot(jnp.concatenate(theirs, axis=1), rsel).reshape(4, 160, 1280)
        mine = dot(jnp.concatenate(mine, axis=1), rsel).reshape(4, 160, 1280)
    with jax.named_scope("mixed_sum"):
        both = [None] * 4
        for q in (2, 1, 3, 0):
            both[q] = mine[q] + flip(theirs[q], core=1)
        upper = flip(both[2][:80], y=1)
        lower = flip(both[2][80:], y=3)

    with jax.named_scope("density_gather"):
        done = flip(dslots, z=1)
        dthree = flip(dslots, z=3)
        upper, lower, done, dthree = lax.optimization_barrier((upper, lower, done, dthree))
        dtwo = (flip(dthree[:160], z=1), flip(done[160:], z=3))

    with jax.named_scope("mixed_sum"):
        third = jnp.concatenate((both[3][:80] + upper, both[3][80:]))
        first = jnp.concatenate((both[1][:80], both[1][80:] + lower))
        sums = [flip(first, y=1), flip(third, y=3)]

    with jax.named_scope("density_rows"):
        dmine = local_call(
            rows_kernel, "density_rows", shape(bf16, 1280, 640), coords, dslots, done, *dtwo, dthree
        )

    with jax.named_scope("mixed_sum"):
        sums, dmine = lax.optimization_barrier((sums, dmine))
        total = both[0] + sums[0] + sums[1]
        mixed = total.astype(bf16)

    with jax.named_scope("mixed_gather"):
        one, three = flip(mixed, y=1), flip(mixed, y=3)
        dother = flip(dmine, core=1)
        two = (three[:80], one[80:])
        two, one, three = lax.optimization_barrier((two, one, three))
        two = (flip(two[0], y=1), flip(two[1], y=3))

    with jax.named_scope("second_product"):

        def pieces_of(count, *rows):
            return local_call(
                second_kernel,
                "second_product",
                [shape(bf16, 2, count, 40, 640)] * 4,
                coords,
                dmine,
                dother,
                *rows,
                scratch=[
                    pltpu.VMEM((count * 160, 1280), bf16),
                    pltpu.VMEM((2, count * 2, 2, 40, 640), f32),
                ],
            )

        def scatter(cut):
            turns = [(r, t) for r in range(2) for t in range(2)]
            return [
                remap(piece, lambda a, b, c, d, e: (a, b, c ^ d, d ^ t, e ^ r))
                for piece, (r, t) in zip(cut, turns)
            ]

        cut = list(pieces_of(3, mixed, one, three))
        cut[3], two = lax.optimization_barrier((cut[3], two))
        many = scatter(cut)
        many[0], two = lax.optimization_barrier((many[0], two))
        last = scatter(pieces_of(1, *two))
        turned, *rows = local_call(
            spread_kernel,
            "spread",
            [shape(bf16, 32, 40, 160), shape(f32, 40, 1280)] + [shape(bf16, 40, 1280)] * 3,
            coords,
            *many,
            *last,
            scratch=[pltpu.VMEM((4, 40, 1280), f32)],
        )

    with jax.named_scope("transposed"):
        turned = lax.all_to_all(
            turned, ("z", "xl", "core", "xh"), split_axis=0, concat_axis=0, tiled=True
        )
    with jax.named_scope("direct"):
        direct = [rows[0]] + [flip(rows[q], y=q) for q in (1, 2, 3)]

    first_row = ((((z * 4 + y) * 2 + xl) * 2 + core) * 2 + xh) * 40
    block_rows = (first_row + jnp.arange(40, dtype=jnp.int32)) // BLK
    block_count = pattern.shape[0]
    onehot = (
        block_rows[:, None] == jnp.arange(block_count, dtype=jnp.int32)[None, :]
    ).astype(f32)
    kept_blocks = jnp.dot(onehot, pattern.astype(f32), preferred_element_type=f32)
    return local_call(
        finish_kernel,
        "finish",
        shape(f32, 40, 5120),
        coords,
        *direct,
        turned,
        kept_blocks,
        scratch=[pltpu.VMEM((4, 40, 1280), f32)],
    )


def solution(mesh):
    fine = Mesh(mesh.devices.reshape(SIZES), AXES)
    split = P(("z", "y", "xl"), ("core", "xh"))
    return jax.shard_map(
        shards,
        mesh=fine,
        in_specs=(split, split, split, split, P()),
        out_specs=P(AXES, None),
        check_vma=False,
    )
```

```python
import jax
import jax.numpy as jnp
from jax import lax
from jax.experimental import pallas as pl
from jax.experimental.pallas import tpu as pltpu
from jax.sharding import Mesh
from jax.sharding import PartitionSpec as P

BLK = 128
AXES = ("z", "y", "xl", "core", "xh")
SIZES = (4, 4, 2, 2, 2)
f32 = jnp.float32
bf16 = jnp.bfloat16


def flip(value, z=0, y=0, xl=0, core=0, xh=0):
    masks = (z, y, xl, core, xh)
    pairs = []
    for source in range(128):
        rest, digits = source, []
        for size in reversed(SIZES):
            digits.append(rest % size)
            rest //= size
        target = 0
        for digit, size, mask in zip(reversed(digits), SIZES, masks):
            target = target * size + (digit ^ mask)
        pairs.append((source, target))
    return lax.ppermute(value, AXES, pairs)


def remap(value, rule):
    pairs = []
    for source in range(128):
        rest, digits = source, []
        for size in reversed(SIZES):
            digits.append(rest % size)
            rest //= size
        target = 0
        for digit, size in zip(rule(*reversed(digits)), SIZES):
            target = target * size + digit
        pairs.append((source, target))
    return lax.ppermute(value, AXES, pairs)


def pick(stack, index):
    return lax.dynamic_index_in_dim(stack, index, 0, keepdims=False)


def dot(a, b):
    return jnp.dot(a, b, preferred_element_type=f32)


VMEM = pl.BlockSpec(memory_space=pltpu.VMEM)


def local_call(kernel, name, outs, *operands, scratch=()):
    def body(*refs):
        kernel([lax.axis_index(axis) for axis in AXES], *refs)

    return pl.pallas_call(
        body,
        out_shape=outs,
        in_specs=[VMEM] * len(operands),
        out_specs=jax.tree.map(lambda _: VMEM, outs),
        scratch_shapes=list(scratch),
        name=name,
    )(*operands)


def shape(dtype, *dims):
    return jax.ShapeDtypeStruct(dims, dtype)


def left_kernel(at, first_ref, second_ref, came_ref, *outs):
    y, core = at[1], at[3]
    low = jnp.where(core == 0, first_ref[...], came_ref[...])
    high = jnp.where(core == 0, came_ref[...], second_ref[...])
    for ny in range(4):
        cut = slice(ny * 320, ny * 320 + 320)
        piece = jnp.concatenate((low[:, cut], high[:, cut]), axis=1)
        for q in range(4):

            @pl.when((y ^ q) == ny)
            def _():
                outs[q][...] = piece


def right_kernel(at, first_ref, second_ref, out_ref):
    for m, ref in enumerate((first_ref, second_ref)):
        whole = ref[...]
        for xl in range(2):
            for xh in range(2):
                out_ref[xl * 4 + m * 2 + xh] = jnp.concatenate(
                    [
                        whole[:, start : start + 40]
                        for ny in range(4)
                        for start in (
                            ny * 320 + xl * 160 + xh * 40,
                            ny * 320 + xl * 160 + 80 + xh * 40,
                        )
                    ],
                    axis=1,
                )


def density_kernel(at, same_ref, other_ref, out_ref):
    xh = at[4]
    first = jnp.where(xh == 0, same_ref[...], other_ref[...])
    second = jnp.where(xh == 0, other_ref[...], same_ref[...])
    for ny in range(4):
        cut = slice(ny * 320, ny * 320 + 320)
        out_ref[ny] = jnp.concatenate((first[:, cut], second[:, cut]), axis=1)


def rows_kernel(at, own_ref, one_ref, upper_ref, lower_ref, three_ref, out_ref):
    z = at[0]

    def place(q, start, count, ref):
        first = pl.multiple_of((z ^ q) * 320 + start, 160)
        out_ref[pl.ds(first, count), :] = ref[...]

    place(0, 0, 320, own_ref)
    place(1, 0, 320, one_ref)
    place(2, 0, 160, upper_ref)
    place(2, 160, 160, lower_ref)
    place(3, 0, 320, three_ref)


def second_kernel(at, mine_ref, other_ref, *refs):
    rows, outs, stack, whole = refs[:-6], refs[-6:-2], refs[-2], refs[-1]
    core, xh = at[3], at[4]
    first = 0
    for ref in rows:
        stack[first : first + ref.shape[0]] = ref[...]
        first += ref.shape[0]
    for side, right in enumerate((mine_ref, other_ref)):
        whole[side] = dot(stack[...], right[...]).reshape(first // 80, 2, 40, 640)
    for i, out in enumerate(outs):
        r, t = i // 2, i % 2
        for side in range(2):
            for slot in range(out.shape[1]):
                out[side, slot] = whole[side, slot * 2 + (core ^ t), xh ^ r].astype(bf16)


def spread_kernel(at, *refs):
    many, last = refs[:4], refs[4:8]
    turned_ref, outs, slots = refs[8], refs[9:13], refs[13]
    y, core = at[1], at[3]
    for q in range(4):
        parts = last if q == 2 else many
        place = 0 if q == 2 else (0, 1, None, 2)[q]

        def total(side):
            terms = [parts[i][side ^ (i % 2), place].astype(f32) for i in range(4)]
            return (terms[0] + terms[1]) + (terms[2] + terms[3])

        mine, other = total(0), total(1)
        low = jnp.where(core == 0, mine, other)
        high = jnp.where(core == 0, other, mine)
        outs[q][:, :640] = low.astype(outs[q].dtype)
        outs[q][:, 640:] = high.astype(outs[q].dtype)
        slots[y ^ q, :, :640] = low
        slots[y ^ q, :, 640:] = high
    for nz in range(4):
        part = jnp.concatenate(
            [slots[ny, :, nz * 320 : nz * 320 + 320] for ny in range(4)], axis=0
        )
        part = part.T
        for j in range(8):
            turned_ref[nz * 8 + j] = part[j * 40 : j * 40 + 40].astype(bf16)


def finish_kernel(at, d0, d1, d2, d3, t_ref, kept_ref, out_ref, slots):
    for q, ref in enumerate((d0, d1, d2, d3)):
        slots[q] = ref[...].astype(f32)
    y = at[1]
    for nz in range(4):
        blocks = []
        for ny in range(4):
            other = jnp.concatenate(
                [
                    t_ref[nz * 8 + s, :, ny * 40 : (ny + 1) * 40]
                    for s in range(8)
                ],
                axis=1,
            ).astype(f32)
            blocks.append(slots[y ^ ny, :, nz * 320 : (nz + 1) * 320] + other)
        block = 0.5 * jnp.concatenate(blocks, axis=1)
        kept = jnp.concatenate(
            [
                jnp.broadcast_to(kept_ref[:, j : j + 1], (40, BLK))
                for j in range(nz * 10, nz * 10 + 10)
            ],
            axis=1,
        )
        out_ref[:, nz * 1280 : (nz + 1) * 1280] = block * kept


def shards(dens_resp, density, fock, fock_resp, pattern):
    z, y, xl, core, xh = (lax.axis_index(name) for name in AXES)

    with jax.named_scope("left_columns"):
        send = jnp.where(core == 0, density, dens_resp)
        came = flip(send, core=1)
    with jax.named_scope("right_columns"):
        first, second, _ = lax.optimization_barrier((fock, fock_resp, send))
        parts = local_call(
            right_kernel, "right_columns", shape(bf16, 8, 160, 320), first, second
        )
    with jax.named_scope("density_turn"):
        halves, _ = lax.optimization_barrier((density.reshape(2, 2, 40, 1280), send))
        same = lax.dynamic_index_in_dim(halves, xh, 1, keepdims=False).reshape(80, 1280)
        other = lax.dynamic_index_in_dim(halves, 1 - xh, 1, keepdims=False).reshape(80, 1280)
        other = flip(other, xh=1)
    with jax.named_scope("left_columns"):
        pieces = local_call(
            left_kernel, "left_columns", [shape(bf16, 160, 640)] * 4, dens_resp, density, came
        )
        parts, pieces = lax.optimization_barrier((parts, pieces))
        left = jnp.concatenate([pieces[0]] + [flip(pieces[q], y=q) for q in (1, 2, 3)])
        left, other = lax.optimization_barrier((left, other))
    with jax.named_scope("right_gather"):
        rounds = lax.all_to_all(
            parts, ("xl", "core", "xh"), split_axis=0, concat_axis=0, tiled=True
        )
        right = rounds.reshape(2, 4, 160, 320).transpose(0, 2, 1, 3).reshape(320, 1280)
        right, left = lax.optimization_barrier((right, left))
        rights = [right] + [flip(right, z=q) for q in (1, 2, 3)]
    with jax.named_scope("left_gather"):
        lefts = {
            (0, 0): left,
            (1, 0): flip(left, xl=1),
            (0, 1): flip(left, xh=1),
            (1, 1): flip(left, xl=1, xh=1),
        }

    with jax.named_scope("density_columns"):
        same, other, lefts[1, 0] = lax.optimization_barrier((same, other, lefts[1, 0]))
        cols = local_call(
            density_kernel, "density_columns", shape(bf16, 4, 80, 640), same, other
        )
        dslots = lax.all_to_all(cols, "y", split_axis=0, concat_axis=0, tiled=True)
        dslots = dslots.reshape(320, 640)

    with jax.named_scope("first_product"):
        rights, dslots = lax.optimization_barrier((rights, dslots))
        rights = jnp.stack(rights)
        rsel = jnp.concatenate(
            [
                pick(rights, z ^ (nzh * 2 + (xh ^ r)))
                for r in range(2)
                for nzh in range(2)
            ]
        )
        theirs = [jnp.where(core == 0, lefts[1, r], lefts[0, r]) for r in range(2)]
        mine = [jnp.where(core == 0, lefts[0, r], lefts[1, r]) for r in range(2)]
        theirs = dot(jnp.concatenate(theirs, axis=1), rsel).reshape(4, 160, 1280)
        mine = dot(jnp.concatenate(mine, axis=1), rsel).reshape(4, 160, 1280)
    with jax.named_scope("mixed_sum"):
        both = [None] * 4
        for q in (2, 1, 3, 0):
            both[q] = mine[q] + flip(theirs[q], core=1)
        upper = flip(both[2][:80], y=1)
        lower = flip(both[2][80:], y=3)

    with jax.named_scope("density_gather"):
        done = flip(dslots, z=1)
        dthree = flip(dslots, z=3)
        upper, lower, done, dthree = lax.optimization_barrier((upper, lower, done, dthree))
        dtwo = (flip(dthree[:160], z=1), flip(done[160:], z=3))

    with jax.named_scope("mixed_sum"):
        third = jnp.concatenate((both[3][:80] + upper, both[3][80:]))
        first = jnp.concatenate((both[1][:80], both[1][80:] + lower))
        sums = [flip(first, y=1), flip(third, y=3)]

    with jax.named_scope("density_rows"):
        dmine = local_call(
            rows_kernel, "density_rows", shape(bf16, 1280, 640), dslots, done, *dtwo, dthree
        )

    with jax.named_scope("mixed_sum"):
        sums, dmine = lax.optimization_barrier((sums, dmine))
        total = both[0] + sums[0] + sums[1]
        mixed = total.astype(bf16)

    with jax.named_scope("mixed_gather"):
        one, three = flip(mixed, y=1), flip(mixed, y=3)
        dother = flip(dmine, core=1)
        two = (three[:80], one[80:])
        two, one, three = lax.optimization_barrier((two, one, three))
        two = (flip(two[0], y=1), flip(two[1], y=3))

    with jax.named_scope("second_product"):

        def pieces_of(count, *rows):
            return local_call(
                second_kernel,
                "second_product",
                [shape(bf16, 2, count, 40, 640)] * 4,
                dmine,
                dother,
                *rows,
                scratch=[
                    pltpu.VMEM((count * 160, 1280), bf16),
                    pltpu.VMEM((2, count * 2, 2, 40, 640), f32),
                ],
            )

        def scatter(cut):
            turns = [(r, t) for r in range(2) for t in range(2)]
            return [
                remap(piece, lambda a, b, c, d, e: (a, b, c ^ d, d ^ t, e ^ r))
                for piece, (r, t) in zip(cut, turns)
            ]

        cut = list(pieces_of(3, mixed, one, three))
        cut[3], two = lax.optimization_barrier((cut[3], two))
        many = scatter(cut)
        many[0], two = lax.optimization_barrier((many[0], two))
        last = scatter(pieces_of(1, *two))
        turned, *rows = local_call(
            spread_kernel,
            "spread",
            [shape(bf16, 32, 40, 160), shape(f32, 40, 1280)] + [shape(bf16, 40, 1280)] * 3,
            *many,
            *last,
            scratch=[pltpu.VMEM((4, 40, 1280), f32)],
        )

    with jax.named_scope("transposed"):
        turned = lax.all_to_all(
            turned, ("z", "xl", "core", "xh"), split_axis=0, concat_axis=0, tiled=True
        )
    with jax.named_scope("direct"):
        direct = [rows[0]] + [flip(rows[q], y=q) for q in (1, 2, 3)]

    first_row = ((((z * 4 + y) * 2 + xl) * 2 + core) * 2 + xh) * 40
    block_rows = (first_row + jnp.arange(40, dtype=jnp.int32)) // BLK
    block_count = pattern.shape[0]
    onehot = (
        block_rows[:, None] == jnp.arange(block_count, dtype=jnp.int32)[None, :]
    ).astype(f32)
    kept_blocks = jnp.dot(onehot, pattern.astype(f32), preferred_element_type=f32)
    return local_call(
        finish_kernel,
        "finish",
        shape(f32, 40, 5120),
        *direct,
        turned,
        kept_blocks,
        scratch=[pltpu.VMEM((4, 40, 1280), f32)],
    )


def solution(mesh):
    fine = Mesh(mesh.devices.reshape(SIZES), AXES)
    split = P(("z", "y", "xl"), ("core", "xh"))
    return jax.shard_map(
        shards,
        mesh=fine,
        in_specs=(split, split, split, split, P()),
        out_specs=P(AXES, None),
        check_vma=False,
    )
```

```python
import jax
import jax.numpy as jnp
from jax import lax
from jax.experimental import pallas as pl
from jax.experimental.pallas import tpu as pltpu
from jax.sharding import Mesh
from jax.sharding import PartitionSpec as P

BLK = 128
AXES = ("z", "y", "xl", "core", "xh")
SIZES = (4, 4, 2, 2, 2)
f32 = jnp.float32
bf16 = jnp.bfloat16


def flip(value, z=0, y=0, xl=0, core=0, xh=0):
    masks = (z, y, xl, core, xh)
    pairs = []
    for source in range(128):
        rest, digits = source, []
        for size in reversed(SIZES):
            digits.append(rest % size)
            rest //= size
        target = 0
        for digit, size, mask in zip(reversed(digits), SIZES, masks):
            target = target * size + (digit ^ mask)
        pairs.append((source, target))
    return lax.ppermute(value, AXES, pairs)


def remap(value, rule):
    pairs = []
    for source in range(128):
        rest, digits = source, []
        for size in reversed(SIZES):
            digits.append(rest % size)
            rest //= size
        target = 0
        for digit, size in zip(rule(*reversed(digits)), SIZES):
            target = target * size + digit
        pairs.append((source, target))
    return lax.ppermute(value, AXES, pairs)


def pick(stack, index):
    return lax.dynamic_index_in_dim(stack, index, 0, keepdims=False)


def dot(a, b):
    return jnp.dot(a, b, preferred_element_type=f32)


VMEM = pl.BlockSpec(memory_space=pltpu.VMEM)
SMEM = pl.BlockSpec(memory_space=pltpu.SMEM)


def local_call(kernel, name, outs, coords, *operands, scratch=()):
    return pl.pallas_call(
        kernel,
        out_shape=outs,
        in_specs=[SMEM] + [VMEM] * len(operands),
        out_specs=jax.tree.map(lambda _: VMEM, outs),
        scratch_shapes=list(scratch),
        name=name,
    )(coords, *operands)


def shape(dtype, *dims):
    return jax.ShapeDtypeStruct(dims, dtype)


def left_kernel(at_ref, first_ref, second_ref, came_ref, *outs):
    y, core = at_ref[1], at_ref[3]
    low = jnp.where(core == 0, first_ref[...], came_ref[...])
    high = jnp.where(core == 0, came_ref[...], second_ref[...])
    for ny in range(4):
        cut = slice(ny * 320, ny * 320 + 320)
        piece = jnp.concatenate((low[:, cut], high[:, cut]), axis=1)
        for q in range(4):

            @pl.when((y ^ q) == ny)
            def _():
                outs[q][...] = piece


def right_kernel(at_ref, first_ref, second_ref, out_ref):
    for m, ref in enumerate((first_ref, second_ref)):
        whole = ref[...]
        for xl in range(2):
            for xh in range(2):
                out_ref[xl * 4 + m * 2 + xh] = jnp.concatenate(
                    [
                        whole[:, start : start + 40]
                        for ny in range(4)
                        for start in (
                            ny * 320 + xl * 160 + xh * 40,
                            ny * 320 + xl * 160 + 80 + xh * 40,
                        )
                    ],
                    axis=1,
                )


def density_kernel(at_ref, same_ref, other_ref, out_ref):
    xh = at_ref[4]
    first = jnp.where(xh == 0, same_ref[...], other_ref[...])
    second = jnp.where(xh == 0, other_ref[...], same_ref[...])
    for ny in range(4):
        cut = slice(ny * 320, ny * 320 + 320)
        out_ref[ny] = jnp.concatenate((first[:, cut], second[:, cut]), axis=1)


def rows_kernel(at_ref, own_ref, one_ref, upper_ref, lower_ref, three_ref, out_ref):
    z = at_ref[0]

    def place(q, start, count, ref):
        first = pl.multiple_of((z ^ q) * 320 + start, 160)
        out_ref[pl.ds(first, count), :] = ref[...]

    place(0, 0, 320, own_ref)
    place(1, 0, 320, one_ref)
    place(2, 0, 160, upper_ref)
    place(2, 160, 160, lower_ref)
    place(3, 0, 320, three_ref)


def second_kernel(at_ref, mine_ref, other_ref, *refs):
    rows, outs, stack, whole = refs[:-6], refs[-6:-2], refs[-2], refs[-1]
    core, xh = at_ref[3], at_ref[4]
    first = 0
    for ref in rows:
        stack[first : first + ref.shape[0]] = ref[...]
        first += ref.shape[0]
    for side, right in enumerate((mine_ref, other_ref)):
        whole[side] = dot(stack[...], right[...]).reshape(first // 80, 2, 40, 640)
    for i, out in enumerate(outs):
        r, t = i // 2, i % 2
        for side in range(2):
            for slot in range(out.shape[1]):
                out[side, slot] = whole[side, slot * 2 + (core ^ t), xh ^ r].astype(bf16)


def spread_kernel(at_ref, *refs):
    many, last = refs[:4], refs[4:8]
    turned_ref, outs, slots = refs[8], refs[9:13], refs[13]
    y, core = at_ref[1], at_ref[3]
    for q in range(4):
        parts = last if q == 2 else many
        place = 0 if q == 2 else (0, 1, None, 2)[q]

        def total(side):
            terms = [parts[i][side ^ (i % 2), place].astype(f32) for i in range(4)]
            return (terms[0] + terms[1]) + (terms[2] + terms[3])

        mine, other = total(0), total(1)
        low = jnp.where(core == 0, mine, other)
        high = jnp.where(core == 0, other, mine)
        outs[q][:, :640] = low.astype(outs[q].dtype)
        outs[q][:, 640:] = high.astype(outs[q].dtype)
        slots[y ^ q, :, :640] = low
        slots[y ^ q, :, 640:] = high
    for nz in range(4):
        part = jnp.concatenate(
            [slots[ny, :, nz * 320 : nz * 320 + 320] for ny in range(4)], axis=0
        )
        part = part.astype(bf16).T
        for j in range(8):
            turned_ref[nz * 8 + j] = part[j * 40 : j * 40 + 40]


def finish_kernel(at_ref, d0, d1, d2, d3, t_ref, kept_ref, out_ref, slots):
    for q, ref in enumerate((d0, d1, d2, d3)):
        slots[q] = ref[...].astype(f32)
    y = at_ref[1]
    for nz in range(4):
        blocks = []
        for ny in range(4):
            other = jnp.concatenate(
                [
                    t_ref[nz * 8 + s, :, ny * 40 : (ny + 1) * 40]
                    for s in range(8)
                ],
                axis=1,
            ).astype(f32)
            blocks.append(slots[y ^ ny, :, nz * 320 : (nz + 1) * 320] + other)
        block = 0.5 * jnp.concatenate(blocks, axis=1)
        kept = jnp.concatenate(
            [
                jnp.broadcast_to(kept_ref[:, j : j + 1], (40, BLK))
                for j in range(nz * 10, nz * 10 + 10)
            ],
            axis=1,
        )
        out_ref[:, nz * 1280 : (nz + 1) * 1280] = block * kept


def shards(dens_resp, density, fock, fock_resp, pattern):
    z, y, xl, core, xh = (lax.axis_index(name) for name in AXES)
    coords = jnp.stack((z, y, xl, core, xh)).astype(jnp.int32)

    with jax.named_scope("left_columns"):
        send = jnp.where(core == 0, density, dens_resp)
        came = flip(send, core=1)
    with jax.named_scope("right_columns"):
        first, second, _ = lax.optimization_barrier((fock, fock_resp, send))
        parts = local_call(
            right_kernel, "right_columns", shape(bf16, 8, 160, 320), coords, first, second
        )
    with jax.named_scope("density_turn"):
        halves, _ = lax.optimization_barrier((density.reshape(2, 2, 40, 1280), send))
        same = lax.dynamic_index_in_dim(halves, xh, 1, keepdims=False).reshape(80, 1280)
        other = lax.dynamic_index_in_dim(halves, 1 - xh, 1, keepdims=False).reshape(80, 1280)
        other = flip(other, xh=1)
    with jax.named_scope("left_columns"):
        pieces = local_call(
            left_kernel, "left_columns", [shape(bf16, 160, 640)] * 4, coords, dens_resp, density, came
        )
        parts, pieces = lax.optimization_barrier((parts, pieces))
        left = jnp.concatenate([pieces[0]] + [flip(pieces[q], y=q) for q in (1, 2, 3)])
        left, other = lax.optimization_barrier((left, other))
    with jax.named_scope("right_gather"):
        rounds = lax.all_to_all(
            parts, ("xl", "core", "xh"), split_axis=0, concat_axis=0, tiled=True
        )
        right = rounds.reshape(2, 4, 160, 320).transpose(0, 2, 1, 3).reshape(320, 1280)
        right, left = lax.optimization_barrier((right, left))
        rights = [right] + [flip(right, z=q) for q in (1, 2, 3)]
    with jax.named_scope("left_gather"):
        lefts = {
            (0, 0): left,
            (1, 0): flip(left, xl=1),
            (0, 1): flip(left, xh=1),
            (1, 1): flip(left, xl=1, xh=1),
        }

    with jax.named_scope("density_columns"):
        same, other, lefts[1, 0] = lax.optimization_barrier((same, other, lefts[1, 0]))
        cols = local_call(
            density_kernel, "density_columns", shape(bf16, 4, 80, 640), coords, same, other
        )
        dslots = lax.all_to_all(cols, "y", split_axis=0, concat_axis=0, tiled=True)
        dslots = dslots.reshape(320, 640)

    with jax.named_scope("first_product"):
        rights, dslots = lax.optimization_barrier((rights, dslots))
        rights = jnp.stack(rights)
        rsel = jnp.concatenate(
            [
                pick(rights, z ^ (nzh * 2 + (xh ^ r)))
                for r in range(2)
                for nzh in range(2)
            ]
        )
        theirs = [jnp.where(core == 0, lefts[1, r], lefts[0, r]) for r in range(2)]
        mine = [jnp.where(core == 0, lefts[0, r], lefts[1, r]) for r in range(2)]
        theirs = dot(jnp.concatenate(theirs, axis=1), rsel).reshape(4, 160, 1280)
        mine = dot(jnp.concatenate(mine, axis=1), rsel).reshape(4, 160, 1280)
    with jax.named_scope("mixed_sum"):
        both = [None] * 4
        for q in (2, 1, 3, 0):
            both[q] = mine[q] + flip(theirs[q], core=1)
        upper = flip(both[2][:80], y=1)
        lower = flip(both[2][80:], y=3)

    with jax.named_scope("density_gather"):
        done = flip(dslots, z=1)
        dthree = flip(dslots, z=3)
        upper, lower, done, dthree = lax.optimization_barrier((upper, lower, done, dthree))
        dtwo = (flip(dthree[:160], z=1), flip(done[160:], z=3))

    with jax.named_scope("mixed_sum"):
        third = jnp.concatenate((both[3][:80] + upper, both[3][80:]))
        first = jnp.concatenate((both[1][:80], both[1][80:] + lower))
        sums = [flip(first, y=1), flip(third, y=3)]

    with jax.named_scope("density_rows"):
        dmine = local_call(
            rows_kernel, "density_rows", shape(bf16, 1280, 640), coords, dslots, done, *dtwo, dthree
        )

    with jax.named_scope("mixed_sum"):
        sums, dmine = lax.optimization_barrier((sums, dmine))
        total = both[0] + sums[0] + sums[1]
        mixed = total.astype(bf16)

    with jax.named_scope("mixed_gather"):
        one, three = flip(mixed, y=1), flip(mixed, y=3)
        dother = flip(dmine, core=1)
        two = (three[:80], one[80:])
        two, one, three = lax.optimization_barrier((two, one, three))
        two = (flip(two[0], y=1), flip(two[1], y=3))

    with jax.named_scope("second_product"):

        def pieces_of(count, *rows):
            return local_call(
                second_kernel,
                "second_product",
                [shape(bf16, 2, count, 40, 640)] * 4,
                coords,
                dmine,
                dother,
                *rows,
                scratch=[
                    pltpu.VMEM((count * 160, 1280), bf16),
                    pltpu.VMEM((2, count * 2, 2, 40, 640), f32),
                ],
            )

        def scatter(cut):
            turns = [(r, t) for r in range(2) for t in range(2)]
            return [
                remap(piece, lambda a, b, c, d, e: (a, b, c ^ d, d ^ t, e ^ r))
                for piece, (r, t) in zip(cut, turns)
            ]

        cut = list(pieces_of(3, mixed, one, three))
        cut[3], two = lax.optimization_barrier((cut[3], two))
        many = scatter(cut)
        many[0], two = lax.optimization_barrier((many[0], two))
        last = scatter(pieces_of(1, *two))
        turned, *rows = local_call(
            spread_kernel,
            "spread",
            [shape(bf16, 32, 40, 160), shape(f32, 40, 1280)] + [shape(bf16, 40, 1280)] * 3,
            coords,
            *many,
            *last,
            scratch=[pltpu.VMEM((4, 40, 1280), f32)],
        )

    with jax.named_scope("transposed"):
        turned = lax.all_to_all(
            turned, ("z", "xl", "core", "xh"), split_axis=0, concat_axis=0, tiled=True
        )
    with jax.named_scope("direct"):
        direct = [rows[0]] + [flip(rows[q], y=q) for q in (1, 2, 3)]

    first_row = ((((z * 4 + y) * 2 + xl) * 2 + core) * 2 + xh) * 40
    block_rows = (first_row + jnp.arange(40, dtype=jnp.int32)) // BLK
    block_count = pattern.shape[0]
    onehot = (
        block_rows[:, None] == jnp.arange(block_count, dtype=jnp.int32)[None, :]
    ).astype(f32)
    kept_blocks = jnp.dot(onehot, pattern.astype(f32), preferred_element_type=f32)
    return local_call(
        finish_kernel,
        "finish",
        shape(f32, 40, 5120),
        coords,
        *direct,
        turned,
        kept_blocks,
        scratch=[pltpu.VMEM((4, 40, 1280), f32)],
    )


def solution(mesh):
    fine = Mesh(mesh.devices.reshape(SIZES), AXES)
    split = P(("z", "y", "xl"), ("core", "xh"))
    return jax.shard_map(
        shards,
        mesh=fine,
        in_specs=(split, split, split, split, P()),
        out_specs=P(AXES, None),
        check_vma=False,
    )
```

```python
import jax
import jax.numpy as jnp
from jax import lax
from jax.experimental import pallas as pl
from jax.experimental.pallas import tpu as pltpu
from jax.sharding import Mesh
from jax.sharding import PartitionSpec as P

BLK = 128
AXES = ("z", "y", "xl", "core", "xh")
SIZES = (4, 4, 2, 2, 2)
f32 = jnp.float32
bf16 = jnp.bfloat16


def flip(value, z=0, y=0, xl=0, core=0, xh=0):
    masks = (z, y, xl, core, xh)
    pairs = []
    for source in range(128):
        rest, digits = source, []
        for size in reversed(SIZES):
            digits.append(rest % size)
            rest //= size
        target = 0
        for digit, size, mask in zip(reversed(digits), SIZES, masks):
            target = target * size + (digit ^ mask)
        pairs.append((source, target))
    return lax.ppermute(value, AXES, pairs)


def remap(value, rule):
    pairs = []
    for source in range(128):
        rest, digits = source, []
        for size in reversed(SIZES):
            digits.append(rest % size)
            rest //= size
        target = 0
        for digit, size in zip(rule(*reversed(digits)), SIZES):
            target = target * size + digit
        pairs.append((source, target))
    return lax.ppermute(value, AXES, pairs)


def pick(stack, index):
    return lax.dynamic_index_in_dim(stack, index, 0, keepdims=False)


def dot(a, b):
    return jnp.dot(a, b, preferred_element_type=f32)


VMEM = pl.BlockSpec(memory_space=pltpu.VMEM)
SMEM = pl.BlockSpec(memory_space=pltpu.SMEM)


def local_call(kernel, name, outs, coords, *operands, scratch=()):
    return pl.pallas_call(
        kernel,
        out_shape=outs,
        in_specs=[SMEM] + [VMEM] * len(operands),
        out_specs=jax.tree.map(lambda _: VMEM, outs),
        scratch_shapes=list(scratch),
        name=name,
    )(coords, *operands)


def shape(dtype, *dims):
    return jax.ShapeDtypeStruct(dims, dtype)


def left_kernel(at_ref, first_ref, second_ref, came_ref, *outs):
    y, core = at_ref[1], at_ref[3]
    low = jnp.where(core == 0, first_ref[...], came_ref[...])
    high = jnp.where(core == 0, came_ref[...], second_ref[...])
    for ny in range(4):
        cut = slice(ny * 320, ny * 320 + 320)
        piece = jnp.concatenate((low[:, cut], high[:, cut]), axis=1)
        for q in range(4):

            @pl.when((y ^ q) == ny)
            def _():
                outs[q][...] = piece


def right_kernel(at_ref, first_ref, second_ref, out_ref):
    for m, ref in enumerate((first_ref, second_ref)):
        whole = ref[...]
        for xl in range(2):
            for xh in range(2):
                out_ref[xl * 4 + m * 2 + xh] = jnp.concatenate(
                    [
                        whole[:, start : start + 40]
                        for ny in range(4)
                        for start in (
                            ny * 320 + xl * 160 + xh * 40,
                            ny * 320 + xl * 160 + 80 + xh * 40,
                        )
                    ],
                    axis=1,
                )


def density_kernel(at_ref, same_ref, other_ref, out_ref):
    xh = at_ref[4]
    first = jnp.where(xh == 0, same_ref[...], other_ref[...])
    second = jnp.where(xh == 0, other_ref[...], same_ref[...])
    for ny in range(4):
        cut = slice(ny * 320, ny * 320 + 320)
        out_ref[ny] = jnp.concatenate((first[:, cut], second[:, cut]), axis=1)


def rows_kernel(at_ref, own_ref, one_ref, upper_ref, lower_ref, three_ref, out_ref):
    z = at_ref[0]

    def place(q, start, count, ref):
        first = pl.multiple_of((z ^ q) * 320 + start, 160)
        out_ref[pl.ds(first, count), :] = ref[...]

    place(0, 0, 320, own_ref)
    place(1, 0, 320, one_ref)
    place(2, 0, 160, upper_ref)
    place(2, 160, 160, lower_ref)
    place(3, 0, 320, three_ref)


def second_kernel(at_ref, mine_ref, other_ref, *refs):
    rows, outs, stack, whole = refs[:-6], refs[-6:-2], refs[-2], refs[-1]
    core, xh = at_ref[3], at_ref[4]
    first = 0
    for ref in rows:
        stack[first : first + ref.shape[0]] = ref[...]
        first += ref.shape[0]
    for side, right in enumerate((mine_ref, other_ref)):
        whole[side] = dot(stack[...], right[...]).reshape(first // 80, 2, 40, 640)
    for i, out in enumerate(outs):
        r, t = i // 2, i % 2
        for side in range(2):
            for slot in range(out.shape[1]):
                out[side, slot] = whole[side, slot * 2 + (core ^ t), xh ^ r].astype(bf16)


def spread_kernel(at_ref, *refs):
    many, last = refs[:4], refs[4:8]
    turned_ref, outs, slots = refs[8], refs[9:13], refs[13]
    y, core = at_ref[1], at_ref[3]
    for q in range(4):
        parts = last if q == 2 else many
        place = 0 if q == 2 else (0, 1, None, 2)[q]

        def total(side):
            terms = [parts[i][side ^ (i % 2), place].astype(f32) for i in range(4)]
            return (terms[0] + terms[1]) + (terms[2] + terms[3])

        mine, other = total(0), total(1)
        low = jnp.where(core == 0, mine, other)
        high = jnp.where(core == 0, other, mine)
        outs[q][:, :640] = low.astype(outs[q].dtype)
        outs[q][:, 640:] = high.astype(outs[q].dtype)
        slots[y ^ q, :, :640] = low
        slots[y ^ q, :, 640:] = high
    for nz in range(4):
        part = jnp.concatenate(
            [slots[ny, :, nz * 320 : nz * 320 + 320] for ny in range(4)], axis=0
        )
        part = part.T
        for j in range(8):
            turned_ref[nz * 8 + j] = part[j * 40 : j * 40 + 40].astype(bf16)


def finish_kernel(at_ref, d0, d1, d2, d3, t_ref, kept_ref, out_ref, slots):
    for q, ref in enumerate((d0, d1, d2, d3)):
        slots[q] = ref[...].astype(f32)
    y = at_ref[1]
    for nz in range(4):
        blocks = []
        for ny in range(4):
            other = jnp.concatenate(
                [
                    t_ref[nz * 8 + s, :, ny * 40 : (ny + 1) * 40]
                    for s in range(8)
                ],
                axis=1,
            ).astype(f32)
            blocks.append(slots[y ^ ny, :, nz * 320 : (nz + 1) * 320] + other)
        block = 0.5 * jnp.concatenate(blocks, axis=1)
        kept = jnp.concatenate(
            [
                jnp.broadcast_to(kept_ref[:, j : j + 1], (40, BLK))
                for j in range(nz * 10, nz * 10 + 10)
            ],
            axis=1,
        )
        out_ref[:, nz * 1280 : (nz + 1) * 1280] = block * kept


def shards(dens_resp, density, fock, fock_resp, pattern):
    z, y, xl, core, xh = (lax.axis_index(name) for name in AXES)
    coords = jnp.stack((z, y, xl, core, xh)).astype(jnp.int32)

    with jax.named_scope("left_columns"):
        send = jnp.where(core == 0, density, dens_resp)
        came = flip(send, core=1)
    with jax.named_scope("right_columns"):
        first, second, _ = lax.optimization_barrier((fock, fock_resp, send))
        parts = local_call(
            right_kernel, "right_columns", shape(bf16, 8, 160, 320), coords, first, second
        )
    with jax.named_scope("density_turn"):
        halves, _ = lax.optimization_barrier((density.reshape(2, 2, 40, 1280), send))
        same = lax.dynamic_index_in_dim(halves, xh, 1, keepdims=False).reshape(80, 1280)
        other = lax.dynamic_index_in_dim(halves, 1 - xh, 1, keepdims=False).reshape(80, 1280)
        other = flip(other, xh=1)
    with jax.named_scope("left_columns"):
        pieces = local_call(
            left_kernel, "left_columns", [shape(bf16, 160, 640)] * 4, coords, dens_resp, density, came
        )
        parts, pieces = lax.optimization_barrier((parts, pieces))
        left = jnp.concatenate([pieces[0]] + [flip(pieces[q], y=q) for q in (1, 2, 3)])
        left, other = lax.optimization_barrier((left, other))
    with jax.named_scope("right_gather"):
        rounds = lax.all_to_all(
            parts, ("xl", "core", "xh"), split_axis=0, concat_axis=0, tiled=True
        )
        right = rounds.reshape(2, 4, 160, 320).transpose(0, 2, 1, 3).reshape(320, 1280)
        right, left = lax.optimization_barrier((right, left))
        rights = [right] + [flip(right, z=q) for q in (1, 2, 3)]
    with jax.named_scope("left_gather"):
        lefts = {
            (0, 0): left,
            (1, 0): flip(left, xl=1),
            (0, 1): flip(left, xh=1),
            (1, 1): flip(left, xl=1, xh=1),
        }

    with jax.named_scope("density_columns"):
        same, other, lefts[1, 0] = lax.optimization_barrier((same, other, lefts[1, 0]))
        cols = local_call(
            density_kernel, "density_columns", shape(bf16, 4, 80, 640), coords, same, other
        )
        dslots = lax.all_to_all(cols, "y", split_axis=0, concat_axis=0, tiled=True)
        dslots = dslots.reshape(320, 640)

    with jax.named_scope("first_product"):
        rights, dslots = lax.optimization_barrier((rights, dslots))
        rights = jnp.stack(rights)
        rsel = jnp.concatenate(
            [
                pick(rights, z ^ (nzh * 2 + (xh ^ r)))
                for r in range(2)
                for nzh in range(2)
            ]
        )
        theirs = [jnp.where(core == 0, lefts[1, r], lefts[0, r]) for r in range(2)]
        mine = [jnp.where(core == 0, lefts[0, r], lefts[1, r]) for r in range(2)]
        theirs = dot(jnp.concatenate(theirs, axis=1), rsel).reshape(4, 160, 1280)
        mine = dot(jnp.concatenate(mine, axis=1), rsel).reshape(4, 160, 1280)
    with jax.named_scope("mixed_sum"):
        both = [None] * 4
        for q in (2, 1, 3, 0):
            both[q] = mine[q] + flip(theirs[q], core=1)
        upper = flip(both[2][:80], y=1)
        lower = flip(both[2][80:], y=3)

    with jax.named_scope("density_gather"):
        done = flip(dslots, z=1)
        dthree = flip(dslots, z=3)
        upper, lower, done, dthree = lax.optimization_barrier((upper, lower, done, dthree))
        dtwo = (flip(dthree[:160], z=1), flip(done[160:], z=3))

    with jax.named_scope("mixed_sum"):
        third = jnp.concatenate((both[3][:80] + upper, both[3][80:]))
        first = jnp.concatenate((both[1][:80], both[1][80:] + lower))
        sums = [flip(first, y=1), flip(third, y=3)]

    with jax.named_scope("density_rows"):
        dmine = local_call(
            rows_kernel, "density_rows", shape(bf16, 1280, 640), coords, dslots, done, *dtwo, dthree
        )

    with jax.named_scope("mixed_sum"):
        sums, dmine = lax.optimization_barrier((sums, dmine))
        total = both[0] + sums[0] + sums[1]
        mixed = total.astype(bf16)

    with jax.named_scope("mixed_gather"):
        one, three = flip(mixed, y=1), flip(mixed, y=3)
        dother = flip(dmine, core=1)
        two = (three[:80], one[80:])
        two, one, three = lax.optimization_barrier((two, one, three))
        two = (flip(two[0], y=1), flip(two[1], y=3))

    with jax.named_scope("second_product"):

        def pieces_of(count, *rows):
            return local_call(
                second_kernel,
                "second_product",
                [shape(bf16, 2, count, 40, 640)] * 4,
                coords,
                dmine,
                dother,
                *rows,
                scratch=[
                    pltpu.VMEM((count * 160, 1280), bf16),
                    pltpu.VMEM((2, count * 2, 2, 40, 640), f32),
                ],
            )

        def scatter(cut):
            turns = [(r, t) for r in range(2) for t in range(2)]
            return [
                remap(piece, lambda a, b, c, d, e: (a, b, c ^ d, d ^ t, e ^ r))
                for piece, (r, t) in zip(cut, turns)
            ]

        cut = list(pieces_of(3, mixed, one, three))
        cut[3], two = lax.optimization_barrier((cut[3], two))
        many = scatter(cut)
        last = scatter(pieces_of(1, *two))
        turned, *rows = local_call(
            spread_kernel,
            "spread",
            [shape(bf16, 32, 40, 160), shape(f32, 40, 1280)] + [shape(bf16, 40, 1280)] * 3,
            coords,
            *many,
            *last,
            scratch=[pltpu.VMEM((4, 40, 1280), f32)],
        )

    with jax.named_scope("transposed"):
        turned = lax.all_to_all(
            turned, ("z", "xl", "core", "xh"), split_axis=0, concat_axis=0, tiled=True
        )
    with jax.named_scope("direct"):
        direct = [rows[0]] + [flip(rows[q], y=q) for q in (1, 2, 3)]

    first_row = ((((z * 4 + y) * 2 + xl) * 2 + core) * 2 + xh) * 40
    block_rows = (first_row + jnp.arange(40, dtype=jnp.int32)) // BLK
    block_count = pattern.shape[0]
    onehot = (
        block_rows[:, None] == jnp.arange(block_count, dtype=jnp.int32)[None, :]
    ).astype(f32)
    kept_blocks = jnp.dot(onehot, pattern.astype(f32), preferred_element_type=f32)
    return local_call(
        finish_kernel,
        "finish",
        shape(f32, 40, 5120),
        coords,
        *direct,
        turned,
        kept_blocks,
        scratch=[pltpu.VMEM((4, 40, 1280), f32)],
    )


def solution(mesh):
    fine = Mesh(mesh.devices.reshape(SIZES), AXES)
    split = P(("z", "y", "xl"), ("core", "xh"))
    return jax.shard_map(
        shards,
        mesh=fine,
        in_specs=(split, split, split, split, P()),
        out_specs=P(AXES, None),
        check_vma=False,
    )
```
